128 devices in a mesh: dp: 2 (over core), expert: 64 (over x, y, z).
Axes of the slice: x: 4, y: 4, z: 4, core: 2. Of those that a mesh axis runs over, the one named last changes fastest.
Arguments:
- tokens: bfloat16 [64, 512, 1024], P('expert', 'dp'), may hold values from -6 to 6
- teacher: bfloat16 [64, 512, 1024], P('expert', 'dp'), may hold values from -6 to 6
- lengths: int32 [64], P('expert'), may hold values from 128 to 512, as said below
- routes: int32 [64, 512, 1], P('expert', 'dp'), may hold values from 0 to 63; in each aligned block of 256 rows (0 to 255, 256 to 511, ..., all dimensions but the last counted through in order) at most 8 rows name the same one
- ln1_gain: bfloat16 [1024], P(('dp', 'expert')), may hold values from 0.5 to 1.5
- ln1_bias: bfloat16 [1024], P(('dp', 'expert')), may hold values from -1.75 to 1.75
- query_key_value_weight: bfloat16 [1024, 3072], P(('dp', 'expert')), may hold values from -0.1875 to 0.1875
- output_weight: bfloat16 [1024, 1024], P(('dp', 'expert')), may hold values from -1.5 to 1.5
- ln2_gain: bfloat16 [1024], P(('dp', 'expert')), may hold values from 0.5 to 1.5
- ln2_bias: bfloat16 [1024], P(('dp', 'expert')), may hold values from -1.75 to 1.75
- router_weight: bfloat16 [1024, 64], P(('dp', 'expert')), may hold values from -0.125 to 0.125
- w_in: bfloat16 [64, 1024, 4096], P('expert', 'dp'), may hold values from -0.1875 to 0.1875
- w_down: bfloat16 [64, 4096, 1024], P('expert', 'dp'), may hold values from -6 to 6
Outputs:
- mixed_out: bfloat16 [64, 512, 1024], P('expert', 'dp')
- loss_value: float32 [], replicated
- grad_tokens: float32 [64, 512, 1024], P('expert', 'dp')
- grad_ln1_gain: float32 [1024], P(('dp', 'expert'))
- grad_ln1_bias: float32 [1024], P(('dp', 'expert'))
- grad_w_qkv: float32 [1024, 3072], P(('dp', 'expert'))
- grad_w_out: float32 [1024, 1024], P(('dp', 'expert'))
- grad_ln2_gain: float32 [1024], P(('dp', 'expert'))
- grad_ln2_bias: float32 [1024], P(('dp', 'expert'))
- grad_w_router: float32 [1024, 64], P(('dp', 'expert'))
- grad_w_in: float32 [64, 1024, 4096], P('expert', 'dp')
- grad_w_down: float32 [64, 4096, 1024], P('expert', 'dp')
The draws below stay inside these ranges and needn't reach their ends.
Inputs may be any that keep to these rules, and one draw needn't show every extreme that they name: `lengths`: some slot has exactly 512 valid tokens in every draw; the tokens of a slot past its length are padding. `routes`: within the rows of one device (aligned blocks of 256 positions of a slot) no expert is named more than 8 times, and 8 is reached.
All inputs are finite; a program needn't handle non-finite values.
Results may differ from the reference program's by a relative error of at most 0.012.
Values may be sent and summed in bfloat16 or wider, within the bound.
A program may use at most 192 MiB of HBM per device.

```python
import math
import jax
import jax.numpy as jnp
import numpy as np
from jax import lax

D = 1024
HEADS = 16
HEAD = 64
FF = 4096
GROUP = 256
SEQ = 512
SLOTS = 64
EXPERTS = 64
CAP = 8
N_DP = 2


def draw_lengths(key, part):
    first_key, second_key = jax.random.split(key)
    spread_lengths = jax.random.randint(first_key, (SLOTS,), SEQ // 4, SEQ + 1)
    longest = jax.random.randint(second_key, (), 0, SLOTS)
    return jnp.where(jnp.arange(SLOTS) == longest, SEQ, spread_lengths).astype(jnp.int32)


def steps_of(own_key, dims, pieces, smallest, largest):
    level, own = 1.0, jax.random.fold_in(own_key, 6)
    for position, parts in pieces:
        heights = jnp.exp(jax.random.uniform(jax.random.fold_in(own, position), (parts,), jnp.float32, smallest / len(pieces), largest / len(pieces)))
        level = level * jnp.repeat(heights, dims[position] // parts).reshape([-1 if axis == position else 1 for axis in range(len(dims))])
    return level


def routed_block(own_key, own, number, rows, amount, top, bound, slope):
    ranking = jax.random.permutation(own_key, amount)
    crowded, ordinary = shares(amount, rows * top, bound, slope, True), shares(amount, rows * top, bound, slope, False)
    places = jnp.arange(amount)

    def named(sizes, turn):
        used = int((sizes > 0).sum())
        fixed = max(1, used // 4)
        passed = fixed + (places - fixed + turn * (used - fixed)) % max(1, amount - fixed)
        return jnp.zeros((amount,), jnp.int32).at[ranking[jnp.where(places < fixed, places, passed)]].set(jnp.asarray(sizes, jnp.int32))

    sizes = jnp.where(number % 4 == 0, named(crowded, number // 4), named(ordinary, number - number // 4 - 1))
    mixed = jax.random.permutation(jax.random.fold_in(own, 3), amount)
    source_of, sink = mixed[0:amount // 2 * 2:2], mixed[1:amount // 2 * 2:2]
    slack = jnp.minimum(sizes[source_of] - 1, bound - sizes[sink]) // 2
    slack = jnp.where((source_of == ranking[0]) | (sink == ranking[0]) | (sizes[sink] == 0), 0, jnp.maximum(slack, 0))
    passed = jax.random.randint(jax.random.fold_in(own, 4), (amount // 2,), 0, 1 << 20) % (slack + 1)
    sizes = sizes.at[source_of].add(-passed).at[sink].add(passed)
    labels = jnp.searchsorted(jnp.cumsum(sizes), jnp.arange(rows * top), side="right").astype(jnp.int32)
    listing = labels.reshape(top, rows).T
    listing = listing[jax.random.permutation(jax.random.fold_in(own, 1), rows)]
    turn = jax.random.randint(jax.random.fold_in(own, 2), (rows, 1), 0, top)
    return jnp.take_along_axis(listing, (jnp.arange(top)[None, :] + turn) % top, axis=1)


def shares(count, total, limit, skew, full):
    portions = [(1 << 20) // math.isqrt(rank ** skew) + 1 for rank in range(1, count + 1)]
    largest = limit if full else min(limit, max(-(-total // count), total * portions[0] // sum(portions)))
    least = 1 if total - largest >= count - 1 else 0
    given, surplus = [largest] + [least] * (count - 1), total - largest - least * (count - 1)
    while surplus > 0:
        candidates = [i for i in range(1, count) if given[i] < largest] or [i for i in range(1, count) if given[i] < limit]
        mass, budget = sum([portions[i] for i in candidates]), surplus
        for i in candidates:
            more = min(limit - given[i], max(1, budget * portions[i] // mass), surplus)
            given[i] = given[i] + more
            surplus = surplus - more
    return np.array(given)


def gaussian(rng, shape, deviation, reach, cuts=(), kind=jnp.bfloat16):
    array = jax.random.normal(rng, shape, jnp.float32) * deviation
    if len(cuts) > 0:
        array = steps_of(rng, shape, cuts, -0.22, 0.18) * array
    return jnp.clip(array, min=-reach, max=reach).astype(kind)


def setup_inputs(seed: int = 0) -> dict:
    keys = jax.random.split(jax.random.key(seed), 14)
    tokens = gaussian(keys[0], (SLOTS, SEQ, D), 1.0, 6.0, ((0, 64), (1, 2)))
    teacher = gaussian(keys[1], (SLOTS, SEQ, D), 1.0, 6.0, ((0, 64), (1, 2)))
    lengths = draw_lengths(jax.random.fold_in(keys[13], 71), 0)
    routes_keys = jax.random.split(jax.random.fold_in(keys[3], 1), SLOTS * SEQ // GROUP)
    routes_turns = jax.random.permutation(jax.random.fold_in(keys[3], 3), SLOTS * SEQ // GROUP)
    routes = jax.vmap(lambda own, number: routed_block(jax.random.fold_in(keys[3], 2), own, number, GROUP, EXPERTS, 1, CAP, 2))(routes_keys, routes_turns).reshape((SLOTS, SEQ, 1))
    ln1_gain = jnp.clip(1.0 + 0.1 * jax.random.normal(keys[4], (D,), jnp.float32), 0.5, 1.5).astype(jnp.bfloat16)
    ln1_bias = gaussian(keys[5], (D,), 0.3, 1.75, ((0, 128),))
    query_key_value_weight = gaussian(keys[6], (D, 3 * D), D ** -0.5, 0.1875, ((0, 128),))
    output_weight = gaussian(keys[7], (D, D), (D // 64) ** -0.5, 1.5, ((0, 128),))
    ln2_gain = jnp.clip(1.0 + 0.1 * jax.random.normal(keys[8], (D,), jnp.float32), 0.5, 1.5).astype(jnp.bfloat16)
    ln2_bias = gaussian(keys[9], (D,), 0.3, 1.75, ((0, 128),))
    router_weight = gaussian(keys[10], (D, EXPERTS), (2 * D) ** -0.5, 0.125, ((0, 128),))
    w_in = gaussian(keys[11], (EXPERTS, D, FF), D ** -0.5, 0.1875, ((0, 64), (1, 2)))
    w_down = gaussian(keys[12], (EXPERTS, FF, D), (max(1, FF // (EXPERTS * EXPERTS))) ** -0.5, 6.0, ((0, 64), (1, 2)))
    return {"tokens": tokens, "teacher": teacher, "lengths": lengths, "routes": routes, "ln1_gain": ln1_gain, "ln1_bias": ln1_bias, "query_key_value_weight": query_key_value_weight, "output_weight": output_weight, "ln2_gain": ln2_gain, "ln2_bias": ln2_bias, "router_weight": router_weight, "w_in": w_in, "w_down": w_down}


@jax.custom_vjp
def reduced_precision(v):
    return lax.optimization_barrier(v.astype(jnp.bfloat16)).astype(jnp.float32)

@jax.custom_vjp
def reduced_backward(v):
    return v

def low_keep(v):
    return (reduced_precision(v), None)

def low_pass(kept, grad):
    return (grad,)

def back_keep(v):
    return (v, None)

def back_low(kept, grad):
    return (reduced_precision(grad),)
reduced_precision.defvjp(low_keep, low_pass)
reduced_backward.defvjp(back_keep, back_low)
precise_setting = lax.Precision.HIGHEST

def layer_norm(values, scale_vec, offset):
    center = lax.optimization_barrier(jnp.mean(values, -1, keepdims=True))
    centred = values - center
    spread = lax.optimization_barrier(jnp.mean(centred * centred, -1, keepdims=True))
    return centred * lax.rsqrt(spread + 1e-05) * scale_vec + offset

def attend(packed):
    qkv_slot, length = packed
    queries = qkv_slot[:, :D].reshape(SEQ, HEADS, HEAD)
    key_rows = qkv_slot[:, D:2 * D].reshape(SEQ, HEADS, HEAD)
    value_rows = qkv_slot[:, 2 * D:].reshape(SEQ, HEADS, HEAD)
    scores = reduced_backward(jnp.einsum('qhd,khd->hqk', queries, key_rows, precision=precise_setting) * 0.125)
    places = jnp.arange(SEQ)
    allowed = (places[None, :] <= places[:, None]) & (places[None, :] < length)
    scores = jnp.where(allowed[None], scores, -1e+30)
    maximum = lax.optimization_barrier(jnp.max(scores, -1, keepdims=True))
    exponent = jnp.exp(scores - maximum)
    attn_probs = reduced_precision(exponent / lax.optimization_barrier(jnp.sum(exponent, -1, keepdims=True)))
    return jnp.einsum('hqk,khd->qhd', attn_probs, value_rows, precision=precise_setting).reshape(SEQ, D)

def expert(packed):
    row_block, w_first, w_second = packed
    pre_act = reduced_backward(jnp.dot(row_block, w_first, precision=precise_setting))
    activated = reduced_precision(jax.nn.gelu(pre_act, approximate=True))
    return jnp.dot(activated, w_second, precision=precise_setting)

def forward(parameters, lengths, routes, teacher):
    tokens, gain_one, bias_one, query_key_value_weight, output_weight, gain_two, bias_two, router_weight, w_in, w_down = parameters
    first_norm = reduced_precision(layer_norm(tokens, gain_one, bias_one))
    query_key_value_rows = reduced_precision(reduced_backward(jnp.einsum('xur,rw->xuw', first_norm, query_key_value_weight, precision=precise_setting)))
    attention_result = lax.map(jax.checkpoint(attend), (query_key_value_rows, lengths))
    attention_result = reduced_precision(reduced_backward(attention_result))
    residual_branch = reduced_backward(jnp.einsum('xur,rw->xuw', attention_result, output_weight, precision=precise_setting))
    residual = tokens + residual_branch
    second_norm = reduced_precision(layer_norm(residual, gain_two, bias_two))
    router_scores = jnp.einsum('xur,rw->xuw', second_norm, router_weight, precision=precise_setting)
    router_probs = jax.nn.softmax(router_scores, -1)
    route_ids = routes[..., 0]
    chosen = route_ids[..., None] == jnp.arange(EXPERTS)[None, None, :]
    gate_prob = lax.optimization_barrier(jnp.sum(jnp.where(chosen, router_probs, 0.0), -1))
    flat_route = route_ids.reshape(-1)
    total_rows = SLOTS * SEQ
    most_rows = CAP * N_DP * SLOTS
    ordering = jnp.argsort(flat_route, stable=True).astype(jnp.int32)
    counts = lax.optimization_barrier(jnp.sum((flat_route[:, None] == jnp.arange(EXPERTS)[None, :]).astype(jnp.int32), 0)).astype(jnp.int32)
    starts = (jnp.cumsum(counts) - counts).astype(jnp.int32)
    offsets = jnp.arange(most_rows).astype(jnp.int32)
    filled = (offsets[None, :] < counts[:, None]).astype(jnp.float32)
    picked = ordering[jnp.minimum(starts[:, None] + offsets[None, :], total_rows - 1).astype(jnp.int32)]
    outgoing = reduced_backward(second_norm).reshape(total_rows, D)
    rows_in = outgoing[picked] * filled[..., None]
    produced = lax.map(jax.checkpoint(expert), (rows_in, w_in, w_down))
    produced = reduced_precision(reduced_backward(produced)) * filled[..., None]
    expert_out = jnp.zeros((total_rows, D), jnp.float32).at[picked.reshape(-1)].add(produced.reshape(-1, D))
    expert_out = expert_out.reshape(SLOTS, SEQ, D)
    mixed_out = reduced_precision(residual + gate_prob[..., None] * expert_out)
    valid_rows = (jnp.arange(SEQ)[None, :] < lengths[:, None]).astype(jnp.float32)
    errors = mixed_out - teacher
    return (mixed_out, 0.5 * jnp.sum(valid_rows[..., None] * errors * errors))

def reference(tokens, teacher, lengths, routes, ln1_gain, ln1_bias, query_key_value_weight, output_weight, ln2_gain, ln2_bias, router_weight, w_in, w_down):
    floats = tuple((item.astype(jnp.float32) for item in (tokens, ln1_gain, ln1_bias, query_key_value_weight, output_weight, ln2_gain, ln2_bias, router_weight, w_in, w_down)))
    target = teacher.astype(jnp.float32)
    outputs, pullback = jax.vjp(lambda parameters: forward(parameters, lengths, routes, target), floats)
    mixed_out, half_sse = outputs
    gradients = pullback((jnp.zeros_like(mixed_out), jnp.ones_like(half_sse)))[0]
    count_all = jnp.sum((jnp.arange(SEQ)[None, :] < lengths[:, None]).astype(jnp.float32))
    loss_value = 2.0 * half_sse / (count_all * D)
    return (mixed_out.astype(jnp.bfloat16), loss_value, gradients[0], gradients[1], gradients[2], gradients[3], gradients[4], gradients[5], gradients[6], gradients[7], gradients[8], gradients[9])
```

```python
import jax
import jax.numpy as jnp
from jax import lax
from jax.experimental import pallas as pl
from jax.experimental.pallas import tpu as pltpu
from jax.sharding import PartitionSpec as P

MESH = pl.DeviceIdType.MESH
SIDE = 4
FULL = slice(None)

AG_COLS = 4224
AG_PIECES = ((0, 768, 1408), (1408, 2176, 2816), (2816, 3584, 4224))


def place(region, c0, c1):
    return tuple(region) + (FULL, pl.ds(c0, c1 - c0))


def coords():
    e = lax.axis_index("expert")
    return [e // 16, (e // 4) % 4, e % 4]


def shifted(pos, axis, by):
    out = list(pos)
    out[axis] = (pos[axis] + by) % SIDE
    return out


def chip(pos):
    return {"expert": pos[0] * 16 + pos[1] * 4 + pos[2]}


def neighbours(pos):
    return [chip(shifted(pos, axis, by)) for axis in range(3) for by in (1, 3)]


def greet(pos, core):
    barrier = pltpu.get_barrier_semaphore()
    for other in neighbours(pos) + [{"dp": 1 - core}]:
        pl.semaphore_signal(barrier, inc=1, device_id=other, device_id_type=MESH)
    pl.semaphore_wait(barrier, 7)


class Sender:
    def __init__(self, send_sems, recv_sems):
        self.send_sems, self.recv_sems, self.count, self.sent = send_sems, recv_sems, 0, []

    def __call__(self, src, dst, device):
        copy = pltpu.make_async_remote_copy(
            src_ref=src,
            dst_ref=dst,
            send_sem=self.send_sems.at[self.count],
            recv_sem=self.recv_sems.at[self.count],
            device_id=device,
            device_id_type=MESH,
        )
        copy.start()
        self.count += 1
        self.sent.append(copy)
        return copy


def gather_kernel(shard, whole, own_sem, send_sems, recv_sems):
    pos = coords()
    core = lax.axis_index("dp")
    partner = {"dp": 1 - core}
    own = pltpu.make_async_copy(shard, whole.at[(core, *pos)], own_sem)
    own.start()
    greet(pos, core)
    send = Sender(send_sems, recv_sems)
    own.wait()

    def share(region, c0, c1, device):
        spot = whole.at[place([core] + region, c0, c1)]
        return send(spot, spot, device)

    across = []
    for stage in range(3):
        first = []
        for piece, (c0, mid, c1) in enumerate(AG_PIECES):
            order = [(piece + step) % 3 for step in range(3)]
            axis = order[stage]
            done = order[:stage]
            region = [FULL if a in done else pos[a] for a in range(3)]
            up, down = chip(shifted(pos, axis, 1)), chip(shifted(pos, axis, 3))
            first.append((axis, region, up, down, share(region, c0, c1, up), share(region, c0, c1, down)))
        if stage == 2:
            for (c0, mid, c1), (axis, region, up, down, _, _) in zip(AG_PIECES, first):
                across.append(share(region, c0, c1, partner))
        second = []
        for (c0, mid, c1), (axis, region, up, down, to_up, to_down) in zip(AG_PIECES, first):
            below, above = list(region), list(region)
            below[axis], above[axis] = (pos[axis] + 3) % SIDE, (pos[axis] + 1) % SIDE
            to_up.wait_recv()
            on_up = share(below, c0, mid, up)
            to_down.wait_recv()
            on_down = share(above, mid, c1, down)
            second.append((on_up, on_down))
            if stage == 2:
                across.append(share(below, c0, c1, partner))
                across.append(share(above, c0, c1, partner))
        for (c0, mid, c1), (axis, region, up, down, _, _), (on_up, on_down) in zip(AG_PIECES, first, second):
            on_up.wait_recv()
            on_down.wait_recv()
            if stage == 2:
                far = list(region)
                far[axis] = (pos[axis] + 2) % SIDE
                across.append(share(far, c0, c1, partner))
    for copy in across:
        copy.wait_recv()
    for copy in send.sent:
        copy.wait_send()


def gather_layer(shard):
    copies = 3 * 3 * 4 + 3 * 4
    whole = pl.pallas_call(
        gather_kernel,
        out_shape=jax.ShapeDtypeStruct((2, SIDE, SIDE, SIDE, 8, AG_COLS), jnp.bfloat16),
        in_specs=[pl.BlockSpec(memory_space=pl.ANY)],
        out_specs=pl.BlockSpec(memory_space=pl.ANY),
        scratch_shapes=[
            pltpu.SemaphoreType.DMA,
            pltpu.SemaphoreType.DMA((copies,)),
            pltpu.SemaphoreType.DMA((copies,)),
        ],
        compiler_params=pltpu.CompilerParams(collective_id=0, has_side_effects=True),
        name="gather_layer",
    )(shard)
    return whole.reshape(1024, AG_COLS)


RS_COLS = (3072, 1024, 256)
RS_KINDS = (jnp.bfloat16, jnp.bfloat16, jnp.float32)
RS_HALVES = (
    (((0, 0, 768),), ((0, 768, 1536),)),
    (((0, 1536, 2304),), ((0, 2304, 3072),)),
    (((1, 0, 768),), ((1, 768, 1024), (2, 0, 256))),
)
RS_PIECES = tuple(h0 + h1 for h0, h1 in RS_HALVES)


def reduce_kernel(*rest):
    source, outs, rest = rest[:3], rest[3:6], rest[6:]
    refs, (send_sems, recv_sems) = list(rest[:-2]), rest[-2:]
    take = iter(refs)
    pos = coords()
    core = lax.axis_index("dp")
    partner = {"dp": 1 - core}
    greet(pos, core)
    send = Sender(send_sems, recv_sems)
    landed = (next(take), next(take), next(take))

    opening = []
    for piece in range(3):
        copies = []
        for kind, c0, c1 in RS_PIECES[piece]:
            copies.append(
                send(
                    source[kind].at[place([1 - core, FULL, FULL, FULL], c0, c1)],
                    landed[kind].at[place([FULL, FULL, FULL], c0, c1)],
                    partner,
                )
            )
        opening.append(copies)

    def whole_sum(kind, index, c0, c1):
        spot = index + (FULL, pl.ds(c0, c1 - c0))
        mine = source[kind][(core,) + spot].astype(jnp.float32)
        return mine + landed[kind][spot].astype(jnp.float32)

    sums = []
    for piece in range(3):
        sums.append(whole_sum)

    for stage in range(3):
        plans = []
        for piece in range(3):
            order = [(piece + step) % 3 for step in range(3)]
            axis = order[stage]
            free = sorted(order[stage + 1:])
            fixed = order[:stage]
            bufs = {}
            for half in range(2):
                for n, (kind, c0, c1) in enumerate(RS_HALVES[piece][half]):
                    for what in ("sendA", "recvA"):
                        bufs[what, half, n] = next(take)
            for way in range(2):
                for n, (kind, c0, c1) in enumerate(RS_PIECES[piece]):
                    for what in ("sendB", "recvB"):
                        bufs[what, way, n] = next(take)
            up, down = chip(shifted(pos, axis, 1)), chip(shifted(pos, axis, 3))
            plans.append((axis, free, fixed, bufs, (up, down)))

        def each(free, body):
            total = SIDE ** len(free)

            @pl.loop(0, total)
            def _(i):
                if len(free) == 2:
                    body((i // SIDE, i % SIDE))
                elif len(free) == 1:
                    body((i,))
                else:
                    body(())

        def index_of(axis, free, fixed, at, spots):
            index = [None] * 3
            for a in fixed:
                index[a] = pos[a]
            index[axis] = at
            for a, s in zip(free, spots):
                index[a] = s
            return tuple(index)

        firsts = []
        for piece, (axis, free, fixed, bufs, ways) in enumerate(plans):
            if stage == 0:
                for copy in opening[piece]:
                    copy.wait_recv()
            far = (pos[axis] + 2) % SIDE
            copies = []
            for half in range(2):
                def fill(spots, half=half, axis=axis, free=free, fixed=fixed, bufs=bufs, piece=piece, far=far):
                    for n, (kind, c0, c1) in enumerate(RS_HALVES[piece][half]):
                        block = sums[piece](kind, index_of(axis, free, fixed, far, spots), c0, c1)
                        buf = bufs["sendA", half, n]
                        buf[spots + (FULL, FULL)] = block.astype(buf.dtype)

                each(free, fill)
                for n in range(len(RS_HALVES[piece][half])):
                    copies.append(send(bufs["sendA", half, n], bufs["recvA", half, n], ways[half]))
            firsts.append(copies)
        seconds = []
        for piece, (axis, free, fixed, bufs, ways) in enumerate(plans):
            for copy in firsts[piece]:
                copy.wait_recv()
            copies = []
            for way in range(2):
                at = (pos[axis] + (1, 3)[way]) % SIDE

                def fill(spots, way=way, axis=axis, free=free, fixed=fixed, bufs=bufs, piece=piece, at=at):
                    index = index_of(axis, free, fixed, at, spots)
                    n = 0
                    for half in range(2):
                        for m, (kind, c0, c1) in enumerate(RS_HALVES[piece][half]):
                            block = sums[piece](kind, index, c0, c1)
                            if half == way:
                                block = block + bufs["recvA", half, m][spots + (FULL, FULL)].astype(jnp.float32)
                            buf = bufs["sendB", way, n]
                            buf[spots + (FULL, FULL)] = block.astype(buf.dtype)
                            n += 1

                each(free, fill)
                for n in range(len(RS_PIECES[piece])):
                    copies.append(send(bufs["sendB", way, n], bufs["recvB", way, n], ways[way]))
            seconds.append(copies)
        for piece, (axis, free, fixed, bufs, ways) in enumerate(plans):
            for copy in seconds[piece]:
                copy.wait_recv()
            if stage < 2:
                total = {n: next(take) for n in range(len(RS_PIECES[piece]))}
            else:
                total = None

            def fill(spots, axis=axis, free=free, fixed=fixed, bufs=bufs, piece=piece, total=total):
                index = index_of(axis, free, fixed, pos[axis], spots)
                for n, (kind, c0, c1) in enumerate(RS_PIECES[piece]):
                    block = sums[piece](kind, index, c0, c1)
                    for way in range(2):
                        block = block + bufs["recvB", way, n][spots + (FULL, FULL)].astype(jnp.float32)
                    if total is None:
                        outs[kind][:, c0:c1] = block
                    else:
                        total[n][spots + (FULL, FULL)] = block

            each(free, fill)
            if total is not None:
                def partial(kind, index, c0, c1, total=total, piece=piece, free=free):
                    spots = tuple(index[a] for a in free)
                    for n, (k, s0, s1) in enumerate(RS_PIECES[piece]):
                        if k == kind and s0 <= c0 and c1 <= s1:
                            return total[n][spots + (FULL, pl.ds(c0 - s0, c1 - c0))]

                sums[piece] = partial
    for copy in send.sent:
        copy.wait_send()


def reduce_layer(*parts):
    parts = [p.reshape(2, SIDE, SIDE, SIDE, 8, c).astype(k) for p, c, k in zip(parts, RS_COLS, RS_KINDS)]
    scratch = [pltpu.VMEM((SIDE, SIDE, SIDE, 8, c), k) for c, k in zip(RS_COLS, RS_KINDS)]
    copies = sum(len(p) for p in RS_PIECES)
    for stage in range(3):
        lead = (SIDE,) * (2 - stage)
        for piece in range(3):
            for half in range(2):
                for kind, c0, c1 in RS_HALVES[piece][half]:
                    scratch += [pltpu.VMEM(lead + (8, c1 - c0), RS_KINDS[kind])] * 2
                    copies += 1
            for way in range(2):
                for kind, c0, c1 in RS_PIECES[piece]:
                    scratch += [pltpu.VMEM(lead + (8, c1 - c0), RS_KINDS[kind])] * 2
                    copies += 1
        if stage < 2:
            for piece in range(3):
                for kind, c0, c1 in RS_PIECES[piece]:
                    scratch += [pltpu.VMEM(lead + (8, c1 - c0), jnp.float32)]
    vmem = pl.BlockSpec(memory_space=pltpu.VMEM)
    return pl.pallas_call(
        reduce_kernel,
        out_shape=tuple(jax.ShapeDtypeStruct((8, c), jnp.float32) for c in RS_COLS),
        in_specs=[vmem] * 3,
        out_specs=(vmem,) * 3,
        scratch_shapes=scratch + [pltpu.SemaphoreType.DMA((copies,)), pltpu.SemaphoreType.DMA((copies,))],
        compiler_params=pltpu.CompilerParams(
            collective_id=1, has_side_effects=True, vmem_limit_bytes=60 * 1024 * 1024
        ),
        name="reduce_layer",
    )(*parts)


HEADS = 16


def layer_norm(values, scale_vec, offset):
    center = jnp.mean(values, -1, keepdims=True)
    centred = values - center
    spread = jnp.mean(centred * centred, -1, keepdims=True)
    inverse = lax.rsqrt(spread + 1e-05)
    normed = centred * inverse
    return (normed * scale_vec + offset, normed, inverse)


def norm_back(upstream, normed, inverse, scale_vec):
    scaled = upstream * scale_vec
    average = jnp.mean(scaled, -1, keepdims=True)
    project = jnp.mean(scaled * normed, -1, keepdims=True)
    return (
        inverse * (scaled - average - normed * project),
        jnp.sum(upstream * normed, 0),
        jnp.sum(upstream, 0),
    )


def times_transposed(left_mat, right_mat):
    return lax.dot_general(
        left_mat, right_mat, (((1,), (1,)), ((), ())), preferred_element_type=jnp.float32
    )


def transposed_times(left_mat, right_mat):
    return lax.dot_general(
        left_mat, right_mat, (((0,), (0,)), ((), ())), preferred_element_type=jnp.float32
    )


def per_device(
    tokens,
    teacher,
    lengths,
    routes,
    ln1_gain,
    ln1_bias,
    query_key_value_weight,
    output_weight,
    ln2_gain,
    ln2_bias,
    router_weight,
    w_in,
    w_down,
):
    group = tokens.shape[1]
    width = tokens.shape[2]
    head_dim = width // HEADS
    sources = lax.axis_size("expert")
    seq_len = group * lax.axis_size("dp")
    capacity = max(2, 2 * group // sources)
    core = lax.axis_index("dp")
    device = core * sources + lax.axis_index("expert")
    vectors = jnp.tile(jnp.stack([ln1_gain, ln1_bias, ln2_gain, ln2_bias]), (1, 8))
    vectors = jnp.where(jnp.arange(64)[None, :] // 8 == device % 8, vectors, 0)
    vectors = jnp.concatenate([vectors, jnp.zeros_like(vectors)], 0)
    layer = gather_layer(
        jnp.concatenate([query_key_value_weight, output_weight, router_weight, vectors], 1)
    )
    w_qkv = layer[:, : 3 * width]
    w_out = layer[:, 3 * width : 4 * width]
    w_router = layer[:, 4 * width : 4 * width + sources]
    vectors = layer[:, 4 * width + sources :].astype(jnp.float32)
    vectors = jnp.sum(vectors.reshape(16, 8, 8, 64), 1)
    gain_one, bias_one, gain_two, bias_two = [vectors[:, n].reshape(width) for n in range(4)]
    experts_whole = (
        lax.all_gather(w_in, "dp", axis=1, tiled=True),
        lax.all_gather(w_down, "dp", axis=1, tiled=True),
    )
    w_first = experts_whole[0][0]
    w_second = experts_whole[1][0]
    inputs = tokens[0].astype(jnp.float32)
    norm_full, normed_one, inverse_one = layer_norm(inputs, gain_one, bias_one)
    first_norm = norm_full.astype(jnp.bfloat16)
    query_key_value_rows = jnp.dot(
        first_norm, w_qkv, preferred_element_type=jnp.float32
    ).astype(jnp.bfloat16)
    queries = query_key_value_rows[:, :width].reshape(group, HEADS, head_dim)
    kv_whole = lax.all_gather(query_key_value_rows[:, width:], "dp", axis=0, tiled=True)
    key_rows = kv_whole[:, :width].reshape(seq_len, HEADS, head_dim)
    value_rows = kv_whole[:, width:].reshape(seq_len, HEADS, head_dim)
    query_pos = lax.axis_index("dp") * group + jnp.arange(group)
    key_pos = jnp.arange(seq_len)
    allowed = (key_pos[None, :] <= query_pos[:, None]) & (key_pos[None, :] < lengths[0])

    def score_block():
        scaled_raw = (
            jnp.einsum("qhd,khd->hqk", queries, key_rows, preferred_element_type=jnp.float32)
            * 0.125
        )
        return jnp.where(allowed[None], scaled_raw, -1e30)

    scores = score_block()
    maximum = jnp.max(scores, -1, keepdims=True)
    exponent = jnp.exp(scores - maximum)
    denominator = jnp.sum(exponent, -1, keepdims=True)
    log_total = maximum + jnp.log(denominator)
    probs_low = (exponent / denominator).astype(jnp.bfloat16)
    attention_result = jnp.einsum(
        "hqk,khd->qhd", probs_low, value_rows, preferred_element_type=jnp.float32
    )
    attention_result = attention_result.reshape(group, width).astype(jnp.bfloat16)
    residual_branch = jnp.dot(attention_result, w_out, preferred_element_type=jnp.float32)
    residual = inputs + residual_branch
    norm_two_full, normed_two, inverse_two = layer_norm(residual, gain_two, bias_two)
    second_norm = norm_two_full.astype(jnp.bfloat16)
    router_scores = jnp.dot(second_norm, w_router, preferred_element_type=jnp.float32)
    router_probs = jax.nn.softmax(router_scores, -1)
    route_ids = routes[0, :, 0]
    chosen = route_ids[:, None] == jnp.arange(sources)[None, :]
    gate_prob = jnp.sum(jnp.where(chosen, router_probs, 0.0), -1)
    ranking = jnp.cumsum(chosen.astype(jnp.int32), 0) - 1
    slot_ids = route_ids * capacity + jnp.sum(jnp.where(chosen, ranking, 0), -1)
    placing = (jnp.arange(sources * capacity)[:, None] == slot_ids[None, :]).astype(jnp.bfloat16)
    outgoing = jnp.dot(placing, second_norm, preferred_element_type=jnp.float32).astype(
        jnp.bfloat16
    )
    outgoing = outgoing.reshape(sources, capacity, width)
    received = lax.all_to_all(outgoing, "expert", split_axis=0, concat_axis=0, tiled=True)
    per_source = received.shape[1]
    valid_rows = (query_pos < lengths[0]).astype(jnp.float32)
    taught = teacher[0].astype(jnp.float32)
    gate_high = gate_prob.astype(jnp.bfloat16)
    gate_low = (gate_prob - gate_high.astype(jnp.float32)).astype(jnp.bfloat16)
    extras = jnp.stack([gate_high, gate_low, valid_rows.astype(jnp.bfloat16)], 1)
    extras = jnp.pad(extras, ((0, 0), (0, 125)))
    parting = jnp.concatenate([(residual - taught).astype(jnp.bfloat16), extras], 1)
    parting = jnp.dot(placing, parting, preferred_element_type=jnp.float32).astype(jnp.bfloat16)
    parted = lax.all_to_all(
        parting.reshape(sources, capacity, width + 128), "expert", split_axis=0, concat_axis=0, tiled=True
    ).reshape(-1, width + 128).astype(jnp.float32)
    flat_rows = received.reshape(-1, width)
    pre_act = jnp.dot(flat_rows, w_first, preferred_element_type=jnp.float32)
    activated = jax.nn.gelu(pre_act, approximate=True).astype(jnp.bfloat16)
    result_rows = jnp.dot(activated, w_second, preferred_element_type=jnp.float32).astype(
        jnp.bfloat16
    )
    produced = result_rows.reshape(sources, per_source, width)
    pre_kept = pre_act.reshape(sources, per_source, -1)
    returned = lax.all_to_all(produced, "expert", split_axis=0, concat_axis=0, tiled=True)
    expert_out = transposed_times(placing, returned.reshape(-1, width))
    mixed_out = (residual + gate_prob[:, None] * expert_out).astype(jnp.bfloat16)
    errors = mixed_out.astype(jnp.float32) - taught
    squares = jnp.sum(valid_rows[:, None] * errors * errors)
    count = jnp.sum(valid_rows)
    d_mixed = valid_rows[:, None] * errors
    d_gate = jnp.sum(d_mixed * expert_out, -1)
    gate_rows = parted[:, width : width + 1] + parted[:, width + 1 : width + 2]
    valid_sent = parted[:, width + 2 : width + 3]
    row_errors = parted[:, :width] + gate_rows * result_rows.astype(jnp.float32)
    d_recv = (gate_rows * valid_sent * row_errors).astype(jnp.bfloat16)
    pre_rows = pre_kept.reshape(d_recv.shape[0], -1)
    d_act = times_transposed(d_recv, w_second)
    act_rows, gelu_back = jax.vjp(lambda inner: jax.nn.gelu(inner, approximate=True), pre_rows)
    d_pre = gelu_back(d_act)[0].astype(jnp.bfloat16)
    act_low = act_rows.astype(jnp.bfloat16)
    arrived_rows = received.reshape(-1, width)
    d_rows = (
        times_transposed(d_pre, w_first).astype(jnp.bfloat16).reshape(sources, capacity, width)
    )
    d_back = lax.all_to_all(d_rows, "expert", split_axis=0, concat_axis=0, tiled=True)
    d_norm_expert = transposed_times(placing, d_back.reshape(-1, width))
    d_logits = (d_gate * gate_prob)[:, None] * (chosen.astype(jnp.float32) - router_probs)
    router_full = w_router.astype(jnp.float32)
    grad_router = jnp.dot(
        second_norm.astype(jnp.float32).T, d_logits, precision=lax.Precision.HIGHEST
    )
    d_norm_two = d_norm_expert + jnp.dot(d_logits, router_full.T, precision=lax.Precision.HIGHEST)
    d_resid_part, grad_gain_two, grad_bias_two = norm_back(
        d_norm_two, normed_two, inverse_two, gain_two
    )
    d_resid = d_mixed + d_resid_part
    d_branch = d_resid.astype(jnp.bfloat16)
    grad_out = transposed_times(attention_result, d_branch)
    d_attended = (
        times_transposed(d_branch, w_out)
        .astype(jnp.bfloat16)
        .reshape(group, HEADS, head_dim)
    )
    probs_again = jnp.exp(score_block() - log_total)
    d_probs = jnp.einsum("qhd,khd->hqk", d_attended, value_rows, preferred_element_type=jnp.float32)
    delta_sum = jnp.sum(probs_again * d_probs, -1, keepdims=True)
    d_scores = (probs_again * (d_probs - delta_sum)).astype(jnp.bfloat16)
    d_queries = (
        jnp.einsum("hqk,khd->qhd", d_scores, key_rows, preferred_element_type=jnp.float32) * 0.125
    )
    d_keys = (
        jnp.einsum("hqk,qhd->khd", d_scores, queries, preferred_element_type=jnp.float32) * 0.125
    )
    d_values = jnp.einsum("hqk,qhd->khd", probs_low, d_attended, preferred_element_type=jnp.float32)
    d_kv_whole = jnp.concatenate(
        [d_keys.reshape(seq_len, width), d_values.reshape(seq_len, width)], 1
    )
    d_kv = lax.psum_scatter(d_kv_whole.astype(jnp.bfloat16), "dp", scatter_dimension=0, tiled=True)
    d_qkv = jnp.concatenate([d_queries.reshape(group, width).astype(jnp.bfloat16), d_kv], 1)
    grad_qkv = transposed_times(first_norm, d_qkv)
    d_norm_one = times_transposed(d_qkv, w_qkv)
    d_input_part, grad_gain_one, grad_bias_one = norm_back(
        d_norm_one, normed_one, inverse_one, gain_one
    )
    grad_tokens = d_resid + d_input_part
    vector_grads = jnp.stack(
        [grad_gain_one, grad_bias_one, grad_gain_two, grad_bias_two]
    ).reshape(4, 128, 8)
    vector_grads = jnp.pad(vector_grads.transpose(1, 0, 2), ((0, 0), (0, 4), (0, 56)))
    totals = jnp.zeros((8, 128), jnp.float32).at[0, 0].set(squares).at[1, 0].set(count)
    side = jnp.concatenate(
        [grad_router.reshape(128, 8, sources), vector_grads, jnp.broadcast_to(totals[None], (128, 8, 128))], 2
    )
    grad_qkv, grad_out, side = reduce_layer(grad_qkv, grad_out, side)
    grad_router = side[:, :sources]
    vector_grads = side[:4, sources : sources + 8]
    loss_value = side[0, 128] / (side[1, 128] * width)
    grad_down = transposed_times(act_low, d_recv)
    grad_in = transposed_times(arrived_rows, d_pre)
    expert_grads = (
        lax.psum_scatter(
            grad_in[None].astype(jnp.bfloat16), "dp", scatter_dimension=1, tiled=True
        ).astype(jnp.float32),
        lax.psum_scatter(
            grad_down[None].astype(jnp.bfloat16), "dp", scatter_dimension=1, tiled=True
        ).astype(jnp.float32),
    )
    grad_in_out = expert_grads[0]
    grad_down_out = expert_grads[1]
    return (
        mixed_out[None],
        loss_value,
        grad_tokens[None],
        vector_grads[0],
        vector_grads[1],
        grad_qkv,
        grad_out,
        vector_grads[2],
        vector_grads[3],
        grad_router,
        grad_in_out,
        grad_down_out,
    )


def solution(mesh):
    placed = (
        P("expert", "dp", None),
        P("expert", "dp", None),
        P("expert"),
        P("expert", "dp", None),
        P(("dp", "expert")),
        P(("dp", "expert")),
        P(("dp", "expert"), None),
        P(("dp", "expert"), None),
        P(("dp", "expert")),
        P(("dp", "expert")),
        P(("dp", "expert"), None),
        P("expert", "dp", None),
        P("expert", "dp", None),
    )
    return jax.shard_map(
        per_device,
        mesh=mesh,
        in_specs=placed,
        out_specs=(
            P("expert", "dp", None),
            P(),
            P("expert", "dp", None),
            P(("dp", "expert")),
            P(("dp", "expert")),
            P(("dp", "expert"), None),
            P(("dp", "expert"), None),
            P(("dp", "expert")),
            P(("dp", "expert")),
            P(("dp", "expert"), None),
            P("expert", "dp", None),
            P("expert", "dp", None),
        ),
        check_vma=False,
    )
```

```python
import jax
import jax.numpy as jnp
from jax import lax
from jax.experimental import pallas as pl
from jax.experimental.pallas import tpu as pltpu
from jax.sharding import PartitionSpec as P

MESH = pl.DeviceIdType.MESH
SIDE = 4
FULL = slice(None)

AG_COLS = 4224
AG_PIECES = ((0, 768, 1408), (1408, 2176, 2816), (2816, 3584, 4224))


def place(region, c0, c1):
    return tuple(region) + (FULL, pl.ds(c0, c1 - c0))


def coords():
    e = lax.axis_index("expert")
    return [e // 16, (e // 4) % 4, e % 4]


def shifted(pos, axis, by):
    out = list(pos)
    out[axis] = (pos[axis] + by) % SIDE
    return out


def chip(pos):
    return {"expert": pos[0] * 16 + pos[1] * 4 + pos[2]}


def neighbours(pos):
    return [chip(shifted(pos, axis, by)) for axis in range(3) for by in (1, 3)]


def greet(pos, core):
    barrier = pltpu.get_barrier_semaphore()
    for other in neighbours(pos) + [{"dp": 1 - core}]:
        pl.semaphore_signal(barrier, inc=1, device_id=other, device_id_type=MESH)
    pl.semaphore_wait(barrier, 7)


class Sender:
    def __init__(self, send_sems, recv_sems):
        self.send_sems, self.recv_sems, self.count, self.sent = send_sems, recv_sems, 0, []

    def __call__(self, src, dst, device):
        copy = pltpu.make_async_remote_copy(
            src_ref=src,
            dst_ref=dst,
            send_sem=self.send_sems.at[self.count],
            recv_sem=self.recv_sems.at[self.count],
            device_id=device,
            device_id_type=MESH,
        )
        copy.start()
        self.count += 1
        self.sent.append(copy)
        return copy


def gather_kernel(shard, w_in, w_down, whole, in_other, down_other, own_sem, send_sems, recv_sems):
    pos = coords()
    core = lax.axis_index("dp")
    partner = {"dp": 1 - core}
    own = pltpu.make_async_copy(shard, whole.at[(core, *pos)], own_sem)
    own.start()
    greet(pos, core)
    send = Sender(send_sems, recv_sems)
    across = [send(w_in, in_other, partner), send(w_down, down_other, partner)]
    own.wait()

    def share(region, c0, c1, device):
        spot = whole.at[place([core] + region, c0, c1)]
        return send(spot, spot, device)

    for stage in range(3):
        first = []
        for piece, (c0, mid, c1) in enumerate(AG_PIECES):
            order = [(piece + step) % 3 for step in range(3)]
            axis = order[stage]
            done = order[:stage]
            region = [FULL if a in done else pos[a] for a in range(3)]
            up, down = chip(shifted(pos, axis, 1)), chip(shifted(pos, axis, 3))
            first.append((axis, region, up, down, share(region, c0, c1, up), share(region, c0, c1, down)))
        if stage == 2:
            for (c0, mid, c1), (axis, region, up, down, _, _) in zip(AG_PIECES, first):
                across.append(share(region, c0, c1, partner))
        second = []
        for (c0, mid, c1), (axis, region, up, down, to_up, to_down) in zip(AG_PIECES, first):
            below, above = list(region), list(region)
            below[axis], above[axis] = (pos[axis] + 3) % SIDE, (pos[axis] + 1) % SIDE
            to_up.wait_recv()
            on_up = share(below, c0, mid, up)
            to_down.wait_recv()
            on_down = share(above, mid, c1, down)
            second.append((on_up, on_down))
            if stage == 2:
                across.append(share(below, c0, c1, partner))
                across.append(share(above, c0, c1, partner))
        for (c0, mid, c1), (axis, region, up, down, _, _), (on_up, on_down) in zip(AG_PIECES, first, second):
            on_up.wait_recv()
            on_down.wait_recv()
            if stage == 2:
                far = list(region)
                far[axis] = (pos[axis] + 2) % SIDE
                across.append(share(far, c0, c1, partner))
    for copy in across:
        copy.wait_recv()
    for copy in send.sent:
        copy.wait_send()


def gather_layer(shard, w_in, w_down):
    copies = 3 * 3 * 4 + 3 * 4 + 2
    anywhere = pl.BlockSpec(memory_space=pl.ANY)
    whole, in_other, down_other = pl.pallas_call(
        gather_kernel,
        out_shape=(
            jax.ShapeDtypeStruct((2, SIDE, SIDE, SIDE, 8, AG_COLS), jnp.bfloat16),
            jax.ShapeDtypeStruct(w_in.shape, w_in.dtype),
            jax.ShapeDtypeStruct(w_down.shape, w_down.dtype),
        ),
        in_specs=[anywhere] * 3,
        out_specs=(anywhere,) * 3,
        scratch_shapes=[
            pltpu.SemaphoreType.DMA,
            pltpu.SemaphoreType.DMA((copies,)),
            pltpu.SemaphoreType.DMA((copies,)),
        ],
        compiler_params=pltpu.CompilerParams(collective_id=0, has_side_effects=True),
        name="gather_layer",
    )(shard, w_in, w_down)
    return whole.reshape(1024, AG_COLS), in_other, down_other


RS_COLS = (3072, 1024, 256)
RS_KINDS = (jnp.bfloat16, jnp.bfloat16, jnp.float32)
RS_HALVES = (
    (((0, 0, 768),), ((0, 768, 1536),)),
    (((0, 1536, 2304),), ((0, 2304, 3072),)),
    (((1, 0, 768),), ((1, 768, 1024), (2, 0, 256))),
)
RS_PIECES = tuple(h0 + h1 for h0, h1 in RS_HALVES)


def reduce_kernel(*rest):
    source, outs, rest = rest[:3], rest[3:6], rest[6:]
    refs, (send_sems, recv_sems) = list(rest[:-2]), rest[-2:]
    take = iter(refs)
    pos = coords()
    core = lax.axis_index("dp")
    partner = {"dp": 1 - core}
    greet(pos, core)
    send = Sender(send_sems, recv_sems)
    landed = (next(take), next(take), next(take))

    opening = []
    for piece in range(3):
        copies = []
        for kind, c0, c1 in RS_PIECES[piece]:
            copies.append(
                send(
                    source[kind].at[place([1 - core, FULL, FULL, FULL], c0, c1)],
                    landed[kind].at[place([FULL, FULL, FULL], c0, c1)],
                    partner,
                )
            )
        opening.append(copies)

    def whole_sum(kind, index, c0, c1):
        spot = index + (FULL, pl.ds(c0, c1 - c0))
        mine = source[kind][(core,) + spot].astype(jnp.float32)
        return mine + landed[kind][spot].astype(jnp.float32)

    sums = []
    for piece in range(3):
        sums.append(whole_sum)

    for stage in range(3):
        plans = []
        for piece in range(3):
            order = [(piece + step) % 3 for step in range(3)]
            axis = order[stage]
            free = sorted(order[stage + 1:])
            fixed = order[:stage]
            bufs = {}
            for half in range(2):
                for n, (kind, c0, c1) in enumerate(RS_HALVES[piece][half]):
                    for what in ("sendA", "recvA"):
                        bufs[what, half, n] = next(take)
            for way in range(2):
                for n, (kind, c0, c1) in enumerate(RS_PIECES[piece]):
                    for what in ("sendB", "recvB"):
                        bufs[what, way, n] = next(take)
            up, down = chip(shifted(pos, axis, 1)), chip(shifted(pos, axis, 3))
            plans.append((axis, free, fixed, bufs, (up, down)))

        def each(free, body):
            total = SIDE ** len(free)

            @pl.loop(0, total)
            def _(i):
                if len(free) == 2:
                    body((i // SIDE, i % SIDE))
                elif len(free) == 1:
                    body((i,))
                else:
                    body(())

        def index_of(axis, free, fixed, at, spots):
            index = [None] * 3
            for a in fixed:
                index[a] = pos[a]
            index[axis] = at
            for a, s in zip(free, spots):
                index[a] = s
            return tuple(index)

        firsts = []
        for piece, (axis, free, fixed, bufs, ways) in enumerate(plans):
            if stage == 0:
                for copy in opening[piece]:
                    copy.wait_recv()
            far = (pos[axis] + 2) % SIDE
            copies = []
            for half in range(2):
                def fill(spots, half=half, axis=axis, free=free, fixed=fixed, bufs=bufs, piece=piece, far=far):
                    for n, (kind, c0, c1) in enumerate(RS_HALVES[piece][half]):
                        block = sums[piece](kind, index_of(axis, free, fixed, far, spots), c0, c1)
                        buf = bufs["sendA", half, n]
                        buf[spots + (FULL, FULL)] = block.astype(buf.dtype)

                each(free, fill)
                for n in range(len(RS_HALVES[piece][half])):
                    copies.append(send(bufs["sendA", half, n], bufs["recvA", half, n], ways[half]))
            firsts.append(copies)
        seconds = []
        for piece, (axis, free, fixed, bufs, ways) in enumerate(plans):
            for copy in firsts[piece]:
                copy.wait_recv()
            copies = []
            for way in range(2):
                at = (pos[axis] + (1, 3)[way]) % SIDE

                def fill(spots, way=way, axis=axis, free=free, fixed=fixed, bufs=bufs, piece=piece, at=at):
                    index = index_of(axis, free, fixed, at, spots)
                    n = 0
                    for half in range(2):
                        for m, (kind, c0, c1) in enumerate(RS_HALVES[piece][half]):
                            block = sums[piece](kind, index, c0, c1)
                            if half == way:
                                block = block + bufs["recvA", half, m][spots + (FULL, FULL)].astype(jnp.float32)
                            buf = bufs["sendB", way, n]
                            buf[spots + (FULL, FULL)] = block.astype(buf.dtype)
                            n += 1

                each(free, fill)
                for n in range(len(RS_PIECES[piece])):
                    copies.append(send(bufs["sendB", way, n], bufs["recvB", way, n], ways[way]))
            seconds.append(copies)
        for piece, (axis, free, fixed, bufs, ways) in enumerate(plans):
            for copy in seconds[piece]:
                copy.wait_recv()
            if stage < 2:
                total = {n: next(take) for n in range(len(RS_PIECES[piece]))}
            else:
                total = None

            def fill(spots, axis=axis, free=free, fixed=fixed, bufs=bufs, piece=piece, total=total):
                index = index_of(axis, free, fixed, pos[axis], spots)
                for n, (kind, c0, c1) in enumerate(RS_PIECES[piece]):
                    block = sums[piece](kind, index, c0, c1)
                    for way in range(2):
                        block = block + bufs["recvB", way, n][spots + (FULL, FULL)].astype(jnp.float32)
                    if total is None:
                        outs[kind][:, c0:c1] = block
                    else:
                        total[n][spots + (FULL, FULL)] = block

            each(free, fill)
            if total is not None:
                def partial(kind, index, c0, c1, total=total, piece=piece, free=free):
                    spots = tuple(index[a] for a in free)
                    for n, (k, s0, s1) in enumerate(RS_PIECES[piece]):
                        if k == kind and s0 <= c0 and c1 <= s1:
                            return total[n][spots + (FULL, pl.ds(c0 - s0, c1 - c0))]

                sums[piece] = partial
    for copy in send.sent:
        copy.wait_send()


def reduce_layer(*parts):
    parts = [p.reshape(2, SIDE, SIDE, SIDE, 8, c).astype(k) for p, c, k in zip(parts, RS_COLS, RS_KINDS)]
    scratch = [pltpu.VMEM((SIDE, SIDE, SIDE, 8, c), k) for c, k in zip(RS_COLS, RS_KINDS)]
    copies = sum(len(p) for p in RS_PIECES)
    for stage in range(3):
        lead = (SIDE,) * (2 - stage)
        for piece in range(3):
            for half in range(2):
                for kind, c0, c1 in RS_HALVES[piece][half]:
                    scratch += [pltpu.VMEM(lead + (8, c1 - c0), RS_KINDS[kind])] * 2
                    copies += 1
            for way in range(2):
                for kind, c0, c1 in RS_PIECES[piece]:
                    scratch += [pltpu.VMEM(lead + (8, c1 - c0), RS_KINDS[kind])] * 2
                    copies += 1
        if stage < 2:
            for piece in range(3):
                for kind, c0, c1 in RS_PIECES[piece]:
                    scratch += [pltpu.VMEM(lead + (8, c1 - c0), jnp.float32)]
    vmem = pl.BlockSpec(memory_space=pltpu.VMEM)
    return pl.pallas_call(
        reduce_kernel,
        out_shape=tuple(jax.ShapeDtypeStruct((8, c), jnp.float32) for c in RS_COLS),
        in_specs=[vmem] * 3,
        out_specs=(vmem,) * 3,
        scratch_shapes=scratch + [pltpu.SemaphoreType.DMA((copies,)), pltpu.SemaphoreType.DMA((copies,))],
        compiler_params=pltpu.CompilerParams(
            collective_id=1, has_side_effects=True, vmem_limit_bytes=60 * 1024 * 1024
        ),
        name="reduce_layer",
    )(*parts)


ROWS = 512
WIDTH = 1024
HIDDEN = 4096
HALF_IN = WIDTH // 2
HALF_FF = HIDDEN // 2
EXTRA = 128
TILE = 512
N_TILES = HIDDEN // TILE
HALF_TILES = N_TILES // 2
CURVE = 0.7978845608028654


def dot_nt(a, b):
    return lax.dot_general(a, b, (((1,), (1,)), ((), ())), preferred_element_type=jnp.float32)


def dot_nn(a, b):
    return lax.dot_general(a, b, (((1,), (0,)), ((), ())), preferred_element_type=jnp.float32)


def dot_tn(a, b):
    return lax.dot_general(a, b, (((0,), (0,)), ((), ())), preferred_element_type=jnp.float32)


def to_chips(pos, me, source, target, send_sem, recv_sem):
    @pl.loop(0, 64)
    def _(n):
        there = [(pos[0] + 2 + n // 16) % 4, (pos[1] + 2 + (n // 4) % 4) % 4, (pos[2] + 2 + n % 4) % 4]
        d = there[0] * 16 + there[1] * 4 + there[2]

        @pl.when(n != 42)
        def _():
            pltpu.make_async_remote_copy(
                src_ref=source.at[d],
                dst_ref=target.at[me],
                send_sem=send_sem,
                recv_sem=recv_sem,
                device_id={"expert": d},
                device_id_type=MESH,
            ).start()


def all_but_one(ref, sem):
    pltpu.make_async_copy(ref.at[pl.ds(0, 63)], ref.at[pl.ds(0, 63)], sem).wait()


def expert_kernel(
    x, r, w1_own, w1_other, w2_own, w2_other,
    y_back, d_back, g1, g2,
    w1, w2, x_in, r_in, xb, xt, act, slope, d_pre, acc, d_exp, out_rows,
    sent1, sent2, got1, got2, stage,
    w_sems, x_sems, r_sems, y_sems, d_sems, own_sems, pass_s, pass_r, out_sems,
):
    pos = coords()
    me = lax.axis_index("expert")
    core = lax.axis_index("dp")
    loads = [
        pltpu.make_async_copy(w1_own, w1.at[core], w_sems.at[0]),
        pltpu.make_async_copy(w1_other, w1.at[1 - core], w_sems.at[1]),
        pltpu.make_async_copy(w2_own, w2.at[core], w_sems.at[2]),
        pltpu.make_async_copy(w2_other, w2.at[1 - core], w_sems.at[3]),
    ]
    barrier = pltpu.get_barrier_semaphore()

    @pl.loop(1, 64)
    def _(n):
        pl.semaphore_signal(barrier, inc=1, device_id={"expert": (me + n) % 64}, device_id_type=MESH)

    pl.semaphore_signal(barrier, inc=1, device_id={"dp": 1 - core}, device_id_type=MESH)
    own_x = pltpu.make_async_copy(x.at[me], x_in.at[me], own_sems.at[0])
    own_r = pltpu.make_async_copy(r.at[me], r_in.at[me], own_sems.at[1])
    own_x.start()
    own_r.start()
    for load in loads:
        load.start()
    pl.semaphore_wait(barrier, 64)
    to_chips(pos, me, x, x_in, x_sems.at[0], x_sems.at[1])
    to_chips(pos, me, r, r_in, r_sems.at[0], r_sems.at[1])
    own_x.wait()
    all_but_one(x_in, x_sems.at[1])
    for load in loads:
        load.wait()

    @pl.loop(0, 8)
    def _(i):
        rows = x_in[pl.ds(i * 8, 8)].astype(jnp.float32).reshape(64, WIDTH)
        xb[pl.ds(pl.multiple_of(i * 64, 64), 64), :] = rows.astype(jnp.bfloat16)

    acc[...] = jnp.zeros_like(acc)

    @pl.loop(0, N_TILES)
    def _(c):
        cols = pl.ds(pl.multiple_of(c * TILE, TILE), TILE)
        pre = dot_nn(xb[:, :HALF_IN], w1[0, :, cols]) + dot_nn(xb[:, HALF_IN:], w1[1, :, cols])
        square = pre * pre
        t = jnp.tanh(CURVE * pre * (1.0 + 0.044715 * square))
        low = (0.5 * pre * (1.0 + t)).astype(jnp.bfloat16)
        act[:, cols] = low
        slope[:, cols] = 0.5 * (1.0 + t) + (0.5 * CURVE) * pre * (1.0 - t * t) * (1.0 + (3 * 0.044715) * square)
        half = c // HALF_TILES
        ff = pl.ds(pl.multiple_of((c % HALF_TILES) * TILE, TILE), TILE)
        acc[...] += dot_nn(low, w2[half, ff, :])

    own_r.wait()
    all_but_one(r_in, r_sems.at[1])

    @pl.loop(0, 8)
    def _(i):
        rows = pl.ds(pl.multiple_of(i * 64, 64), 64)
        low = acc[rows, :].astype(jnp.bfloat16)
        out = low.astype(jnp.float32)
        out_rows[pl.ds(i * 8, 8)] = out.reshape(8, 8, WIDTH).astype(jnp.bfloat16)
        parted = r_in[pl.ds(i * 8, 8)].astype(jnp.float32).reshape(64, WIDTH + EXTRA)
        gate = parted[:, WIDTH : WIDTH + 1] + parted[:, WIDTH + 1 : WIDTH + 2]
        valid = parted[:, WIDTH + 2 : WIDTH + 3]
        d_exp[rows, :] = (gate * valid * (parted[:, :WIDTH] + gate * out)).astype(jnp.bfloat16)

    own_y = pltpu.make_async_copy(out_rows.at[me], y_back.at[me], own_sems.at[2])
    own_y.start()
    to_chips(pos, me, out_rows, y_back, y_sems.at[0], y_sems.at[1])
    acc[...] = jnp.zeros_like(acc)

    @pl.loop(0, N_TILES)
    def _(c):
        cols = pl.ds(pl.multiple_of(c * TILE, TILE), TILE)
        half = c // HALF_TILES
        ff = pl.ds(pl.multiple_of((c % HALF_TILES) * TILE, TILE), TILE)
        d_act = dot_nt(d_exp[...], w2[half, ff, :])
        low = (slope[:, cols] * d_act).astype(jnp.bfloat16)
        d_pre[:, cols] = low
        acc[:, :HALF_IN] += dot_nt(low, w1[0, :, cols])
        acc[:, HALF_IN:] += dot_nt(low, w1[1, :, cols])

    own_y.wait()
    all_but_one(out_rows, y_sems.at[0])

    @pl.loop(0, 8)
    def _(i):
        rows = pl.ds(pl.multiple_of(i * 64, 64), 64)
        out_rows[pl.ds(i * 8, 8)] = acc[rows, :].reshape(8, 8, WIDTH).astype(jnp.bfloat16)

    own_d = pltpu.make_async_copy(out_rows.at[me], d_back.at[me], own_sems.at[3])
    own_d.start()
    to_chips(pos, me, out_rows, d_back, d_sems.at[0], d_sems.at[1])

    xt[...] = xb[...].astype(jnp.float32).T.astype(jnp.bfloat16)

    def passed(buf, got, c, base):
        return pltpu.make_async_remote_copy(
            src_ref=buf.at[c],
            dst_ref=got.at[c],
            send_sem=pass_s.at[base + c],
            recv_sem=pass_r.at[base + c],
            device_id={"dp": 1 - core},
            device_id_type=MESH,
        )

    def in_rows(half):
        return xt[pl.ds(pl.multiple_of(half * HALF_IN, HALF_IN), HALF_IN), :]

    @pl.loop(0, N_TILES)
    def _(c):
        cols = pl.ds(pl.multiple_of(c * TILE, TILE), TILE)
        sent1[c] = dot_nn(in_rows(1 - core), d_pre[:, cols]).astype(jnp.bfloat16)
        passed(sent1, got1, c, 0).start()

    @pl.loop(0, HALF_TILES)
    def _(c):
        cols = pl.ds(pl.multiple_of((1 - core) * HALF_FF + c * TILE, TILE), TILE)
        sent2[c] = dot_tn(act[:, cols], d_exp[...]).astype(jnp.bfloat16)
        passed(sent2, got2, c, N_TILES).start()

    def out1(c, slot):
        cols = pl.ds(pl.multiple_of(c * TILE, TILE), TILE)
        return pltpu.make_async_copy(stage.at[slot, :, pl.ds(0, TILE)], g1.at[:, cols], out_sems.at[slot])

    def out2(c, slot):
        rows = pl.ds(pl.multiple_of(c * TILE, TILE), TILE)
        return pltpu.make_async_copy(stage.at[slot], g2.at[rows, :], out_sems.at[slot])

    @pl.loop(0, N_TILES)
    def _(c):
        slot = c % 2
        cols = pl.ds(pl.multiple_of(c * TILE, TILE), TILE)

        @pl.when(c >= 2)
        def _():
            out1(c - 2, slot).wait()

        passed(sent1, got1, c, 0).wait_recv()
        stage[slot, :, pl.ds(0, TILE)] = dot_nn(in_rows(core), d_pre[:, cols]) + got1[c].astype(jnp.float32)
        out1(c, slot).start()

    out1(N_TILES - 2, 0).wait()
    out1(N_TILES - 1, 1).wait()

    @pl.loop(0, HALF_TILES)
    def _(c):
        slot = c % 2
        cols = pl.ds(pl.multiple_of(core * HALF_FF + c * TILE, TILE), TILE)

        @pl.when(c >= 2)
        def _():
            out2(c - 2, slot).wait()

        passed(sent2, got2, c, N_TILES).wait_recv()
        stage[slot] = dot_tn(act[:, cols], d_exp[...]) + got2[c].astype(jnp.float32)
        out2(c, slot).start()

    out2(HALF_TILES - 2, 0).wait()
    out2(HALF_TILES - 1, 1).wait()

    @pl.loop(0, N_TILES)
    def _(c):
        passed(sent1, got1, c, 0).wait_send()

    @pl.loop(0, HALF_TILES)
    def _(c):
        passed(sent2, got2, c, N_TILES).wait_send()

    own_d.wait()
    all_but_one(x_in, x_sems.at[0])
    all_but_one(r_in, r_sems.at[0])
    all_but_one(out_rows, d_sems.at[0])
    all_but_one(out_rows, y_sems.at[1])
    all_but_one(out_rows, d_sems.at[1])


def experts(x, r, w1_own, w1_other, w2_own, w2_other):
    low, wide = jnp.bfloat16, jnp.float32
    anywhere = pl.BlockSpec(memory_space=pl.ANY)
    return pl.pallas_call(
        expert_kernel,
        out_shape=(
            jax.ShapeDtypeStruct((64, 8, WIDTH), low),
            jax.ShapeDtypeStruct((64, 8, WIDTH), low),
            jax.ShapeDtypeStruct((HALF_IN, HIDDEN), wide),
            jax.ShapeDtypeStruct((HALF_FF, WIDTH), wide),
        ),
        in_specs=[anywhere] * 6,
        out_specs=(anywhere,) * 4,
        scratch_shapes=[
            pltpu.VMEM((2, HALF_IN, HIDDEN), low),
            pltpu.VMEM((2, HALF_FF, WIDTH), low),
            pltpu.VMEM((64, 8, WIDTH), low),
            pltpu.VMEM((64, 8, WIDTH + EXTRA), low),
            pltpu.VMEM((ROWS, WIDTH), low),
            pltpu.VMEM((WIDTH, ROWS), low),
            pltpu.VMEM((ROWS, HIDDEN), low),
            pltpu.VMEM((ROWS, HIDDEN), wide),
            pltpu.VMEM((ROWS, HIDDEN), low),
            pltpu.VMEM((ROWS, WIDTH), wide),
            pltpu.VMEM((ROWS, WIDTH), low),
            pltpu.VMEM((64, 8, WIDTH), low),
            pltpu.VMEM((N_TILES, HALF_IN, TILE), low),
            pltpu.VMEM((HALF_TILES, TILE, WIDTH), low),
            pltpu.VMEM((N_TILES, HALF_IN, TILE), low),
            pltpu.VMEM((HALF_TILES, TILE, WIDTH), low),
            pltpu.VMEM((2, HALF_IN, WIDTH), wide),
            pltpu.SemaphoreType.DMA((4,)),
            pltpu.SemaphoreType.DMA((2,)),
            pltpu.SemaphoreType.DMA((2,)),
            pltpu.SemaphoreType.DMA((2,)),
            pltpu.SemaphoreType.DMA((2,)),
            pltpu.SemaphoreType.DMA((4,)),
            pltpu.SemaphoreType.DMA((N_TILES + HALF_TILES,)),
            pltpu.SemaphoreType.DMA((N_TILES + HALF_TILES,)),
            pltpu.SemaphoreType.DMA((2,)),
        ],
        compiler_params=pltpu.CompilerParams(
            collective_id=2, has_side_effects=True, vmem_limit_bytes=63 * 1024 * 1024
        ),
        name="experts",
    )(x, r, w1_own, w1_other, w2_own, w2_other)


HEADS = 16


def layer_norm(values, scale_vec, offset):
    center = jnp.mean(values, -1, keepdims=True)
    centred = values - center
    spread = jnp.mean(centred * centred, -1, keepdims=True)
    inverse = lax.rsqrt(spread + 1e-05)
    normed = centred * inverse
    return (normed * scale_vec + offset, normed, inverse)


def norm_back(upstream, normed, inverse, scale_vec):
    scaled = upstream * scale_vec
    average = jnp.mean(scaled, -1, keepdims=True)
    project = jnp.mean(scaled * normed, -1, keepdims=True)
    return (
        inverse * (scaled - average - normed * project),
        jnp.sum(upstream * normed, 0),
        jnp.sum(upstream, 0),
    )


def times_transposed(left_mat, right_mat):
    return lax.dot_general(
        left_mat, right_mat, (((1,), (1,)), ((), ())), preferred_element_type=jnp.float32
    )


def transposed_times(left_mat, right_mat):
    return lax.dot_general(
        left_mat, right_mat, (((0,), (0,)), ((), ())), preferred_element_type=jnp.float32
    )


def per_device(
    tokens,
    teacher,
    lengths,
    routes,
    ln1_gain,
    ln1_bias,
    query_key_value_weight,
    output_weight,
    ln2_gain,
    ln2_bias,
    router_weight,
    w_in,
    w_down,
):
    group = tokens.shape[1]
    width = tokens.shape[2]
    head_dim = width // HEADS
    sources = lax.axis_size("expert")
    seq_len = group * lax.axis_size("dp")
    capacity = max(2, 2 * group // sources)
    core = lax.axis_index("dp")
    device = core * sources + lax.axis_index("expert")
    vectors = jnp.tile(jnp.stack([ln1_gain, ln1_bias, ln2_gain, ln2_bias]), (1, 8))
    vectors = jnp.where(jnp.arange(64)[None, :] // 8 == device % 8, vectors, 0)
    vectors = jnp.concatenate([vectors, jnp.zeros_like(vectors)], 0)
    layer, in_other, down_other = gather_layer(
        jnp.concatenate([query_key_value_weight, output_weight, router_weight, vectors], 1),
        w_in[0],
        w_down[0],
    )
    w_qkv = layer[:, : 3 * width]
    w_out = layer[:, 3 * width : 4 * width]
    w_router = layer[:, 4 * width : 4 * width + sources]
    vectors = layer[:, 4 * width + sources :].astype(jnp.float32)
    vectors = jnp.sum(vectors.reshape(16, 8, 8, 64), 1)
    gain_one, bias_one, gain_two, bias_two = [vectors[:, n].reshape(width) for n in range(4)]
    inputs = tokens[0].astype(jnp.float32)
    norm_full, normed_one, inverse_one = layer_norm(inputs, gain_one, bias_one)
    first_norm = norm_full.astype(jnp.bfloat16)
    query_key_value_rows = jnp.dot(
        first_norm, w_qkv, preferred_element_type=jnp.float32
    ).astype(jnp.bfloat16)
    queries = query_key_value_rows[:, :width].reshape(group, HEADS, head_dim)
    kv_whole = lax.all_gather(query_key_value_rows[:, width:], "dp", axis=0, tiled=True)
    key_rows = kv_whole[:, :width].reshape(seq_len, HEADS, head_dim)
    value_rows = kv_whole[:, width:].reshape(seq_len, HEADS, head_dim)
    query_pos = lax.axis_index("dp") * group + jnp.arange(group)
    key_pos = jnp.arange(seq_len)
    allowed = (key_pos[None, :] <= query_pos[:, None]) & (key_pos[None, :] < lengths[0])

    def score_block():
        scaled_raw = (
            jnp.einsum("qhd,khd->hqk", queries, key_rows, preferred_element_type=jnp.float32)
            * 0.125
        )
        return jnp.where(allowed[None], scaled_raw, -1e30)

    scores = score_block()
    maximum = jnp.max(scores, -1, keepdims=True)
    exponent = jnp.exp(scores - maximum)
    denominator = jnp.sum(exponent, -1, keepdims=True)
    log_total = maximum + jnp.log(denominator)
    probs_low = (exponent / denominator).astype(jnp.bfloat16)
    attention_result = jnp.einsum(
        "hqk,khd->qhd", probs_low, value_rows, preferred_element_type=jnp.float32
    )
    attention_result = attention_result.reshape(group, width).astype(jnp.bfloat16)
    residual_branch = jnp.dot(attention_result, w_out, preferred_element_type=jnp.float32)
    residual = inputs + residual_branch
    norm_two_full, normed_two, inverse_two = layer_norm(residual, gain_two, bias_two)
    second_norm = norm_two_full.astype(jnp.bfloat16)
    router_scores = jnp.dot(second_norm, w_router, preferred_element_type=jnp.float32)
    router_probs = jax.nn.softmax(router_scores, -1)
    route_ids = routes[0, :, 0]
    chosen = route_ids[:, None] == jnp.arange(sources)[None, :]
    gate_prob = jnp.sum(jnp.where(chosen, router_probs, 0.0), -1)
    ranking = jnp.cumsum(chosen.astype(jnp.int32), 0) - 1
    slot_ids = route_ids * capacity + jnp.sum(jnp.where(chosen, ranking, 0), -1)
    placing = (jnp.arange(sources * capacity)[:, None] == slot_ids[None, :]).astype(jnp.bfloat16)
    outgoing = jnp.dot(placing, second_norm, preferred_element_type=jnp.float32).astype(
        jnp.bfloat16
    )
    outgoing = outgoing.reshape(sources, capacity, width)
    valid_rows = (query_pos < lengths[0]).astype(jnp.float32)
    taught = teacher[0].astype(jnp.float32)
    gate_high = gate_prob.astype(jnp.bfloat16)
    gate_low = (gate_prob - gate_high.astype(jnp.float32)).astype(jnp.bfloat16)
    extras = jnp.stack([gate_high, gate_low, valid_rows.astype(jnp.bfloat16)], 1)
    extras = jnp.pad(extras, ((0, 0), (0, 125)))
    parting = jnp.concatenate([(residual - taught).astype(jnp.bfloat16), extras], 1)
    parting = jnp.dot(placing, parting, preferred_element_type=jnp.float32).astype(jnp.bfloat16)
    returned, d_back, grad_in_out, grad_down_out = experts(
        outgoing,
        parting.reshape(sources, capacity, width + 128),
        w_in[0],
        in_other,
        w_down[0],
        down_other,
    )
    expert_out = transposed_times(placing, returned.reshape(-1, width))
    mixed_out = (residual + gate_prob[:, None] * expert_out).astype(jnp.bfloat16)
    errors = mixed_out.astype(jnp.float32) - taught
    squares = jnp.sum(valid_rows[:, None] * errors * errors)
    count = jnp.sum(valid_rows)
    d_mixed = valid_rows[:, None] * errors
    d_gate = jnp.sum(d_mixed * expert_out, -1)
    d_norm_expert = transposed_times(placing, d_back.reshape(-1, width))
    d_logits = (d_gate * gate_prob)[:, None] * (chosen.astype(jnp.float32) - router_probs)
    router_full = w_router.astype(jnp.float32)
    grad_router = jnp.dot(
        second_norm.astype(jnp.float32).T, d_logits, precision=lax.Precision.HIGHEST
    )
    d_norm_two = d_norm_expert + jnp.dot(d_logits, router_full.T, precision=lax.Precision.HIGHEST)
    d_resid_part, grad_gain_two, grad_bias_two = norm_back(
        d_norm_two, normed_two, inverse_two, gain_two
    )
    d_resid = d_mixed + d_resid_part
    d_branch = d_resid.astype(jnp.bfloat16)
    grad_out = transposed_times(attention_result, d_branch)
    d_attended = (
        times_transposed(d_branch, w_out)
        .astype(jnp.bfloat16)
        .reshape(group, HEADS, head_dim)
    )
    probs_again = jnp.exp(score_block() - log_total)
    d_probs = jnp.einsum("qhd,khd->hqk", d_attended, value_rows, preferred_element_type=jnp.float32)
    delta_sum = jnp.sum(probs_again * d_probs, -1, keepdims=True)
    d_scores = (probs_again * (d_probs - delta_sum)).astype(jnp.bfloat16)
    d_queries = (
        jnp.einsum("hqk,khd->qhd", d_scores, key_rows, preferred_element_type=jnp.float32) * 0.125
    )
    d_keys = (
        jnp.einsum("hqk,qhd->khd", d_scores, queries, preferred_element_type=jnp.float32) * 0.125
    )
    d_values = jnp.einsum("hqk,qhd->khd", probs_low, d_attended, preferred_element_type=jnp.float32)
    d_kv_whole = jnp.concatenate(
        [d_keys.reshape(seq_len, width), d_values.reshape(seq_len, width)], 1
    )
    d_kv = lax.psum_scatter(d_kv_whole.astype(jnp.bfloat16), "dp", scatter_dimension=0, tiled=True)
    d_qkv = jnp.concatenate([d_queries.reshape(group, width).astype(jnp.bfloat16), d_kv], 1)
    grad_qkv = transposed_times(first_norm, d_qkv)
    d_norm_one = times_transposed(d_qkv, w_qkv)
    d_input_part, grad_gain_one, grad_bias_one = norm_back(
        d_norm_one, normed_one, inverse_one, gain_one
    )
    grad_tokens = d_resid + d_input_part
    vector_grads = jnp.stack(
        [grad_gain_one, grad_bias_one, grad_gain_two, grad_bias_two]
    ).reshape(4, 128, 8)
    vector_grads = jnp.pad(vector_grads.transpose(1, 0, 2), ((0, 0), (0, 4), (0, 56)))
    totals = jnp.zeros((8, 128), jnp.float32).at[0, 0].set(squares).at[1, 0].set(count)
    side = jnp.concatenate(
        [grad_router.reshape(128, 8, sources), vector_grads, jnp.broadcast_to(totals[None], (128, 8, 128))], 2
    )
    grad_qkv, grad_out, side = reduce_layer(grad_qkv, grad_out, side)
    grad_router = side[:, :sources]
    vector_grads = side[:4, sources : sources + 8]
    loss_value = side[0, 128] / (side[1, 128] * width)
    return (
        mixed_out[None],
        loss_value,
        grad_tokens[None],
        vector_grads[0],
        vector_grads[1],
        grad_qkv,
        grad_out,
        vector_grads[2],
        vector_grads[3],
        grad_router,
        grad_in_out[None],
        grad_down_out[None],
    )


def solution(mesh):
    placed = (
        P("expert", "dp", None),
        P("expert", "dp", None),
        P("expert"),
        P("expert", "dp", None),
        P(("dp", "expert")),
        P(("dp", "expert")),
        P(("dp", "expert"), None),
        P(("dp", "expert"), None),
        P(("dp", "expert")),
        P(("dp", "expert")),
        P(("dp", "expert"), None),
        P("expert", "dp", None),
        P("expert", "dp", None),
    )
    return jax.shard_map(
        per_device,
        mesh=mesh,
        in_specs=placed,
        out_specs=(
            P("expert", "dp", None),
            P(),
            P("expert", "dp", None),
            P(("dp", "expert")),
            P(("dp", "expert")),
            P(("dp", "expert"), None),
            P(("dp", "expert"), None),
            P(("dp", "expert")),
            P(("dp", "expert")),
            P(("dp", "expert"), None),
            P("expert", "dp", None),
            P("expert", "dp", None),
        ),
        check_vma=False,
    )
```

```python
import jax
import jax.numpy as jnp
from jax import lax
from jax.experimental import pallas as pl
from jax.experimental.pallas import tpu as pltpu
from jax.sharding import PartitionSpec as P

MESH = pl.DeviceIdType.MESH
SIDE = 4
FULL = slice(None)

AG_COLS = 4224
AG_PIECES = ((0, 768, 1408), (1408, 2176, 2816), (2816, 3584, 4224))


def place(region, c0, c1):
    return tuple(region) + (FULL, pl.ds(c0, c1 - c0))


def coords():
    e = lax.axis_index("expert")
    return [e // 16, (e // 4) % 4, e % 4]


def shifted(pos, axis, by):
    out = list(pos)
    out[axis] = (pos[axis] + by) % SIDE
    return out


def chip(pos):
    return {"expert": pos[0] * 16 + pos[1] * 4 + pos[2]}


def neighbours(pos):
    return [chip(shifted(pos, axis, by)) for axis in range(3) for by in (1, 3)]


def greet(pos, core):
    barrier = pltpu.get_barrier_semaphore()
    for other in neighbours(pos) + [{"dp": 1 - core}]:
        pl.semaphore_signal(barrier, inc=1, device_id=other, device_id_type=MESH)
    pl.semaphore_wait(barrier, 7)


class Sender:
    def __init__(self, send_sems, recv_sems):
        self.send_sems, self.recv_sems, self.count, self.sent = send_sems, recv_sems, 0, []

    def __call__(self, src, dst, device):
        copy = pltpu.make_async_remote_copy(
            src_ref=src,
            dst_ref=dst,
            send_sem=self.send_sems.at[self.count],
            recv_sem=self.recv_sems.at[self.count],
            device_id=device,
            device_id_type=MESH,
        )
        copy.start()
        self.count += 1
        self.sent.append(copy)
        return copy


def gather_kernel(shard, w_in, w_down, whole, in_other, down_other, own_sem, send_sems, recv_sems):
    pos = coords()
    core = lax.axis_index("dp")
    partner = {"dp": 1 - core}
    own = pltpu.make_async_copy(shard, whole.at[(core, *pos)], own_sem)
    own.start()
    greet(pos, core)
    send = Sender(send_sems, recv_sems)
    across = [send(w_in, in_other, partner), send(w_down, down_other, partner)]
    own.wait()

    def share(region, c0, c1, device):
        spot = whole.at[place([core] + region, c0, c1)]
        return send(spot, spot, device)

    for stage in range(3):
        first = []
        for piece, (c0, mid, c1) in enumerate(AG_PIECES):
            order = [(piece + step) % 3 for step in range(3)]
            axis = order[stage]
            done = order[:stage]
            region = [FULL if a in done else pos[a] for a in range(3)]
            up, down = chip(shifted(pos, axis, 1)), chip(shifted(pos, axis, 3))
            first.append((axis, region, up, down, share(region, c0, c1, up), share(region, c0, c1, down)))
        if stage == 2:
            for (c0, mid, c1), (axis, region, up, down, _, _) in zip(AG_PIECES, first):
                across.append(share(region, c0, c1, partner))
        second = []
        for (c0, mid, c1), (axis, region, up, down, to_up, to_down) in zip(AG_PIECES, first):
            below, above = list(region), list(region)
            below[axis], above[axis] = (pos[axis] + 3) % SIDE, (pos[axis] + 1) % SIDE
            to_up.wait_recv()
            on_up = share(below, c0, mid, up)
            to_down.wait_recv()
            on_down = share(above, mid, c1, down)
            second.append((on_up, on_down))
            if stage == 2:
                across.append(share(below, c0, c1, partner))
                across.append(share(above, c0, c1, partner))
        for (c0, mid, c1), (axis, region, up, down, _, _), (on_up, on_down) in zip(AG_PIECES, first, second):
            on_up.wait_recv()
            on_down.wait_recv()
            if stage == 2:
                far = list(region)
                far[axis] = (pos[axis] + 2) % SIDE
                across.append(share(far, c0, c1, partner))
    for copy in across:
        copy.wait_recv()
    for copy in send.sent:
        copy.wait_send()


def gather_layer(shard, w_in, w_down):
    copies = 3 * 3 * 4 + 3 * 4 + 2
    anywhere = pl.BlockSpec(memory_space=pl.ANY)
    whole, in_other, down_other = pl.pallas_call(
        gather_kernel,
        out_shape=(
            jax.ShapeDtypeStruct((2, SIDE, SIDE, SIDE, 8, AG_COLS), jnp.bfloat16),
            jax.ShapeDtypeStruct(w_in.shape, w_in.dtype),
            jax.ShapeDtypeStruct(w_down.shape, w_down.dtype),
        ),
        in_specs=[anywhere] * 3,
        out_specs=(anywhere,) * 3,
        scratch_shapes=[
            pltpu.SemaphoreType.DMA,
            pltpu.SemaphoreType.DMA((copies,)),
            pltpu.SemaphoreType.DMA((copies,)),
        ],
        compiler_params=pltpu.CompilerParams(collective_id=0, has_side_effects=True),
        name="gather_layer",
    )(shard, w_in, w_down)
    return whole.reshape(1024, AG_COLS), in_other, down_other


RS_COLS = (3072, 1024, 256)
RS_KINDS = (jnp.bfloat16, jnp.bfloat16, jnp.float32)
RS_HALVES = (
    (((0, 0, 768),), ((0, 768, 1536),)),
    (((0, 1536, 2304),), ((0, 2304, 3072),)),
    (((1, 0, 768),), ((1, 768, 1024), (2, 0, 256))),
)
RS_PIECES = tuple(h0 + h1 for h0, h1 in RS_HALVES)


def reduce_all(pos, core, source, outs, rest):
    refs, (send_sems, recv_sems) = list(rest[:-2]), rest[-2:]
    take = iter(refs)
    partner = {"dp": 1 - core}
    send = Sender(send_sems, recv_sems)
    landed = (next(take), next(take), next(take))

    opening = []
    for piece in range(3):
        copies = []
        for kind, c0, c1 in RS_PIECES[piece]:
            copies.append(
                send(
                    source[kind].at[place([1 - core, FULL, FULL, FULL], c0, c1)],
                    landed[kind].at[place([FULL, FULL, FULL], c0, c1)],
                    partner,
                )
            )
        opening.append(copies)

    def whole_sum(kind, index, c0, c1):
        spot = index + (FULL, pl.ds(c0, c1 - c0))
        mine = source[kind][(core,) + spot].astype(jnp.float32)
        return mine + landed[kind][spot].astype(jnp.float32)

    sums = []
    for piece in range(3):
        sums.append(whole_sum)

    for stage in range(3):
        plans = []
        for piece in range(3):
            order = [(piece + step) % 3 for step in range(3)]
            axis = order[stage]
            free = sorted(order[stage + 1:])
            fixed = order[:stage]
            bufs = {}
            for half in range(2):
                for n, (kind, c0, c1) in enumerate(RS_HALVES[piece][half]):
                    for what in ("sendA", "recvA"):
                        bufs[what, half, n] = next(take)
            for way in range(2):
                for n, (kind, c0, c1) in enumerate(RS_PIECES[piece]):
                    for what in ("sendB", "recvB"):
                        bufs[what, way, n] = next(take)
            up, down = chip(shifted(pos, axis, 1)), chip(shifted(pos, axis, 3))
            plans.append((axis, free, fixed, bufs, (up, down)))

        def each(free, body):
            total = SIDE ** len(free)

            @pl.loop(0, total)
            def _(i):
                if len(free) == 2:
                    body((i // SIDE, i % SIDE))
                elif len(free) == 1:
                    body((i,))
                else:
                    body(())

        def index_of(axis, free, fixed, at, spots):
            index = [None] * 3
            for a in fixed:
                index[a] = pos[a]
            index[axis] = at
            for a, s in zip(free, spots):
                index[a] = s
            return tuple(index)

        firsts = []
        for piece, (axis, free, fixed, bufs, ways) in enumerate(plans):
            if stage == 0:
                for copy in opening[piece]:
                    copy.wait_recv()
            far = (pos[axis] + 2) % SIDE
            copies = []
            for half in range(2):
                def fill(spots, half=half, axis=axis, free=free, fixed=fixed, bufs=bufs, piece=piece, far=far):
                    for n, (kind, c0, c1) in enumerate(RS_HALVES[piece][half]):
                        block = sums[piece](kind, index_of(axis, free, fixed, far, spots), c0, c1)
                        buf = bufs["sendA", half, n]
                        buf[spots + (FULL, FULL)] = block.astype(buf.dtype)

                each(free, fill)
                for n in range(len(RS_HALVES[piece][half])):
                    copies.append(send(bufs["sendA", half, n], bufs["recvA", half, n], ways[half]))
            firsts.append(copies)
        seconds = []
        for piece, (axis, free, fixed, bufs, ways) in enumerate(plans):
            for copy in firsts[piece]:
                copy.wait_recv()
            copies = []
            for way in range(2):
                at = (pos[axis] + (1, 3)[way]) % SIDE

                def fill(spots, way=way, axis=axis, free=free, fixed=fixed, bufs=bufs, piece=piece, at=at):
                    index = index_of(axis, free, fixed, at, spots)
                    n = 0
                    for half in range(2):
                        for m, (kind, c0, c1) in enumerate(RS_HALVES[piece][half]):
                            block = sums[piece](kind, index, c0, c1)
                            if half == way:
                                block = block + bufs["recvA", half, m][spots + (FULL, FULL)].astype(jnp.float32)
                            buf = bufs["sendB", way, n]
                            buf[spots + (FULL, FULL)] = block.astype(buf.dtype)
                            n += 1

                each(free, fill)
                for n in range(len(RS_PIECES[piece])):
                    copies.append(send(bufs["sendB", way, n], bufs["recvB", way, n], ways[way]))
            seconds.append(copies)
        for piece, (axis, free, fixed, bufs, ways) in enumerate(plans):
            for copy in seconds[piece]:
                copy.wait_recv()
            if stage < 2:
                total = {n: next(take) for n in range(len(RS_PIECES[piece]))}
            else:
                total = None

            def fill(spots, axis=axis, free=free, fixed=fixed, bufs=bufs, piece=piece, total=total):
                index = index_of(axis, free, fixed, pos[axis], spots)
                for n, (kind, c0, c1) in enumerate(RS_PIECES[piece]):
                    block = sums[piece](kind, index, c0, c1)
                    for way in range(2):
                        block = block + bufs["recvB", way, n][spots + (FULL, FULL)].astype(jnp.float32)
                    if total is None:
                        outs[kind][:, c0:c1] = block
                    else:
                        total[n][spots + (FULL, FULL)] = block

            each(free, fill)
            if total is not None:
                def partial(kind, index, c0, c1, total=total, piece=piece, free=free):
                    spots = tuple(index[a] for a in free)
                    for n, (k, s0, s1) in enumerate(RS_PIECES[piece]):
                        if k == kind and s0 <= c0 and c1 <= s1:
                            return total[n][spots + (FULL, pl.ds(c0 - s0, c1 - c0))]

                sums[piece] = partial
    for copy in send.sent:
        copy.wait_send()


def reduce_scratch():
    scratch = [pltpu.VMEM((SIDE, SIDE, SIDE, 8, c), k) for c, k in zip(RS_COLS, RS_KINDS)]
    copies = sum(len(p) for p in RS_PIECES)
    for stage in range(3):
        lead = (SIDE,) * (2 - stage)
        for piece in range(3):
            for half in range(2):
                for kind, c0, c1 in RS_HALVES[piece][half]:
                    scratch += [pltpu.VMEM(lead + (8, c1 - c0), RS_KINDS[kind])] * 2
                    copies += 1
            for way in range(2):
                for kind, c0, c1 in RS_PIECES[piece]:
                    scratch += [pltpu.VMEM(lead + (8, c1 - c0), RS_KINDS[kind])] * 2
                    copies += 1
        if stage < 2:
            for piece in range(3):
                for kind, c0, c1 in RS_PIECES[piece]:
                    scratch += [pltpu.VMEM(lead + (8, c1 - c0), jnp.float32)]
    return scratch, copies


ROWS = 512
WIDTH = 1024
HIDDEN = 4096
HALF_IN = WIDTH // 2
HALF_FF = HIDDEN // 2
EXTRA = 128
TILE = 512
N_TILES = HIDDEN // TILE
HALF_TILES = N_TILES // 2
CURVE = 0.7978845608028654


def dot_nt(a, b):
    return lax.dot_general(a, b, (((1,), (1,)), ((), ())), preferred_element_type=jnp.float32)


def dot_nn(a, b):
    return lax.dot_general(a, b, (((1,), (0,)), ((), ())), preferred_element_type=jnp.float32)


def dot_tn(a, b):
    return lax.dot_general(a, b, (((0,), (0,)), ((), ())), preferred_element_type=jnp.float32)


def to_chips(pos, me, source, target, send_sem, recv_sem):
    @pl.loop(0, 64)
    def _(n):
        there = [(pos[0] + 2 + n // 16) % 4, (pos[1] + 2 + (n // 4) % 4) % 4, (pos[2] + 2 + n % 4) % 4]
        d = there[0] * 16 + there[1] * 4 + there[2]

        @pl.when(n != 42)
        def _():
            pltpu.make_async_remote_copy(
                src_ref=source.at[d],
                dst_ref=target.at[me],
                send_sem=send_sem,
                recv_sem=recv_sem,
                device_id={"expert": d},
                device_id_type=MESH,
            ).start()


def all_but_one(ref, sem):
    pltpu.make_async_copy(ref.at[pl.ds(0, 63)], ref.at[pl.ds(0, 63)], sem).wait()


def expert_kernel(
    x, r, w1_own, w1_other, w2_own, w2_other,
    y_back, d_back, g1, g2,
    w1, w2, x_in, r_in, xb, xt, act, slope, d_pre, acc, d_exp, out_rows,
    sent1, sent2, got1, got2, stage,
    w_sems, x_sems, r_sems, y_sems, d_sems, own_sems, pass_s, pass_r, out_sems,
):
    pos = coords()
    me = lax.axis_index("expert")
    core = lax.axis_index("dp")
    loads = [
        pltpu.make_async_copy(w1_own, w1.at[core], w_sems.at[0]),
        pltpu.make_async_copy(w1_other, w1.at[1 - core], w_sems.at[1]),
        pltpu.make_async_copy(w2_own, w2.at[core], w_sems.at[2]),
        pltpu.make_async_copy(w2_other, w2.at[1 - core], w_sems.at[3]),
    ]
    barrier = pltpu.get_barrier_semaphore()

    @pl.loop(1, 64)
    def _(n):
        pl.semaphore_signal(barrier, inc=1, device_id={"expert": (me + n) % 64}, device_id_type=MESH)

    pl.semaphore_signal(barrier, inc=1, device_id={"dp": 1 - core}, device_id_type=MESH)
    own_x = pltpu.make_async_copy(x.at[me], x_in.at[me], own_sems.at[0])
    own_r = pltpu.make_async_copy(r.at[me], r_in.at[me], own_sems.at[1])
    own_x.start()
    own_r.start()
    for load in loads:
        load.start()
    pl.semaphore_wait(barrier, 64)
    to_chips(pos, me, x, x_in, x_sems.at[0], x_sems.at[1])
    to_chips(pos, me, r, r_in, r_sems.at[0], r_sems.at[1])
    own_x.wait()
    all_but_one(x_in, x_sems.at[1])
    for load in loads:
        load.wait()

    @pl.loop(0, 8)
    def _(i):
        rows = x_in[pl.ds(i * 8, 8)].astype(jnp.float32).reshape(64, WIDTH)
        xb[pl.ds(pl.multiple_of(i * 64, 64), 64), :] = rows.astype(jnp.bfloat16)

    acc[...] = jnp.zeros_like(acc)

    @pl.loop(0, N_TILES)
    def _(c):
        cols = pl.ds(pl.multiple_of(c * TILE, TILE), TILE)
        pre = dot_nn(xb[:, :HALF_IN], w1[0, :, cols]) + dot_nn(xb[:, HALF_IN:], w1[1, :, cols])
        square = pre * pre
        t = jnp.tanh(CURVE * pre * (1.0 + 0.044715 * square))
        low = (0.5 * pre * (1.0 + t)).astype(jnp.bfloat16)
        act[:, cols] = low
        slope[:, cols] = 0.5 * (1.0 + t) + (0.5 * CURVE) * pre * (1.0 - t * t) * (1.0 + (3 * 0.044715) * square)
        half = c // HALF_TILES
        ff = pl.ds(pl.multiple_of((c % HALF_TILES) * TILE, TILE), TILE)
        acc[...] += dot_nn(low, w2[half, ff, :])

    own_r.wait()
    all_but_one(r_in, r_sems.at[1])

    @pl.loop(0, 8)
    def _(i):
        rows = pl.ds(pl.multiple_of(i * 64, 64), 64)
        low = acc[rows, :].astype(jnp.bfloat16)
        out = low.astype(jnp.float32)
        out_rows[pl.ds(i * 8, 8)] = out.reshape(8, 8, WIDTH).astype(jnp.bfloat16)
        parted = r_in[pl.ds(i * 8, 8)].astype(jnp.float32).reshape(64, WIDTH + EXTRA)
        gate = parted[:, WIDTH : WIDTH + 1] + parted[:, WIDTH + 1 : WIDTH + 2]
        valid = parted[:, WIDTH + 2 : WIDTH + 3]
        d_exp[rows, :] = (gate * valid * (parted[:, :WIDTH] + gate * out)).astype(jnp.bfloat16)

    own_y = pltpu.make_async_copy(out_rows.at[me], y_back.at[me], own_sems.at[2])
    own_y.start()
    to_chips(pos, me, out_rows, y_back, y_sems.at[0], y_sems.at[1])
    acc[...] = jnp.zeros_like(acc)

    @pl.loop(0, N_TILES)
    def _(c):
        cols = pl.ds(pl.multiple_of(c * TILE, TILE), TILE)
        half = c // HALF_TILES
        ff = pl.ds(pl.multiple_of((c % HALF_TILES) * TILE, TILE), TILE)
        d_act = dot_nt(d_exp[...], w2[half, ff, :])
        low = (slope[:, cols] * d_act).astype(jnp.bfloat16)
        d_pre[:, cols] = low
        acc[:, :HALF_IN] += dot_nt(low, w1[0, :, cols])
        acc[:, HALF_IN:] += dot_nt(low, w1[1, :, cols])

    own_y.wait()
    all_but_one(out_rows, y_sems.at[0])

    @pl.loop(0, 8)
    def _(i):
        rows = pl.ds(pl.multiple_of(i * 64, 64), 64)
        out_rows[pl.ds(i * 8, 8)] = acc[rows, :].reshape(8, 8, WIDTH).astype(jnp.bfloat16)

    own_d = pltpu.make_async_copy(out_rows.at[me], d_back.at[me], own_sems.at[3])
    own_d.start()
    to_chips(pos, me, out_rows, d_back, d_sems.at[0], d_sems.at[1])

    xt[...] = xb[...].astype(jnp.float32).T.astype(jnp.bfloat16)

    def passed(buf, got, c, base):
        return pltpu.make_async_remote_copy(
            src_ref=buf.at[c],
            dst_ref=got.at[c],
            send_sem=pass_s.at[base + c],
            recv_sem=pass_r.at[base + c],
            device_id={"dp": 1 - core},
            device_id_type=MESH,
        )

    def in_rows(half):
        return xt[pl.ds(pl.multiple_of(half * HALF_IN, HALF_IN), HALF_IN), :]

    @pl.loop(0, N_TILES)
    def _(c):
        cols = pl.ds(pl.multiple_of(c * TILE, TILE), TILE)
        sent1[c] = dot_nn(in_rows(1 - core), d_pre[:, cols]).astype(jnp.bfloat16)
        passed(sent1, got1, c, 0).start()

    @pl.loop(0, HALF_TILES)
    def _(c):
        cols = pl.ds(pl.multiple_of((1 - core) * HALF_FF + c * TILE, TILE), TILE)
        sent2[c] = dot_tn(act[:, cols], d_exp[...]).astype(jnp.bfloat16)
        passed(sent2, got2, c, N_TILES).start()

    def out1(c, slot):
        cols = pl.ds(pl.multiple_of(c * TILE, TILE), TILE)
        return pltpu.make_async_copy(stage.at[slot, :, pl.ds(0, TILE)], g1.at[:, cols], out_sems.at[slot])

    def out2(c, slot):
        rows = pl.ds(pl.multiple_of(c * TILE, TILE), TILE)
        return pltpu.make_async_copy(stage.at[slot], g2.at[rows, :], out_sems.at[slot])

    @pl.loop(0, N_TILES)
    def _(c):
        slot = c % 2
        cols = pl.ds(pl.multiple_of(c * TILE, TILE), TILE)

        @pl.when(c >= 2)
        def _():
            out1(c - 2, slot).wait()

        passed(sent1, got1, c, 0).wait_recv()
        stage[slot, :, pl.ds(0, TILE)] = dot_nn(in_rows(core), d_pre[:, cols]) + got1[c].astype(jnp.float32)
        out1(c, slot).start()

    out1(N_TILES - 2, 0).wait()
    out1(N_TILES - 1, 1).wait()

    @pl.loop(0, HALF_TILES)
    def _(c):
        slot = c % 2
        cols = pl.ds(pl.multiple_of(core * HALF_FF + c * TILE, TILE), TILE)

        @pl.when(c >= 2)
        def _():
            out2(c - 2, slot).wait()

        passed(sent2, got2, c, N_TILES).wait_recv()
        stage[slot] = dot_tn(act[:, cols], d_exp[...]) + got2[c].astype(jnp.float32)
        out2(c, slot).start()

    out2(HALF_TILES - 2, 0).wait()
    out2(HALF_TILES - 1, 1).wait()

    @pl.loop(0, N_TILES)
    def _(c):
        passed(sent1, got1, c, 0).wait_send()

    @pl.loop(0, HALF_TILES)
    def _(c):
        passed(sent2, got2, c, N_TILES).wait_send()

    own_d.wait()
    all_but_one(x_in, x_sems.at[0])
    all_but_one(r_in, r_sems.at[0])
    all_but_one(out_rows, d_sems.at[0])
    all_but_one(out_rows, y_sems.at[1])
    all_but_one(out_rows, d_sems.at[1])


def experts(x, r, w1_own, w1_other, w2_own, w2_other):
    low, wide = jnp.bfloat16, jnp.float32
    anywhere = pl.BlockSpec(memory_space=pl.ANY)
    return pl.pallas_call(
        expert_kernel,
        out_shape=(
            jax.ShapeDtypeStruct((64, 8, WIDTH), low),
            jax.ShapeDtypeStruct((64, 8, WIDTH), low),
            jax.ShapeDtypeStruct((HALF_IN, HIDDEN), wide),
            jax.ShapeDtypeStruct((HALF_FF, WIDTH), wide),
        ),
        in_specs=[anywhere] * 6,
        out_specs=(anywhere,) * 4,
        scratch_shapes=[
            pltpu.VMEM((2, HALF_IN, HIDDEN), low),
            pltpu.VMEM((2, HALF_FF, WIDTH), low),
            pltpu.VMEM((64, 8, WIDTH), low),
            pltpu.VMEM((64, 8, WIDTH + EXTRA), low),
            pltpu.VMEM((ROWS, WIDTH), low),
            pltpu.VMEM((WIDTH, ROWS), low),
            pltpu.VMEM((ROWS, HIDDEN), low),
            pltpu.VMEM((ROWS, HIDDEN), wide),
            pltpu.VMEM((ROWS, HIDDEN), low),
            pltpu.VMEM((ROWS, WIDTH), wide),
            pltpu.VMEM((ROWS, WIDTH), low),
            pltpu.VMEM((64, 8, WIDTH), low),
            pltpu.VMEM((N_TILES, HALF_IN, TILE), low),
            pltpu.VMEM((HALF_TILES, TILE, WIDTH), low),
            pltpu.VMEM((N_TILES, HALF_IN, TILE), low),
            pltpu.VMEM((HALF_TILES, TILE, WIDTH), low),
            pltpu.VMEM((2, HALF_IN, WIDTH), wide),
            pltpu.SemaphoreType.DMA((4,)),
            pltpu.SemaphoreType.DMA((2,)),
            pltpu.SemaphoreType.DMA((2,)),
            pltpu.SemaphoreType.DMA((2,)),
            pltpu.SemaphoreType.DMA((2,)),
            pltpu.SemaphoreType.DMA((4,)),
            pltpu.SemaphoreType.DMA((N_TILES + HALF_TILES,)),
            pltpu.SemaphoreType.DMA((N_TILES + HALF_TILES,)),
            pltpu.SemaphoreType.DMA((2,)),
        ],
        compiler_params=pltpu.CompilerParams(
            collective_id=2, has_side_effects=True, vmem_limit_bytes=63 * 1024 * 1024
        ),
        name="experts",
    )(x, r, w1_own, w1_other, w2_own, w2_other)


GROUP = 256
HEADS = 16
PAIRS = HEADS // 2
SLOTS = 512
BLOCK = 32
EPS = 1e-05
MASKED = -1e30


def lanes(start, size):
    return pl.ds(pl.multiple_of(start, 128), size)


def row_blocks(body, size=BLOCK):
    @pl.loop(0, GROUP // size)
    def _(i):
        body(pl.ds(pl.multiple_of(i * size, size), size), i * size)


def normed(v):
    centred = v - jnp.mean(v, -1, keepdims=True)
    inverse = lax.rsqrt(jnp.mean(centred * centred, -1, keepdims=True) + EPS)
    return centred * inverse, inverse


def lane_ids(rows, columns):
    return lax.broadcasted_iota(jnp.int32, (rows, columns), 1)


def row_ids(rows, columns):
    return lax.broadcasted_iota(jnp.int32, (rows, columns), 0)


def allowed_keys(core, length):
    query, key = row_ids(GROUP, GROUP), lane_ids(GROUP, GROUP)
    own = (key <= query) & (key + core * GROUP < length)
    other = (key < length) & (core == 1)
    return own, other


def head_scores(q, k_own, k_other, own, other):
    s_own = jnp.where(own, dot_nt(q, k_own) * 0.125, MASKED)
    s_other = jnp.where(other, dot_nt(q, k_other) * 0.125, MASKED)
    return s_own, s_other


def forward_kernel(
    tokens, teacher, routes, lengths, layer,
    x_out, parting_out, qkv_out, kv_other_out, attended_out, norm1_out, norm2_out, residual_out,
    lse_out, probs_out, placing_out, vectors_out,
    weights, norm1, qkv, kv_other, attended, norm2, residual, lse, probs, placing, vectors, parted, packed_x, packed_r,
    load_sems, out_sems, kv_sems,
):
    core = lax.axis_index("dp")
    length = lengths[0]
    spans = ((4096, 128), (1024, 1024), (2048, 1024), (0, 1024), (3072, 1024))
    loads = [
        pltpu.make_async_copy(layer.at[:, pl.ds(c, n)], weights.at[:, pl.ds(c, n)], load_sems.at[i])
        for i, (c, n) in enumerate(spans)
    ]
    for load in loads:
        load.start()
    outs = []

    def save(src, dst):
        copy = pltpu.make_async_copy(src, dst, out_sems.at[len(outs)])
        copy.start()
        outs.append(copy)

    barrier = pltpu.get_barrier_semaphore()
    pl.semaphore_signal(barrier, inc=1, device_id={"dp": 1 - core}, device_id_type=MESH)

    loads[0].wait()
    for g in range(16):
        part = weights[pl.ds(g * 64, 64), pl.ds(4096, 128)].astype(jnp.float32)
        part = jnp.sum(part.reshape(8, 8, 128), 0)
        vectors[:, g * 64 : (g + 1) * 64] = part[:, 64:]
    save(vectors, vectors_out)

    def first_norm(rows, _):
        n, _ = normed(tokens[rows, :].astype(jnp.float32))
        norm1[rows, :] = (n * vectors[0:1, :] + vectors[1:2, :]).astype(jnp.bfloat16)

    row_blocks(first_norm)
    save(norm1, norm1_out)

    def project(block):
        @pl.loop(0, 2)
        def _(i):
            cols = lanes(block * 1024 + i * 512, 512)
            qkv[:, cols] = dot_nn(norm1[...], weights[:, cols]).astype(jnp.bfloat16)

    loads[1].wait()
    project(1)
    loads[2].wait()
    project(2)
    pl.semaphore_wait(barrier, 1)
    passed = pltpu.make_async_remote_copy(
        src_ref=qkv.at[:, pl.ds(1024, 2048)],
        dst_ref=kv_other,
        send_sem=kv_sems.at[0],
        recv_sem=kv_sems.at[1],
        device_id={"dp": 1 - core},
        device_id_type=MESH,
    )
    passed.start()
    loads[3].wait()
    project(0)
    save(qkv, qkv_out)
    passed.wait_recv()
    save(kv_other, kv_other_out)

    own, other = allowed_keys(core, length)
    lse[...] = jnp.zeros_like(lse)

    @pl.loop(0, PAIRS)
    def _(pair):
        q = qkv[:, lanes(pair * 128, 128)]
        k_own, v_own = qkv[:, lanes(1024 + pair * 128, 128)], qkv[:, lanes(2048 + pair * 128, 128)]
        k_other, v_other = kv_other[:, lanes(pair * 128, 128)], kv_other[:, lanes(1024 + pair * 128, 128)]
        left = lane_ids(GROUP, 128) < 64
        results = []
        for h in range(2):
            qh = jnp.where(left == (h == 0), q, jnp.zeros_like(q))
            s_own, s_other = head_scores(qh, k_own, k_other, own, other)
            top = jnp.max(jnp.maximum(s_own, s_other), -1, keepdims=True)
            e_own, e_other = jnp.exp(s_own - top), jnp.exp(s_other - top)
            total = jnp.sum(e_own + e_other, -1, keepdims=True)
            scale = 1.0 / total
            p_own, p_other = (e_own * scale).astype(jnp.bfloat16), (e_other * scale).astype(jnp.bfloat16)
            results.append(dot_nn(p_own, v_own) + dot_nn(p_other, v_other))
            lse[...] = jnp.where(lane_ids(GROUP, 128) == pair * 2 + h, top + jnp.log(total), lse[...])
        attended[:, lanes(pair * 128, 128)] = jnp.where(left, results[0], results[1]).astype(jnp.bfloat16)

    save(attended, attended_out)
    save(lse, lse_out)
    loads[4].wait()

    @pl.loop(0, 2)
    def _(i):
        cols = lanes(i * 512, 512)
        branch = dot_nn(attended[...], weights[:, lanes(3072 + i * 512, 512)])
        residual[:, cols] = tokens[:, cols].astype(jnp.float32) + branch

    save(residual, residual_out)

    def second_norm(rows, _):
        n, _ = normed(residual[rows, :])
        norm2[rows, :] = (n * vectors[2:3, :] + vectors[3:4, :]).astype(jnp.bfloat16)
        parted[rows, :WIDTH] = (residual[rows, :] - teacher[rows, :].astype(jnp.float32)).astype(jnp.bfloat16)

    row_blocks(second_norm)
    save(norm2, norm2_out)
    logits = dot_nn(norm2[...], weights[:, pl.ds(4096, 128)])
    ids = lane_ids(GROUP, 128)
    logits = jnp.where(ids < 64, logits, MASKED)
    e = jnp.exp(logits - jnp.max(logits, -1, keepdims=True))
    share = e / jnp.sum(e, -1, keepdims=True)
    probs[...] = share
    save(probs, probs_out)
    chosen = ids == routes[...]
    gate = jnp.sum(jnp.where(chosen, share, 0.0), -1, keepdims=True)
    low_gate = gate.astype(jnp.bfloat16).astype(jnp.float32)
    valid = (row_ids(GROUP, 128) + core * GROUP < length).astype(jnp.float32)
    extras = jnp.where(ids == 0, low_gate, jnp.where(ids == 1, gate - low_gate, jnp.where(ids == 2, valid, 0.0)))
    parted[:, WIDTH:] = extras.astype(jnp.bfloat16)
    marks = chosen.astype(jnp.float32).astype(jnp.bfloat16)
    before = (lane_ids(GROUP, GROUP) < row_ids(GROUP, GROUP)).astype(jnp.float32).astype(jnp.bfloat16)
    rank = jnp.sum(jnp.where(chosen, dot_nn(before, marks), 0.0), -1, keepdims=True)
    slot = routes[...].astype(jnp.float32) * 8.0 + rank
    placing[...] = (lane_ids(GROUP, SLOTS).astype(jnp.float32) == slot).astype(jnp.float32).astype(jnp.bfloat16)
    save(placing, placing_out)
    for half in range(2):
        spread = placing[:, half * 256 : (half + 1) * 256].astype(jnp.float32).T.astype(jnp.bfloat16)
        sent = dot_nn(spread, norm2[...])
        packed_x[half * 32 : (half + 1) * 32] = sent.reshape(32, 8, WIDTH).astype(jnp.bfloat16)
        sent = dot_nn(spread, parted[...])
        packed_r[half * 32 : (half + 1) * 32] = sent.reshape(32, 8, WIDTH + EXTRA).astype(jnp.bfloat16)
    save(packed_x, x_out)
    save(packed_r, parting_out)
    passed.wait_send()
    for copy in outs:
        copy.wait()


def forward(tokens, teacher, routes, lengths, layer):
    low, wide = jnp.bfloat16, jnp.float32
    anywhere = pl.BlockSpec(memory_space=pl.ANY)
    vmem = pl.BlockSpec(memory_space=pltpu.VMEM)
    saved = [
        ((64, 8, WIDTH), low),
        ((64, 8, WIDTH + EXTRA), low),
        ((GROUP, 3 * WIDTH), low),
        ((GROUP, 2 * WIDTH), low),
        ((GROUP, WIDTH), low),
        ((GROUP, WIDTH), low),
        ((GROUP, WIDTH), low),
        ((GROUP, WIDTH), wide),
        ((GROUP, 128), wide),
        ((GROUP, 128), wide),
        ((GROUP, SLOTS), low),
        ((8, WIDTH), wide),
    ]
    return pl.pallas_call(
        forward_kernel,
        out_shape=tuple(jax.ShapeDtypeStruct(s, t) for s, t in saved),
        in_specs=[vmem, vmem, vmem, pl.BlockSpec(memory_space=pltpu.SMEM), anywhere],
        out_specs=(anywhere,) * len(saved),
        scratch_shapes=[
            pltpu.VMEM((WIDTH, AG_COLS), low),
            pltpu.VMEM((GROUP, WIDTH), low),
            pltpu.VMEM((GROUP, 3 * WIDTH), low),
            pltpu.VMEM((GROUP, 2 * WIDTH), low),
            pltpu.VMEM((GROUP, WIDTH), low),
            pltpu.VMEM((GROUP, WIDTH), low),
            pltpu.VMEM((GROUP, WIDTH), wide),
            pltpu.VMEM((GROUP, 128), wide),
            pltpu.VMEM((GROUP, 128), wide),
            pltpu.VMEM((GROUP, SLOTS), low),
            pltpu.VMEM((8, WIDTH), wide),
            pltpu.VMEM((GROUP, WIDTH + EXTRA), low),
            pltpu.VMEM((64, 8, WIDTH), low),
            pltpu.VMEM((64, 8, WIDTH + EXTRA), low),
            pltpu.SemaphoreType.DMA((5,)),
            pltpu.SemaphoreType.DMA((len(saved),)),
            pltpu.SemaphoreType.DMA((2,)),
        ],
        compiler_params=pltpu.CompilerParams(
            collective_id=3, has_side_effects=True, vmem_limit_bytes=56 * 1024 * 1024
        ),
        name="forward",
    )(tokens, teacher, routes, lengths, layer)


def backward_kernel(
    y_back, d_back, teacher, routes, lengths, layer, qkv, kv_other, attended, norm2, residual, lse, probs,
    placing, vectors, g1, g2,
    mixed_out, d_resid, dq, dkv_own, dkv_other, grad_out, grad_router, norm_grads, g1_out, g2_out,
    w_out, w_router, eo, dn, sums, d_branch, d_attended, attended_t, delta, logit_parts,
    held1, held2, pass_sems, load_sems,
):
    core = lax.axis_index("dp")
    length = lengths[0]
    passing = [
        pltpu.make_async_copy(g1, held1, pass_sems.at[0]),
        pltpu.make_async_copy(g2, held2, pass_sems.at[1]),
    ]
    passed_on = [
        pltpu.make_async_copy(held1, g1_out, pass_sems.at[2]),
        pltpu.make_async_copy(held2, g2_out, pass_sems.at[3]),
    ]
    loads = [
        pltpu.make_async_copy(layer.at[:, pl.ds(3072, 1024)], w_out, load_sems.at[0]),
        pltpu.make_async_copy(layer.at[:, pl.ds(4096, 128)], w_router, load_sems.at[1]),
    ]
    for copy in loads + passing:
        copy.start()
    rows_back = y_back[...].astype(jnp.float32).reshape(SLOTS, WIDTH).astype(jnp.bfloat16)
    eo[...] = dot_nn(placing[...], rows_back)
    rows_back = d_back[...].astype(jnp.float32).reshape(SLOTS, WIDTH).astype(jnp.bfloat16)
    dn[...] = dot_nn(placing[...], rows_back)
    sums[...] = jnp.zeros_like(sums)

    def loss(rows, first):
        ids = lane_ids(BLOCK, 128)
        share = probs[rows, :]
        chosen = ids == routes[rows, :]
        gate = jnp.sum(jnp.where(chosen, share, 0.0), -1, keepdims=True)
        out = eo[rows, :]
        mixed = (residual[rows, :] + gate * out).astype(jnp.bfloat16)
        mixed_out[rows, :] = mixed
        valid = (row_ids(BLOCK, 1) + first + core * GROUP < length).astype(jnp.float32)
        d_mixed = valid * (mixed.astype(jnp.float32) - teacher[rows, :].astype(jnp.float32))
        d_resid[rows, :] = d_mixed
        d_gate = jnp.sum(d_mixed * out, -1, keepdims=True)
        d_logits = d_gate * gate * (chosen.astype(jnp.float32) - share)
        high = d_logits.astype(jnp.bfloat16)
        logit_parts[rows, :128] = high
        logit_parts[rows, 128:] = (d_logits - high.astype(jnp.float32)).astype(jnp.bfloat16)
        square = jnp.sum((d_mixed * d_mixed).reshape(BLOCK // 8, 8, WIDTH), 0)
        sums[0] += square

    row_blocks(loss)
    loads[0].wait()
    loads[1].wait()
    dn[...] += dot_nt(logit_parts[:, :128], w_router[...]) + dot_nt(logit_parts[:, 128:], w_router[...])
    both = dot_tn(norm2[...], logit_parts[...])
    grad_router[...] = both[:, :128] + both[:, 128:]

    def norm_back(rows, _):
        n, inverse = normed(residual[rows, :])
        u = dn[rows, :]
        scaled = u * vectors[2:3, :]
        average = jnp.mean(scaled, -1, keepdims=True)
        project = jnp.mean(scaled * n, -1, keepdims=True)
        d = d_resid[rows, :] + inverse * (scaled - average - n * project)
        d_resid[rows, :] = d
        d_branch[rows, :] = d.astype(jnp.bfloat16)
        sums[1] += jnp.sum((u * n).reshape(BLOCK // 8, 8, WIDTH), 0)
        sums[2] += jnp.sum(u.reshape(BLOCK // 8, 8, WIDTH), 0)

    row_blocks(norm_back)
    valid_all = jnp.clip(length - core * GROUP, 0, GROUP).astype(jnp.float32)
    ids = row_ids(8, WIDTH)
    square = jnp.sum(sums[0])
    norm_grads[...] = jnp.where(
        ids == 2,
        jnp.sum(sums[1], 0, keepdims=True),
        jnp.where(
            ids == 3,
            jnp.sum(sums[2], 0, keepdims=True),
            jnp.where(ids == 4, square, jnp.where(ids == 5, valid_all, 0.0)),
        ),
    )
    attended_t[...] = attended[...].astype(jnp.float32).T.astype(jnp.bfloat16)

    @pl.loop(0, 2)
    def _(i):
        cols = lanes(i * 512, 512)
        grad_out[:, cols] = dot_nn(attended_t[...], d_branch[:, cols]).astype(jnp.bfloat16)
        rows = pl.ds(pl.multiple_of(i * 512, 512), 512)
        d_attended[:, cols] = dot_nt(d_branch[...], w_out[rows, :]).astype(jnp.bfloat16)

    own, other = allowed_keys(core, length)
    for copy, onward in zip(passing, passed_on):
        copy.wait()
        onward.start()

    @pl.loop(0, PAIRS)
    def _(pair):
        q, do = qkv[:, lanes(pair * 128, 128)], d_attended[:, lanes(pair * 128, 128)]
        k_own, v_own = qkv[:, lanes(1024 + pair * 128, 128)], qkv[:, lanes(2048 + pair * 128, 128)]
        k_other, v_other = kv_other[:, lanes(pair * 128, 128)], kv_other[:, lanes(1024 + pair * 128, 128)]
        left = lane_ids(GROUP, 128) < 64
        zero = jnp.zeros_like(q)
        parts = []
        for h in range(2):
            qh = jnp.where(left == (h == 0), q, zero)
            doh = jnp.where(left == (h == 0), do, zero)
            s_own, s_other = head_scores(qh, k_own, k_other, own, other)
            log_total = jnp.sum(jnp.where(lane_ids(GROUP, 128) == pair * 2 + h, lse[...], 0.0), -1, keepdims=True)
            p_own, p_other = jnp.exp(s_own - log_total), jnp.exp(s_other - log_total)
            dp_own, dp_other = dot_nt(doh, v_own), dot_nt(doh, v_other)
            total = jnp.sum(p_own * dp_own + p_other * dp_other, -1, keepdims=True)
            ds_own = (p_own * (dp_own - total)).astype(jnp.bfloat16)
            ds_other = (p_other * (dp_other - total)).astype(jnp.bfloat16)
            p_own, p_other = p_own.astype(jnp.bfloat16), p_other.astype(jnp.bfloat16)
            parts.append((
                dot_nn(ds_own, k_own) + dot_nn(ds_other, k_other),
                dot_tn(ds_own, q),
                dot_tn(ds_other, q),
                dot_tn(p_own, do),
                dot_tn(p_other, do),
            ))
        d_q, d_k, d_k_other, d_v, d_v_other = [jnp.where(left, a, b) for a, b in zip(*parts)]
        dq[:, lanes(pair * 128, 128)] = (d_q * 0.125).astype(jnp.bfloat16)
        dkv_own[:, lanes(pair * 128, 128)] = d_k * 0.125
        dkv_own[:, lanes(1024 + pair * 128, 128)] = d_v
        dkv_other[:, lanes(pair * 128, 128)] = (d_k_other * 0.125).astype(jnp.bfloat16)
        dkv_other[:, lanes(1024 + pair * 128, 128)] = d_v_other.astype(jnp.bfloat16)

    for onward in passed_on:
        onward.wait()


def backward(y_back, d_back, teacher, routes, lengths, layer, qkv, kv_other, attended, norm2, residual, lse, probs,
             placing, vectors, g1, g2):
    low, wide = jnp.bfloat16, jnp.float32
    anywhere = pl.BlockSpec(memory_space=pl.ANY)
    vmem = pl.BlockSpec(memory_space=pltpu.VMEM)
    made = [
        ((GROUP, WIDTH), low),
        ((GROUP, WIDTH), wide),
        ((GROUP, WIDTH), low),
        ((GROUP, 2 * WIDTH), wide),
        ((GROUP, 2 * WIDTH), low),
        ((WIDTH, WIDTH), low),
        ((WIDTH, 128), wide),
        ((8, WIDTH), wide),
        (g1.shape, wide),
        (g2.shape, wide),
    ]
    return pl.pallas_call(
        backward_kernel,
        out_shape=tuple(jax.ShapeDtypeStruct(s, t) for s, t in made),
        in_specs=[vmem, vmem, vmem, vmem, pl.BlockSpec(memory_space=pltpu.SMEM), anywhere] + [vmem] * 9 + [anywhere] * 2,
        out_specs=(vmem,) * 8 + (anywhere,) * 2,
        scratch_shapes=[
            pltpu.VMEM((WIDTH, WIDTH), low),
            pltpu.VMEM((WIDTH, 128), low),
            pltpu.VMEM((GROUP, WIDTH), wide),
            pltpu.VMEM((GROUP, WIDTH), wide),
            pltpu.VMEM((3, 8, WIDTH), wide),
            pltpu.VMEM((GROUP, WIDTH), low),
            pltpu.VMEM((GROUP, WIDTH), low),
            pltpu.VMEM((WIDTH, GROUP), low),
            pltpu.VMEM((GROUP, 128), wide),
            pltpu.VMEM((GROUP, 256), low),
            pltpu.VMEM(g1.shape, wide),
            pltpu.VMEM(g2.shape, wide),
            pltpu.SemaphoreType.DMA((4,)),
            pltpu.SemaphoreType.DMA((2,)),
        ],
        compiler_params=pltpu.CompilerParams(vmem_limit_bytes=56 * 1024 * 1024),
        name="backward",
    )(y_back, d_back, teacher, routes, lengths, layer, qkv, kv_other, attended, norm2, residual, lse, probs,
      placing, vectors, g1, g2)


def finish_kernel(
    tokens, norm1, vectors, d_resid, dq, dkv_own, dkv_other, grad_out, grad_router, norm_grads, layer,
    sum_qkv, sum_out, sum_side, grad_tokens,
    weights, norm1_t, landed_kv, dqkv, acc, sums, grad_qkv, side, load_sem, kv_sems, *rest,
):
    pos = coords()
    core = lax.axis_index("dp")
    load = pltpu.make_async_copy(layer.at[:, pl.ds(0, 3072)], weights, load_sem)
    load.start()
    greet(pos, core)
    passed = pltpu.make_async_remote_copy(
        src_ref=dkv_other,
        dst_ref=landed_kv,
        send_sem=kv_sems.at[0],
        recv_sem=kv_sems.at[1],
        device_id={"dp": 1 - core},
        device_id_type=MESH,
    )
    passed.start()
    norm1_t[...] = norm1[...].astype(jnp.float32).T.astype(jnp.bfloat16)
    acc[...] = jnp.zeros_like(acc)
    dqkv[:, pl.ds(0, WIDTH)] = dq[...]

    def project(first):
        @pl.loop(0, 2)
        def _(i):
            cols = lanes(first + i * 512, 512)
            d = dqkv[:, cols]
            for half in range(2):
                part = dot_nn(norm1_t[half * 512 : (half + 1) * 512, :], d)
                grad_qkv[half, :, :, :, :, cols] = part.reshape(SIDE, SIDE, SIDE, 8, 512).astype(jnp.bfloat16)
            acc[...] += dot_nt(d, weights[:, cols])

    load.wait()
    project(0)
    passed.wait_recv()

    def join(rows, _):
        dqkv[rows, pl.ds(WIDTH, 2 * WIDTH)] = (
            dkv_own[rows, :] + landed_kv[rows, :].astype(jnp.float32)
        ).astype(jnp.bfloat16)

    row_blocks(join)
    project(1024)
    project(2048)
    sums[...] = jnp.zeros_like(sums)

    def norm_back(rows, _):
        n, inverse = normed(tokens[rows, :].astype(jnp.float32))
        u = acc[rows, :]
        scaled = u * vectors[0:1, :]
        average = jnp.mean(scaled, -1, keepdims=True)
        project = jnp.mean(scaled * n, -1, keepdims=True)
        grad_tokens[rows, :] = d_resid[rows, :] + inverse * (scaled - average - n * project)
        sums[0] += jnp.sum((u * n).reshape(BLOCK // 8, 8, WIDTH), 0)
        sums[1] += jnp.sum(u.reshape(BLOCK // 8, 8, WIDTH), 0)

    row_blocks(norm_back)
    ids = row_ids(8, WIDTH)
    vector_grads = jnp.where(
        ids == 0,
        jnp.sum(sums[0], 0, keepdims=True),
        jnp.where(ids == 1, jnp.sum(sums[1], 0, keepdims=True), norm_grads[...]),
    )
    for half in range(2):
        rows = grad_router[half * 512 : (half + 1) * 512, :]
        side[half, :, :, :, :, pl.ds(0, 128)] = rows.reshape(SIDE, SIDE, SIDE, 8, 128)
        for x in range(SIDE):
            block = vector_grads[:, (half * SIDE + x) * 128 : (half * SIDE + x + 1) * 128]
            side[half, x, :, :, :, pl.ds(128, 128)] = jnp.broadcast_to(block[None, None], (SIDE, SIDE, 8, 128))
    reduce_all(pos, core, (grad_qkv, grad_out, side), (sum_qkv, sum_out, sum_side), rest)
    passed.wait_send()


def finish(tokens, norm1, vectors, d_resid, dq, dkv_own, dkv_other, grad_out, grad_router, norm_grads, layer):
    low, wide = jnp.bfloat16, jnp.float32
    anywhere = pl.BlockSpec(memory_space=pl.ANY)
    vmem = pl.BlockSpec(memory_space=pltpu.VMEM)
    lead = (2, SIDE, SIDE, SIDE, 8)
    scratch, copies = reduce_scratch()
    return pl.pallas_call(
        finish_kernel,
        out_shape=tuple(jax.ShapeDtypeStruct((8, c), wide) for c in RS_COLS)
        + (jax.ShapeDtypeStruct((GROUP, WIDTH), wide),),
        in_specs=[vmem] * 10 + [anywhere],
        out_specs=(vmem,) * 4,
        scratch_shapes=[
            pltpu.VMEM((WIDTH, 3 * WIDTH), low),
            pltpu.VMEM((WIDTH, GROUP), low),
            pltpu.VMEM((GROUP, 2 * WIDTH), low),
            pltpu.VMEM((GROUP, 3 * WIDTH), low),
            pltpu.VMEM((GROUP, WIDTH), wide),
            pltpu.VMEM((2, 8, WIDTH), wide),
            pltpu.VMEM(lead + (3 * WIDTH,), low),
            pltpu.VMEM(lead + (256,), wide),
            pltpu.SemaphoreType.DMA,
            pltpu.SemaphoreType.DMA((2,)),
            *scratch,
            pltpu.SemaphoreType.DMA((copies,)),
            pltpu.SemaphoreType.DMA((copies,)),
        ],
        compiler_params=pltpu.CompilerParams(
            collective_id=1, has_side_effects=True, vmem_limit_bytes=60 * 1024 * 1024
        ),
        name="finish",
    )(tokens, norm1, vectors, d_resid, dq, dkv_own, dkv_other, grad_out.reshape(lead + (WIDTH,)), grad_router,
      norm_grads, layer)


def per_device(
    tokens,
    teacher,
    lengths,
    routes,
    ln1_gain,
    ln1_bias,
    query_key_value_weight,
    output_weight,
    ln2_gain,
    ln2_bias,
    router_weight,
    w_in,
    w_down,
):
    device = lax.axis_index("dp") * 64 + lax.axis_index("expert")
    vectors = jnp.tile(jnp.stack([ln1_gain, ln1_bias, ln2_gain, ln2_bias]), (1, 8))
    vectors = jnp.where(jnp.arange(64)[None, :] // 8 == device % 8, vectors, 0)
    vectors = jnp.concatenate([vectors, jnp.zeros_like(vectors)], 0)
    layer, in_other, down_other = gather_layer(
        jnp.concatenate([query_key_value_weight, output_weight, router_weight, vectors], 1),
        w_in[0],
        w_down[0],
    )
    x, parting, qkv, kv_other, attended, norm1, norm2, residual, lse, probs, placing, vectors = forward(
        tokens[0], teacher[0], routes[0], lengths, layer
    )
    y_back, d_back, g1, g2 = experts(x, parting, w_in[0], in_other, w_down[0], down_other)
    mixed, d_resid, dq, dkv_own, dkv_other, grad_out, grad_router, norm_grads, g1, g2 = backward(
        y_back, d_back, teacher[0], routes[0], lengths, layer, qkv, kv_other, attended, norm2, residual, lse, probs,
        placing, vectors, g1, g2,
    )
    grad_qkv, grad_out, side, grad_tokens = finish(
        tokens[0], norm1, vectors, d_resid, dq, dkv_own, dkv_other, grad_out, grad_router, norm_grads, layer
    )
    vector_grads = lax.dynamic_slice(side, (0, 128 + (device % 16) * 8), (4, 8))
    loss_value = side[4, 128] / (side[5, 128] * WIDTH)
    return (
        mixed[None],
        loss_value,
        grad_tokens[None],
        vector_grads[0],
        vector_grads[1],
        grad_qkv,
        grad_out,
        vector_grads[2],
        vector_grads[3],
        side[:, :64],
        g1[None],
        g2[None],
    )


def solution(mesh):
    placed = (
        P("expert", "dp", None),
        P("expert", "dp", None),
        P("expert"),
        P("expert", "dp", None),
        P(("dp", "expert")),
        P(("dp", "expert")),
        P(("dp", "expert"), None),
        P(("dp", "expert"), None),
        P(("dp", "expert")),
        P(("dp", "expert")),
        P(("dp", "expert"), None),
        P("expert", "dp", None),
        P("expert", "dp", None),
    )
    return jax.shard_map(
        per_device,
        mesh=mesh,
        in_specs=placed,
        out_specs=(
            P("expert", "dp", None),
            P(),
            P("expert", "dp", None),
            P(("dp", "expert")),
            P(("dp", "expert")),
            P(("dp", "expert"), None),
            P(("dp", "expert"), None),
            P(("dp", "expert")),
            P(("dp", "expert")),
            P(("dp", "expert"), None),
            P("expert", "dp", None),
            P("expert", "dp", None),
        ),
        check_vma=False,
    )
```

```python
import jax
import jax.numpy as jnp
from jax import lax
from jax.experimental import pallas as pl
from jax.experimental.pallas import tpu as pltpu
from jax.sharding import PartitionSpec as P

MESH = pl.DeviceIdType.MESH
SIDE = 4
FULL = slice(None)

AG_COLS = 4224
AG_PIECES = ((0, 768, 1408), (1408, 2176, 2816), (2816, 3584, 4224))


def coords():
    e = lax.axis_index("expert")
    return [e // 16, (e // 4) % 4, e % 4]


def shifted(pos, axis, by):
    out = list(pos)
    out[axis] = (pos[axis] + by) % SIDE
    return out


def chip(pos):
    return {"expert": pos[0] * 16 + pos[1] * 4 + pos[2]}


def greet(pos, core):
    barrier = pltpu.get_barrier_semaphore()
    for axis in range(3):
        for by in range(1, SIDE):
            pl.semaphore_signal(barrier, inc=1, device_id=chip(shifted(pos, axis, by)), device_id_type=MESH)
    pl.semaphore_signal(barrier, inc=1, device_id={"dp": 1 - core}, device_id_type=MESH)
    pl.semaphore_wait(barrier, 10)


class Sender:
    def __init__(self, send_sems, recv_sems):
        self.send_sems, self.recv_sems, self.count, self.sent = send_sems, recv_sems, 0, []

    def __call__(self, src, dst, device):
        copy = pltpu.make_async_remote_copy(
            src_ref=src,
            dst_ref=dst,
            send_sem=self.send_sems.at[self.count],
            recv_sem=self.recv_sems.at[self.count],
            device_id=device,
            device_id_type=MESH,
        )
        copy.start()
        self.count += 1
        self.sent.append(copy)
        return copy

    def close(self):
        for copy in self.sent:
            copy.wait_send()


def gather_kernel(
    q, o, r, vectors, w_in, w_down, whole, in_other, down_other, shard, own_sem, send_sems, recv_sems
):
    pos = coords()
    core = lax.axis_index("dp")
    partner = {"dp": 1 - core}
    shard[:, :3072] = q[...]
    shard[:, 3072:4096] = o[...]
    shard[:, 4096:] = jnp.concatenate([r[...].astype(jnp.float32), vectors[...]], 1).astype(jnp.bfloat16)
    own = pltpu.make_async_copy(shard, whole.at[(core, *pos)], own_sem)
    own.start()
    greet(pos, core)
    send = Sender(send_sems, recv_sems)

    def share(region, c0, c1, device):
        spot = whole.at[(core, *region, FULL, pl.ds(c0, c1 - c0))]
        return send(spot, spot, device)

    plans = []
    for piece, (c0, mid, c1) in enumerate(AG_PIECES):
        axes = [(piece + step) % 3 for step in range(3)]
        spot = whole.at[(core, *pos, FULL, pl.ds(c0, c1 - c0))]
        first = [send(shard.at[:, pl.ds(c0, c1 - c0)], spot, chip(shifted(pos, axes[0], by))) for by in (1, 3, 2)]
        plans.append((axes, c0, mid, c1, first))
    across = [send(w_in, in_other, partner), send(w_down, down_other, partner)]
    own.wait()

    def line(axes, second, third):
        region = [None] * 3
        region[axes[0]], region[axes[1]], region[axes[2]] = FULL, second, third
        return region

    def at(axis, by):
        return (pos[axis] + by) % SIDE

    seconds, lines = [], [{} for _ in plans]

    def onward(piece, by):
        axes, c0, mid, c1, _ = plans[piece]
        region = line(axes, at(axes[1], by), pos[axes[2]])
        lines[piece][by] = (
            share(region, c0, c1, chip(shifted(pos, axes[2], 1))),
            share(region, c0, c1, chip(shifted(pos, axes[2], 3))),
        )
        across.append(share(region, c0, c1, partner))

    def relay(piece, by):
        axes, c0, mid, c1, _ = plans[piece]
        up, down = lines[piece][by]
        up.wait_recv()
        below = line(axes, at(axes[1], by), at(axes[2], 3))
        on_up = share(below, c0, mid, chip(shifted(pos, axes[2], 1)))
        down.wait_recv()
        above = line(axes, at(axes[1], by), at(axes[2], 1))
        on_down = share(above, mid, c1, chip(shifted(pos, axes[2], 3)))
        across.append(share(below, c0, c1, partner))
        across.append(share(above, c0, c1, partner))
        lines[piece][by] = (on_up, on_down)

    def end(piece, by):
        axes, c0, mid, c1, _ = plans[piece]
        for copy in lines[piece][by]:
            copy.wait_recv()
        across.append(share(line(axes, at(axes[1], by), at(axes[2], 2)), c0, c1, partner))

    for piece, (axes, c0, mid, c1, first) in enumerate(plans):
        for copy in first:
            copy.wait_recv()
        region = line(axes, pos[axes[1]], pos[axes[2]])
        seconds.append([share(region, c0, c1, chip(shifted(pos, axes[1], by))) for by in (1, 3, 2)])
        onward(piece, 0)
    for n, by in enumerate((3, 1)):
        for piece in range(3):
            seconds[piece][n].wait_recv()
            onward(piece, by)
    for piece in range(3):
        relay(piece, 0)
    for piece in range(3):
        seconds[piece][2].wait_recv()
        onward(piece, 2)
    for by in (3, 1, 2):
        for piece in range(3):
            relay(piece, by)
    for by in (0, 3, 1, 2):
        for piece in range(3):
            end(piece, by)
    for copy in across:
        copy.wait_recv()
    send.close()


def gather_layer(q, o, r, vectors, w_in, w_down):
    copies = 3 * (3 + 3 + 4 * 4 + 4 * 4) + 2
    anywhere, vmem = pl.BlockSpec(memory_space=pl.ANY), pl.BlockSpec(memory_space=pltpu.VMEM)
    whole, in_other, down_other = pl.pallas_call(
        gather_kernel,
        out_shape=(
            jax.ShapeDtypeStruct((2, SIDE, SIDE, SIDE, 8, AG_COLS), jnp.bfloat16),
            jax.ShapeDtypeStruct(w_in.shape, w_in.dtype),
            jax.ShapeDtypeStruct(w_down.shape, w_down.dtype),
        ),
        in_specs=[vmem] * 4 + [anywhere] * 2,
        out_specs=(anywhere,) * 3,
        scratch_shapes=[
            pltpu.VMEM((8, AG_COLS), jnp.bfloat16),
            pltpu.SemaphoreType.DMA,
            pltpu.SemaphoreType.DMA((copies,)),
            pltpu.SemaphoreType.DMA((copies,)),
        ],
        compiler_params=pltpu.CompilerParams(collective_id=0, has_side_effects=True),
        name="gather_layer",
    )(q, o, r, vectors, w_in, w_down)
    return whole.reshape(1024, AG_COLS), in_other, down_other


RS_COLS = (3072, 1024, 256)
RS_PIECES = ((0, 0, 768, 1536, 0), (0, 1536, 2304, 3072, 1), (1, 0, 512, 1024, 2))
ORDER = (2, 1, 3, 0)


class Reduction:
    low = jnp.bfloat16
    COPIES = 8 + 8 + 3 + 3

    def __init__(self, piece, pos, send, source, out, bufs):
        _, self.c0, self.mid, self.c1, first = piece
        self.axes = [(first + step) % 3 for step in range(3)]
        self.pos, self.send, self.source, self.out = pos, send, source, out
        (self.total, self.send_2, self.recv_2, self.mine, self.send_3, self.recv_3) = bufs[:6]
        self.take(bufs[6:])

    def take(self, bufs):
        self.send_a, self.recv_a, self.send_b, self.recv_b = bufs

    @classmethod
    def scratch(cls, piece):
        _, c0, mid, c1, _ = piece
        width, low, wide = c1 - c0, cls.low, jnp.float32
        return [
            pltpu.VMEM((SIDE, 8, width), wide),
            pltpu.VMEM((3, SIDE, 8, width), low),
            pltpu.VMEM((3, SIDE, 8, width), low),
            pltpu.VMEM((8, width), wide),
            pltpu.VMEM((3, 8, width), low),
            pltpu.VMEM((3, 8, width), low),
        ] + cls.more(mid - c0, width)

    @classmethod
    def more(cls, half, width):
        return [pltpu.VMEM((2, SIDE, SIDE, 8, half), cls.low)] * 2 + [pltpu.VMEM((2, SIDE, SIDE, 8, width), cls.low)] * 2

    def to(self, step, by):
        return chip(shifted(self.pos, self.axes[step], by))

    def term(self, first, second, third, c0, c1):
        spot = [None] * 3
        spot[self.axes[0]] = (self.pos[self.axes[0]] + first) % SIDE
        spot[self.axes[1]] = (self.pos[self.axes[1]] + second) % SIDE
        spot[self.axes[2]] = third
        return self.source[(*spot, FULL, pl.ds(c0, c1 - c0))]

    def first(self):
        self.firsts = []
        for group in ORDER:
            @pl.loop(0, SIDE)
            def _(s):
                self.send_a[0, group, s] = self.term(2, group, s, self.c0, self.mid).astype(self.low)
                self.send_a[1, group, s] = self.term(2, group, s, self.mid, self.c1).astype(self.low)

            self.firsts.append([
                self.send(self.send_a.at[way, group], self.recv_a.at[way, group], self.to(0, (1, 3)[way]))
                for way in range(2)
            ])

    def second(self):
        self.seconds = []
        half = self.mid - self.c0
        for n, group in enumerate(ORDER):
            for copy in self.firsts[n]:
                copy.wait_recv()

            @pl.loop(0, SIDE)
            def _(s):
                for way, by in enumerate((1, 3)):
                    for part, (c0, c1) in enumerate(((self.c0, self.mid), (self.mid, self.c1))):
                        block = self.term(by, group, s, c0, c1)
                        if part == way:
                            block = block + self.recv_a[way, group, s].astype(jnp.float32)
                        self.send_b[way, group, s, :, pl.ds(part * half, half)] = block.astype(self.low)

            self.seconds.append([
                self.send(self.send_b.at[way, group], self.recv_b.at[way, group], self.to(0, (1, 3)[way]))
                for way in range(2)
            ])

    def arrived(self, n, group, s):
        block = self.term(0, group, s, self.c0, self.c1)
        for way in range(2):
            block = block + self.recv_b[way, group, s].astype(jnp.float32)
        return block

    def third(self):
        self.thirds = []
        for n, group in enumerate(ORDER):
            for copy in self.seconds[n]:
                copy.wait_recv()

            @pl.loop(0, SIDE)
            def _(s):
                block = self.arrived(n, group, s)
                if group:
                    self.send_2[group - 1, s] = block.astype(self.low)
                else:
                    self.total[s] = block

            if group:
                self.thirds.append(self.send(self.send_2.at[group - 1], self.recv_2.at[group - 1], self.to(1, group)))

    def fourth(self):
        for copy in self.thirds:
            copy.wait_recv()
        self.fourths = []
        for by in ORDER:
            s = (self.pos[self.axes[2]] + by) % SIDE
            block = self.total[s]
            for n in range(3):
                block = block + self.recv_2[n, s].astype(jnp.float32)
            if by:
                self.send_3[by - 1] = block.astype(self.low)
                self.fourths.append(self.send(self.send_3.at[by - 1], self.recv_3.at[by - 1], self.to(2, by)))
            else:
                self.mine[...] = block

    def last(self):
        for copy in self.fourths:
            copy.wait_recv()
        block = self.mine[...]
        for n in range(3):
            block = block + self.recv_3[n].astype(jnp.float32)
        self.out[:, pl.ds(self.c0, self.c1 - self.c0)] = block


class SmallReduction(Reduction):
    low = jnp.float32
    COPIES = 1 + 3 + 3 + 3

    def take(self, bufs):
        self.landed, self.send_1, self.recv_1 = bufs

    @classmethod
    def more(cls, half, width):
        return [pltpu.VMEM((SIDE, SIDE, SIDE, 8, width), cls.low)] + [
            pltpu.VMEM((3, SIDE, SIDE, 8, width), cls.low)
        ] * 2

    def open(self, core, both):
        self.source = both.at[core]
        self.opening = self.send(both.at[1 - core], self.landed, {"dp": 1 - core})

    def term(self, *spot):
        kept = self.source
        mine = super().term(*spot)
        self.source = self.landed
        theirs = super().term(*spot)
        self.source = kept
        return mine + theirs

    def first(self):
        self.opening.wait_recv()
        self.seconds = [[]] * SIDE
        copies = []
        for by in (2, 1, 3):
            @pl.loop(0, SIDE)
            def _(s):
                for group in range(SIDE):
                    self.send_1[by - 1, group, s] = self.term(by, group, s, self.c0, self.c1)

            copies.append(self.send(self.send_1.at[by - 1], self.recv_1.at[by - 1], self.to(0, by)))
        self.seconds = [copies] + [[]] * 3

    def arrived(self, n, group, s):
        block = self.term(0, group, s, self.c0, self.c1)
        for way in range(3):
            block = block + self.recv_1[way, group, s]
        return block


SMALL = (2, 0, 128, 256, 2)


ROWS = 512
WIDTH = 1024
HIDDEN = 4096
HALF_IN = WIDTH // 2
HALF_FF = HIDDEN // 2
EXTRA = 128
TILE = 512
N_TILES = HIDDEN // TILE
HALF_TILES = N_TILES // 2
CURVE = 0.7978845608028654


def dot_nt(a, b):
    return lax.dot_general(a, b, (((1,), (1,)), ((), ())), preferred_element_type=jnp.float32)


def dot_nn(a, b):
    return lax.dot_general(a, b, (((1,), (0,)), ((), ())), preferred_element_type=jnp.float32)


def dot_tn(a, b):
    return lax.dot_general(a, b, (((0,), (0,)), ((), ())), preferred_element_type=jnp.float32)


def to_chips(pos, me, source, target, send_sem, recv_sem):
    @pl.loop(0, 64)
    def _(n):
        there = [(pos[0] + 2 + n // 16) % 4, (pos[1] + 2 + (n // 4) % 4) % 4, (pos[2] + 2 + n % 4) % 4]
        d = there[0] * 16 + there[1] * 4 + there[2]

        @pl.when(n != 42)
        def _():
            pltpu.make_async_remote_copy(
                src_ref=source.at[d],
                dst_ref=target.at[me],
                send_sem=send_sem,
                recv_sem=recv_sem,
                device_id={"expert": d},
                device_id_type=MESH,
            ).start()


def all_but_one(ref, sem):
    pltpu.make_async_copy(ref.at[pl.ds(0, 63)], ref.at[pl.ds(0, 63)], sem).wait()


def expert_kernel(
    x, r, w1_own, w1_other, w2_own, w2_other,
    y_back, d_back, g1, g2,
    w1, w2, x_in, r_in, xb, xt, act, slope, d_pre, acc, d_exp, out_rows,
    sent1, sent2, got1, got2, stage,
    w_sems, x_sems, r_sems, y_sems, d_sems, own_sems, pass_s, pass_r, out_sems,
):
    pos = coords()
    me = lax.axis_index("expert")
    core = lax.axis_index("dp")
    loads = [
        pltpu.make_async_copy(w1_own, w1.at[core], w_sems.at[0]),
        pltpu.make_async_copy(w1_other, w1.at[1 - core], w_sems.at[1]),
        pltpu.make_async_copy(w2_own, w2.at[core], w_sems.at[2]),
        pltpu.make_async_copy(w2_other, w2.at[1 - core], w_sems.at[3]),
    ]
    barrier = pltpu.get_barrier_semaphore()

    @pl.loop(1, 64)
    def _(n):
        pl.semaphore_signal(barrier, inc=1, device_id={"expert": (me + n) % 64}, device_id_type=MESH)

    pl.semaphore_signal(barrier, inc=1, device_id={"dp": 1 - core}, device_id_type=MESH)
    own_x = pltpu.make_async_copy(x.at[me], x_in.at[me], own_sems.at[0])
    own_r = pltpu.make_async_copy(r.at[me], r_in.at[me], own_sems.at[1])
    own_x.start()
    own_r.start()
    for load in loads:
        load.start()
    pl.semaphore_wait(barrier, 64)
    to_chips(pos, me, x, x_in, x_sems.at[0], x_sems.at[1])
    to_chips(pos, me, r, r_in, r_sems.at[0], r_sems.at[1])
    own_x.wait()
    all_but_one(x_in, x_sems.at[1])
    for load in loads:
        load.wait()

    @pl.loop(0, 8)
    def _(i):
        rows = x_in[pl.ds(i * 8, 8)].astype(jnp.float32).reshape(64, WIDTH)
        xb[pl.ds(pl.multiple_of(i * 64, 64), 64), :] = rows.astype(jnp.bfloat16)

    acc[...] = jnp.zeros_like(acc)

    @pl.loop(0, N_TILES)
    def _(c):
        cols = pl.ds(pl.multiple_of(c * TILE, TILE), TILE)
        pre = dot_nn(xb[:, :HALF_IN], w1[0, :, cols]) + dot_nn(xb[:, HALF_IN:], w1[1, :, cols])
        square = pre * pre
        t = jnp.tanh(CURVE * pre * (1.0 + 0.044715 * square))
        low = (0.5 * pre * (1.0 + t)).astype(jnp.bfloat16)
        act[:, cols] = low
        slope[:, cols] = 0.5 * (1.0 + t) + (0.5 * CURVE) * pre * (1.0 - t * t) * (1.0 + (3 * 0.044715) * square)
        half = c // HALF_TILES
        ff = pl.ds(pl.multiple_of((c % HALF_TILES) * TILE, TILE), TILE)
        acc[...] += dot_nn(low, w2[half, ff, :])

    own_r.wait()
    all_but_one(r_in, r_sems.at[1])

    @pl.loop(0, 8)
    def _(i):
        rows = pl.ds(pl.multiple_of(i * 64, 64), 64)
        low = acc[rows, :].astype(jnp.bfloat16)
        out = low.astype(jnp.float32)
        out_rows[pl.ds(i * 8, 8)] = out.reshape(8, 8, WIDTH).astype(jnp.bfloat16)
        parted = r_in[pl.ds(i * 8, 8)].astype(jnp.float32).reshape(64, WIDTH + EXTRA)
        gate = parted[:, WIDTH : WIDTH + 1] + parted[:, WIDTH + 1 : WIDTH + 2]
        valid = parted[:, WIDTH + 2 : WIDTH + 3]
        d_exp[rows, :] = (gate * valid * (parted[:, :WIDTH] + gate * out)).astype(jnp.bfloat16)

    own_y = pltpu.make_async_copy(out_rows.at[me], y_back.at[me], own_sems.at[2])
    own_y.start()
    to_chips(pos, me, out_rows, y_back, y_sems.at[0], y_sems.at[1])
    acc[...] = jnp.zeros_like(acc)

    @pl.loop(0, N_TILES)
    def _(c):
        cols = pl.ds(pl.multiple_of(c * TILE, TILE), TILE)
        half = c // HALF_TILES
        ff = pl.ds(pl.multiple_of((c % HALF_TILES) * TILE, TILE), TILE)
        d_act = dot_nt(d_exp[...], w2[half, ff, :])
        low = (slope[:, cols] * d_act).astype(jnp.bfloat16)
        d_pre[:, cols] = low
        acc[:, :HALF_IN] += dot_nt(low, w1[0, :, cols])
        acc[:, HALF_IN:] += dot_nt(low, w1[1, :, cols])

    own_y.wait()
    all_but_one(out_rows, y_sems.at[0])

    @pl.loop(0, 8)
    def _(i):
        rows = pl.ds(pl.multiple_of(i * 64, 64), 64)
        out_rows[pl.ds(i * 8, 8)] = acc[rows, :].reshape(8, 8, WIDTH).astype(jnp.bfloat16)

    own_d = pltpu.make_async_copy(out_rows.at[me], d_back.at[me], own_sems.at[3])
    own_d.start()
    to_chips(pos, me, out_rows, d_back, d_sems.at[0], d_sems.at[1])

    xt[...] = xb[...].astype(jnp.float32).T.astype(jnp.bfloat16)

    def passed(buf, got, c, base):
        return pltpu.make_async_remote_copy(
            src_ref=buf.at[c],
            dst_ref=got.at[c],
            send_sem=pass_s.at[base + c],
            recv_sem=pass_r.at[base + c],
            device_id={"dp": 1 - core},
            device_id_type=MESH,
        )

    def in_rows(half):
        return xt[pl.ds(pl.multiple_of(half * HALF_IN, HALF_IN), HALF_IN), :]

    @pl.loop(0, N_TILES)
    def _(c):
        cols = pl.ds(pl.multiple_of(c * TILE, TILE), TILE)
        sent1[c] = dot_nn(in_rows(1 - core), d_pre[:, cols]).astype(jnp.bfloat16)
        passed(sent1, got1, c, 0).start()

    @pl.loop(0, HALF_TILES)
    def _(c):
        cols = pl.ds(pl.multiple_of((1 - core) * HALF_FF + c * TILE, TILE), TILE)
        sent2[c] = dot_tn(act[:, cols], d_exp[...]).astype(jnp.bfloat16)
        passed(sent2, got2, c, N_TILES).start()

    def out1(c, slot):
        cols = pl.ds(pl.multiple_of(c * TILE, TILE), TILE)
        return pltpu.make_async_copy(stage.at[slot, :, pl.ds(0, TILE)], g1.at[:, cols], out_sems.at[slot])

    def out2(c, slot):
        rows = pl.ds(pl.multiple_of(c * TILE, TILE), TILE)
        return pltpu.make_async_copy(stage.at[slot], g2.at[rows, :], out_sems.at[slot])

    @pl.loop(0, N_TILES)
    def _(c):
        slot = c % 2
        cols = pl.ds(pl.multiple_of(c * TILE, TILE), TILE)

        @pl.when(c >= 2)
        def _():
            out1(c - 2, slot).wait()

        passed(sent1, got1, c, 0).wait_recv()
        stage[slot, :, pl.ds(0, TILE)] = dot_nn(in_rows(core), d_pre[:, cols]) + got1[c].astype(jnp.float32)
        out1(c, slot).start()

    out1(N_TILES - 2, 0).wait()
    out1(N_TILES - 1, 1).wait()

    @pl.loop(0, HALF_TILES)
    def _(c):
        slot = c % 2
        cols = pl.ds(pl.multiple_of(core * HALF_FF + c * TILE, TILE), TILE)

        @pl.when(c >= 2)
        def _():
            out2(c - 2, slot).wait()

        passed(sent2, got2, c, N_TILES).wait_recv()
        stage[slot] = dot_tn(act[:, cols], d_exp[...]) + got2[c].astype(jnp.float32)
        out2(c, slot).start()

    out2(HALF_TILES - 2, 0).wait()
    out2(HALF_TILES - 1, 1).wait()

    @pl.loop(0, N_TILES)
    def _(c):
        passed(sent1, got1, c, 0).wait_send()

    @pl.loop(0, HALF_TILES)
    def _(c):
        passed(sent2, got2, c, N_TILES).wait_send()

    own_d.wait()
    all_but_one(x_in, x_sems.at[0])
    all_but_one(r_in, r_sems.at[0])
    all_but_one(out_rows, d_sems.at[0])
    all_but_one(out_rows, y_sems.at[1])
    all_but_one(out_rows, d_sems.at[1])


def experts(x, r, w1_own, w1_other, w2_own, w2_other):
    low, wide = jnp.bfloat16, jnp.float32
    anywhere = pl.BlockSpec(memory_space=pl.ANY)
    return pl.pallas_call(
        expert_kernel,
        out_shape=(
            jax.ShapeDtypeStruct((64, 8, WIDTH), low),
            jax.ShapeDtypeStruct((64, 8, WIDTH), low),
            jax.ShapeDtypeStruct((HALF_IN, HIDDEN), wide),
            jax.ShapeDtypeStruct((HALF_FF, WIDTH), wide),
        ),
        in_specs=[anywhere] * 6,
        out_specs=(anywhere,) * 4,
        scratch_shapes=[
            pltpu.VMEM((2, HALF_IN, HIDDEN), low),
            pltpu.VMEM((2, HALF_FF, WIDTH), low),
            pltpu.VMEM((64, 8, WIDTH), low),
            pltpu.VMEM((64, 8, WIDTH + EXTRA), low),
            pltpu.VMEM((ROWS, WIDTH), low),
            pltpu.VMEM((WIDTH, ROWS), low),
            pltpu.VMEM((ROWS, HIDDEN), low),
            pltpu.VMEM((ROWS, HIDDEN), wide),
            pltpu.VMEM((ROWS, HIDDEN), low),
            pltpu.VMEM((ROWS, WIDTH), wide),
            pltpu.VMEM((ROWS, WIDTH), low),
            pltpu.VMEM((64, 8, WIDTH), low),
            pltpu.VMEM((N_TILES, HALF_IN, TILE), low),
            pltpu.VMEM((HALF_TILES, TILE, WIDTH), low),
            pltpu.VMEM((N_TILES, HALF_IN, TILE), low),
            pltpu.VMEM((HALF_TILES, TILE, WIDTH), low),
            pltpu.VMEM((2, HALF_IN, WIDTH), wide),
            pltpu.SemaphoreType.DMA((4,)),
            pltpu.SemaphoreType.DMA((2,)),
            pltpu.SemaphoreType.DMA((2,)),
            pltpu.SemaphoreType.DMA((2,)),
            pltpu.SemaphoreType.DMA((2,)),
            pltpu.SemaphoreType.DMA((4,)),
            pltpu.SemaphoreType.DMA((N_TILES + HALF_TILES,)),
            pltpu.SemaphoreType.DMA((N_TILES + HALF_TILES,)),
            pltpu.SemaphoreType.DMA((2,)),
        ],
        compiler_params=pltpu.CompilerParams(
            collective_id=2, has_side_effects=True, vmem_limit_bytes=63 * 1024 * 1024
        ),
        name="experts",
    )(x, r, w1_own, w1_other, w2_own, w2_other)


GROUP = 256
HEADS = 16
PAIRS = HEADS // 2
SLOTS = 512
BLOCK = 32
EPS = 1e-05
MASKED = -1e30


def lanes(start, size):
    return pl.ds(pl.multiple_of(start, 128), size)


def row_blocks(body, size=BLOCK):
    @pl.loop(0, GROUP // size)
    def _(i):
        body(pl.ds(pl.multiple_of(i * size, size), size), i * size)


def normed(v):
    centred = v - jnp.mean(v, -1, keepdims=True)
    inverse = lax.rsqrt(jnp.mean(centred * centred, -1, keepdims=True) + EPS)
    return centred * inverse, inverse


def lane_ids(rows, columns):
    return lax.broadcasted_iota(jnp.int32, (rows, columns), 1)


def row_ids(rows, columns):
    return lax.broadcasted_iota(jnp.int32, (rows, columns), 0)


def allowed_keys(core, length):
    query, key = row_ids(GROUP, GROUP), lane_ids(GROUP, GROUP)
    own = (key <= query) & (key + core * GROUP < length)
    other = (key < length) & (core == 1)
    return own, other


def head_scores(q, k_own, k_other, own, other):
    s_own = jnp.where(own, dot_nt(q, k_own) * 0.125, MASKED)
    s_other = jnp.where(other, dot_nt(q, k_other) * 0.125, MASKED)
    return s_own, s_other


def forward_kernel(
    tokens, teacher, routes_row, lengths, layer,
    x_out, parting_out, qkv_out, kv_other_out, attended_out, norm1_out, norm2_out, residual_out,
    lse_out, probs_out, placing_out, vectors_out,
    weights, norm1, qkv, kv_other, attended, norm2, residual, lse, probs, placing, vectors, parted, packed_x, packed_r,
    load_sems, out_sems, kv_sems,
):
    core = lax.axis_index("dp")
    length = lengths[0]
    spans = ((4096, 128), (1024, 1024), (2048, 1024), (0, 1024), (3072, 1024))
    loads = [
        pltpu.make_async_copy(layer.at[:, pl.ds(c, n)], weights.at[:, pl.ds(c, n)], load_sems.at[i])
        for i, (c, n) in enumerate(spans)
    ]
    for load in loads:
        load.start()
    outs = []

    def save(src, dst):
        copy = pltpu.make_async_copy(src, dst, out_sems.at[len(outs)])
        copy.start()
        outs.append(copy)

    barrier = pltpu.get_barrier_semaphore()
    pl.semaphore_signal(barrier, inc=1, device_id={"dp": 1 - core}, device_id_type=MESH)

    loads[0].wait()
    for g in range(16):
        part = weights[pl.ds(g * 64, 64), pl.ds(4096, 128)].astype(jnp.float32)
        part = jnp.sum(part.reshape(8, 8, 128), 0)
        vectors[:, g * 64 : (g + 1) * 64] = part[:, 64:]
    save(vectors, vectors_out)

    routes = jnp.where(row_ids(GROUP, GROUP) == lane_ids(GROUP, GROUP), routes_row[...], 0)
    route = jnp.sum(routes.astype(jnp.float32), -1, keepdims=True)

    def first_norm(rows, _):
        n, _ = normed(tokens[rows, :].astype(jnp.float32))
        norm1[rows, :] = (n * vectors[0:1, :] + vectors[1:2, :]).astype(jnp.bfloat16)

    row_blocks(first_norm)
    save(norm1, norm1_out)

    def project(block):
        @pl.loop(0, 2)
        def _(i):
            cols = lanes(block * 1024 + i * 512, 512)
            qkv[:, cols] = dot_nn(norm1[...], weights[:, cols]).astype(jnp.bfloat16)

    loads[1].wait()
    project(1)
    loads[2].wait()
    project(2)
    pl.semaphore_wait(barrier, 1)
    passed = pltpu.make_async_remote_copy(
        src_ref=qkv.at[:, pl.ds(1024, 2048)],
        dst_ref=kv_other,
        send_sem=kv_sems.at[0],
        recv_sem=kv_sems.at[1],
        device_id={"dp": 1 - core},
        device_id_type=MESH,
    )
    passed.start()
    loads[3].wait()
    project(0)
    save(qkv, qkv_out)
    passed.wait_recv()
    save(kv_other, kv_other_out)

    own, other = allowed_keys(core, length)
    lse[...] = jnp.zeros_like(lse)

    @pl.loop(0, PAIRS)
    def _(pair):
        q = qkv[:, lanes(pair * 128, 128)]
        k_own, v_own = qkv[:, lanes(1024 + pair * 128, 128)], qkv[:, lanes(2048 + pair * 128, 128)]
        k_other, v_other = kv_other[:, lanes(pair * 128, 128)], kv_other[:, lanes(1024 + pair * 128, 128)]
        left = lane_ids(GROUP, 128) < 64
        results = []
        for h in range(2):
            qh = jnp.where(left == (h == 0), q, jnp.zeros_like(q))
            s_own, s_other = head_scores(qh, k_own, k_other, own, other)
            top = jnp.max(jnp.maximum(s_own, s_other), -1, keepdims=True)
            e_own, e_other = jnp.exp(s_own - top), jnp.exp(s_other - top)
            total = jnp.sum(e_own + e_other, -1, keepdims=True)
            scale = 1.0 / total
            p_own, p_other = (e_own * scale).astype(jnp.bfloat16), (e_other * scale).astype(jnp.bfloat16)
            results.append(dot_nn(p_own, v_own) + dot_nn(p_other, v_other))
            lse[...] = jnp.where(lane_ids(GROUP, 128) == pair * 2 + h, top + jnp.log(total), lse[...])
        attended[:, lanes(pair * 128, 128)] = jnp.where(left, results[0], results[1]).astype(jnp.bfloat16)

    save(attended, attended_out)
    save(lse, lse_out)
    loads[4].wait()

    @pl.loop(0, 2)
    def _(i):
        cols = lanes(i * 512, 512)
        branch = dot_nn(attended[...], weights[:, lanes(3072 + i * 512, 512)])
        residual[:, cols] = tokens[:, cols].astype(jnp.float32) + branch

    save(residual, residual_out)

    def second_norm(rows, _):
        n, _ = normed(residual[rows, :])
        norm2[rows, :] = (n * vectors[2:3, :] + vectors[3:4, :]).astype(jnp.bfloat16)
        parted[rows, :WIDTH] = (residual[rows, :] - teacher[rows, :].astype(jnp.float32)).astype(jnp.bfloat16)

    row_blocks(second_norm)
    save(norm2, norm2_out)
    logits = dot_nn(norm2[...], weights[:, pl.ds(4096, 128)])
    ids = lane_ids(GROUP, 128)
    logits = jnp.where(ids < 64, logits, MASKED)
    e = jnp.exp(logits - jnp.max(logits, -1, keepdims=True))
    share = e / jnp.sum(e, -1, keepdims=True)
    chosen = ids.astype(jnp.float32) == route
    gate = jnp.sum(jnp.where(chosen, share, 0.0), -1, keepdims=True)
    probs[...] = jnp.where(ids == 64, gate, jnp.where(ids == 65, route, share))
    save(probs, probs_out)
    low_gate = gate.astype(jnp.bfloat16).astype(jnp.float32)
    valid = (row_ids(GROUP, 128) + core * GROUP < length).astype(jnp.float32)
    extras = jnp.where(ids == 0, low_gate, jnp.where(ids == 1, gate - low_gate, jnp.where(ids == 2, valid, 0.0)))
    parted[:, WIDTH:] = extras.astype(jnp.bfloat16)
    marks = chosen.astype(jnp.float32).astype(jnp.bfloat16)
    before = (lane_ids(GROUP, GROUP) < row_ids(GROUP, GROUP)).astype(jnp.float32).astype(jnp.bfloat16)
    rank = jnp.sum(jnp.where(chosen, dot_nn(before, marks), 0.0), -1, keepdims=True)
    slot = route * 8.0 + rank
    placing[...] = (lane_ids(GROUP, SLOTS).astype(jnp.float32) == slot).astype(jnp.float32).astype(jnp.bfloat16)
    save(placing, placing_out)
    for half in range(2):
        spread = placing[:, half * 256 : (half + 1) * 256].astype(jnp.float32).T.astype(jnp.bfloat16)
        sent = dot_nn(spread, norm2[...])
        packed_x[half * 32 : (half + 1) * 32] = sent.reshape(32, 8, WIDTH).astype(jnp.bfloat16)
        sent = dot_nn(spread, parted[...])
        packed_r[half * 32 : (half + 1) * 32] = sent.reshape(32, 8, WIDTH + EXTRA).astype(jnp.bfloat16)
    save(packed_x, x_out)
    save(packed_r, parting_out)
    passed.wait_send()
    for copy in outs:
        copy.wait()


def forward(tokens, teacher, routes, lengths, layer):
    low, wide = jnp.bfloat16, jnp.float32
    anywhere = pl.BlockSpec(memory_space=pl.ANY)
    vmem = pl.BlockSpec(memory_space=pltpu.VMEM)
    saved = [
        ((64, 8, WIDTH), low),
        ((64, 8, WIDTH + EXTRA), low),
        ((GROUP, 3 * WIDTH), low),
        ((GROUP, 2 * WIDTH), low),
        ((GROUP, WIDTH), low),
        ((GROUP, WIDTH), low),
        ((GROUP, WIDTH), low),
        ((GROUP, WIDTH), wide),
        ((GROUP, 128), wide),
        ((GROUP, 128), wide),
        ((GROUP, SLOTS), low),
        ((8, WIDTH), wide),
    ]
    return pl.pallas_call(
        forward_kernel,
        out_shape=tuple(jax.ShapeDtypeStruct(s, t) for s, t in saved),
        in_specs=[vmem, vmem, vmem, pl.BlockSpec(memory_space=pltpu.SMEM), anywhere],
        out_specs=(anywhere,) * len(saved),
        scratch_shapes=[
            pltpu.VMEM((WIDTH, AG_COLS), low),
            pltpu.VMEM((GROUP, WIDTH), low),
            pltpu.VMEM((GROUP, 3 * WIDTH), low),
            pltpu.VMEM((GROUP, 2 * WIDTH), low),
            pltpu.VMEM((GROUP, WIDTH), low),
            pltpu.VMEM((GROUP, WIDTH), low),
            pltpu.VMEM((GROUP, WIDTH), wide),
            pltpu.VMEM((GROUP, 128), wide),
            pltpu.VMEM((GROUP, 128), wide),
            pltpu.VMEM((GROUP, SLOTS), low),
            pltpu.VMEM((8, WIDTH), wide),
            pltpu.VMEM((GROUP, WIDTH + EXTRA), low),
            pltpu.VMEM((64, 8, WIDTH), low),
            pltpu.VMEM((64, 8, WIDTH + EXTRA), low),
            pltpu.SemaphoreType.DMA((5,)),
            pltpu.SemaphoreType.DMA((len(saved),)),
            pltpu.SemaphoreType.DMA((2,)),
        ],
        compiler_params=pltpu.CompilerParams(
            collective_id=3, has_side_effects=True, vmem_limit_bytes=56 * 1024 * 1024
        ),
        name="forward",
    )(tokens, teacher, routes, lengths, layer)


def backward_kernel(
    y_back, d_back, teacher, lengths, layer, qkv, kv_other, norm2, residual, lse, probs,
    placing, vectors, g1, g2,
    mixed_out, d_resid, dq, dkv_own, dkv_other, d_branch, grad_router, norm_grads, g1_out, g2_out,
    w_out, w_router, eo, dn, sums, d_attended, logit_parts,
    held1, held2, pass_sems, load_sems,
):
    core = lax.axis_index("dp")
    length = lengths[0]
    passing = [
        pltpu.make_async_copy(g1, held1, pass_sems.at[0]),
        pltpu.make_async_copy(g2, held2, pass_sems.at[1]),
    ]
    passed_on = [
        pltpu.make_async_copy(held1, g1_out, pass_sems.at[2]),
        pltpu.make_async_copy(held2, g2_out, pass_sems.at[3]),
    ]
    loads = [
        pltpu.make_async_copy(layer.at[:, pl.ds(3072, 1024)], w_out, load_sems.at[0]),
        pltpu.make_async_copy(layer.at[:, pl.ds(4096, 128)], w_router, load_sems.at[1]),
    ]
    for copy in loads + passing:
        copy.start()
    rows_back = y_back[...].astype(jnp.float32).reshape(SLOTS, WIDTH).astype(jnp.bfloat16)
    eo[...] = dot_nn(placing[...], rows_back)
    rows_back = d_back[...].astype(jnp.float32).reshape(SLOTS, WIDTH).astype(jnp.bfloat16)
    dn[...] = dot_nn(placing[...], rows_back)
    sums[...] = jnp.zeros_like(sums)

    def loss(rows, first):
        ids = lane_ids(BLOCK, 128)
        share = probs[rows, :]
        gate = share[:, 64:65]
        chosen = ids.astype(jnp.float32) == share[:, 65:66]
        share = jnp.where(ids < 64, share, 0.0)
        out = eo[rows, :]
        mixed = (residual[rows, :] + gate * out).astype(jnp.bfloat16)
        mixed_out[rows, :] = mixed
        valid = (row_ids(BLOCK, 1) + first + core * GROUP < length).astype(jnp.float32)
        d_mixed = valid * (mixed.astype(jnp.float32) - teacher[rows, :].astype(jnp.float32))
        d_resid[rows, :] = d_mixed
        d_gate = jnp.sum(d_mixed * out, -1, keepdims=True)
        d_logits = d_gate * gate * (chosen.astype(jnp.float32) - share)
        high = d_logits.astype(jnp.bfloat16)
        logit_parts[rows, :128] = high
        logit_parts[rows, 128:] = (d_logits - high.astype(jnp.float32)).astype(jnp.bfloat16)
        square = jnp.sum((d_mixed * d_mixed).reshape(BLOCK // 8, 8, WIDTH), 0)
        sums[0] += square

    row_blocks(loss)
    loads[0].wait()
    loads[1].wait()
    dn[...] += dot_nt(logit_parts[:, :128], w_router[...]) + dot_nt(logit_parts[:, 128:], w_router[...])
    both = dot_tn(norm2[...], logit_parts[...])
    grad_router[...] = both[:, :128] + both[:, 128:]

    def norm_back(rows, _):
        n, inverse = normed(residual[rows, :])
        u = dn[rows, :]
        scaled = u * vectors[2:3, :]
        average = jnp.mean(scaled, -1, keepdims=True)
        project = jnp.mean(scaled * n, -1, keepdims=True)
        d = d_resid[rows, :] + inverse * (scaled - average - n * project)
        d_resid[rows, :] = d
        d_branch[rows, :] = d.astype(jnp.bfloat16)
        sums[1] += jnp.sum((u * n).reshape(BLOCK // 8, 8, WIDTH), 0)
        sums[2] += jnp.sum(u.reshape(BLOCK // 8, 8, WIDTH), 0)

    row_blocks(norm_back)
    valid_all = jnp.clip(length - core * GROUP, 0, GROUP).astype(jnp.float32)
    ids = row_ids(8, WIDTH)
    square = jnp.sum(sums[0])
    norm_grads[...] = jnp.where(
        ids == 2,
        jnp.sum(sums[1], 0, keepdims=True),
        jnp.where(
            ids == 3,
            jnp.sum(sums[2], 0, keepdims=True),
            jnp.where(ids == 4, square, jnp.where(ids == 5, valid_all, 0.0)),
        ),
    )

    @pl.loop(0, 2)
    def _(i):
        cols = lanes(i * 512, 512)
        rows = pl.ds(pl.multiple_of(i * 512, 512), 512)
        d_attended[:, cols] = dot_nt(d_branch[...], w_out[rows, :]).astype(jnp.bfloat16)

    own, other = allowed_keys(core, length)
    for copy, onward in zip(passing, passed_on):
        copy.wait()
        onward.start()

    @pl.loop(0, PAIRS)
    def _(pair):
        q, do = qkv[:, lanes(pair * 128, 128)], d_attended[:, lanes(pair * 128, 128)]
        k_own, v_own = qkv[:, lanes(1024 + pair * 128, 128)], qkv[:, lanes(2048 + pair * 128, 128)]
        k_other, v_other = kv_other[:, lanes(pair * 128, 128)], kv_other[:, lanes(1024 + pair * 128, 128)]
        left = lane_ids(GROUP, 128) < 64
        zero = jnp.zeros_like(q)
        parts = []
        for h in range(2):
            qh = jnp.where(left == (h == 0), q, zero)
            doh = jnp.where(left == (h == 0), do, zero)
            s_own, s_other = head_scores(qh, k_own, k_other, own, other)
            log_total = jnp.sum(jnp.where(lane_ids(GROUP, 128) == pair * 2 + h, lse[...], 0.0), -1, keepdims=True)
            p_own, p_other = jnp.exp(s_own - log_total), jnp.exp(s_other - log_total)
            dp_own, dp_other = dot_nt(doh, v_own), dot_nt(doh, v_other)
            total = jnp.sum(p_own * dp_own + p_other * dp_other, -1, keepdims=True)
            ds_own = (p_own * (dp_own - total)).astype(jnp.bfloat16)
            ds_other = (p_other * (dp_other - total)).astype(jnp.bfloat16)
            p_own, p_other = p_own.astype(jnp.bfloat16), p_other.astype(jnp.bfloat16)
            parts.append((
                dot_nn(ds_own, k_own) + dot_nn(ds_other, k_other),
                dot_tn(ds_own, q),
                dot_tn(ds_other, q),
                dot_tn(p_own, do),
                dot_tn(p_other, do),
            ))
        d_q, d_k, d_k_other, d_v, d_v_other = [jnp.where(left, a, b) for a, b in zip(*parts)]
        dq[:, lanes(pair * 128, 128)] = (d_q * 0.125).astype(jnp.bfloat16)
        dkv_own[:, lanes(pair * 128, 128)] = (d_k * 0.125).astype(jnp.bfloat16)
        dkv_own[:, lanes(1024 + pair * 128, 128)] = d_v.astype(jnp.bfloat16)
        dkv_other[:, lanes(pair * 128, 128)] = (d_k_other * 0.125).astype(jnp.bfloat16)
        dkv_other[:, lanes(1024 + pair * 128, 128)] = d_v_other.astype(jnp.bfloat16)

    for onward in passed_on:
        onward.wait()


def backward(y_back, d_back, teacher, lengths, layer, qkv, kv_other, norm2, residual, lse, probs,
             placing, vectors, g1, g2):
    low, wide = jnp.bfloat16, jnp.float32
    anywhere = pl.BlockSpec(memory_space=pl.ANY)
    vmem = pl.BlockSpec(memory_space=pltpu.VMEM)
    made = [
        ((GROUP, WIDTH), low),
        ((GROUP, WIDTH), wide),
        ((GROUP, WIDTH), low),
        ((GROUP, 2 * WIDTH), low),
        ((GROUP, 2 * WIDTH), low),
        ((GROUP, WIDTH), low),
        ((WIDTH, 128), wide),
        ((8, WIDTH), wide),
        (g1.shape, wide),
        (g2.shape, wide),
    ]
    return pl.pallas_call(
        backward_kernel,
        out_shape=tuple(jax.ShapeDtypeStruct(s, t) for s, t in made),
        in_specs=[vmem, vmem, vmem, pl.BlockSpec(memory_space=pltpu.SMEM), anywhere] + [vmem] * 8 + [anywhere] * 2,
        out_specs=(vmem,) * 8 + (anywhere,) * 2,
        scratch_shapes=[
            pltpu.VMEM((WIDTH, WIDTH), low),
            pltpu.VMEM((WIDTH, 128), low),
            pltpu.VMEM((GROUP, WIDTH), wide),
            pltpu.VMEM((GROUP, WIDTH), wide),
            pltpu.VMEM((3, 8, WIDTH), wide),
            pltpu.VMEM((GROUP, WIDTH), low),
            pltpu.VMEM((GROUP, 256), low),
            pltpu.VMEM(g1.shape, wide),
            pltpu.VMEM(g2.shape, wide),
            pltpu.SemaphoreType.DMA((4,)),
            pltpu.SemaphoreType.DMA((2,)),
        ],
        compiler_params=pltpu.CompilerParams(vmem_limit_bytes=56 * 1024 * 1024),
        name="backward",
    )(y_back, d_back, teacher, lengths, layer, qkv, kv_other, norm2, residual, lse, probs,
      placing, vectors, g1, g2)


HALF = WIDTH // 2


def transposed(block):
    return block.astype(jnp.float32).T.astype(jnp.bfloat16)


def finish_kernel(
    tokens, norm1, attended, vectors, d_resid, dq, dkv_own, dkv_other, d_branch, grad_router, norm_grads, layer,
    sum_qkv, sum_out, sum_side, grad_tokens,
    weights, x, d_res, left, left_t, mine, theirs, got_left, dqkv, d_both, acc, sums, grad_qkv, grad_out,
    router, vec, norms, side, load_sems, *rest,
):
    pos = coords()
    core = lax.axis_index("dp")
    partner = {"dp": 1 - core}
    keep, give = pl.ds(core * HALF, HALF), pl.ds((1 - core) * HALF, HALF)
    own, other = pl.ds(0, GROUP), pl.ds(GROUP, GROUP)
    spans = (
        (norm1.at[:, keep], left.at[0]),
        (attended.at[:, keep], left.at[1]),
        (d_branch, d_both.at[own, :]),
        (layer.at[:, pl.ds(0, 3072)], weights),
        (dq, dqkv.at[own, pl.ds(0, WIDTH)]),
        (dkv_own, mine.at[0]),
        (dkv_other, mine.at[1]),
        (tokens, x),
        (vectors, vec),
        (d_resid, d_res),
        (grad_router, router),
        (norm_grads, norms),
    )
    loads = [pltpu.make_async_copy(src, dst, load_sems.at[n]) for n, (src, dst) in enumerate(spans)]
    for load in loads:
        load.start()
    greet(pos, core)
    send = Sender(*rest[-2:])
    to_left = send(attended.at[:, give], got_left.at[1], partner)
    to_branch = send(d_branch, d_both.at[other, :], partner)
    to_other = send(dkv_other, theirs.at[1], partner)
    to_norm = send(norm1.at[:, give], got_left.at[0], partner)
    to_query = send(dq, dqkv.at[other, pl.ds(0, WIDTH)], partner)
    to_own = send(dkv_own, theirs.at[0], partner)
    bufs, groups = list(rest[:-2]), []
    for piece in RS_PIECES + (SMALL,):
        kind = Reduction if piece is not SMALL else SmallReduction
        count = len(kind.scratch(piece))
        source, out = ((grad_qkv, sum_qkv), (grad_out, sum_out), (side, sum_side))[piece[0]]
        groups.append(kind(piece, pos, send, source, out, bufs[:count]))
        bufs = bufs[count:]
    query, value, branch, small = groups

    loads[0].wait()
    left_t[0, :, own] = transposed(left[0])
    loads[1].wait()
    left_t[1, :, own] = transposed(left[1])
    loads[2].wait()
    to_left.wait_recv()
    left_t[1, :, other] = transposed(got_left[1])
    to_branch.wait_recv()

    @pl.loop(0, 2)
    def _(i):
        cols = lanes(i * 512, 512)
        grad_out[:, :, :, :, cols] = dot_nn(left_t[1], d_both[:, cols]).reshape(SIDE, SIDE, SIDE, 8, 512)

    branch.first()
    loads[3].wait()
    loads[4].wait()
    acc[...] = jnp.zeros_like(acc)

    def back(first, count):
        @pl.loop(0, count)
        def _(i):
            cols = lanes(first + i * 512, 512)
            acc[...] += dot_nt(dqkv[own, cols], weights[:, cols])

    def grads(first, count):
        @pl.loop(0, count)
        def _(i):
            cols = lanes(first + i * 512, 512)
            grad_qkv[:, :, :, :, cols] = dot_nn(left_t[0], dqkv[:, cols]).reshape(SIDE, SIDE, SIDE, 8, 512)

    back(0, 2)
    loads[5].wait()
    loads[6].wait()
    to_other.wait_recv()

    def join(first, a, b):
        def add(rows, start):
            spot = pl.ds(pl.multiple_of(first + start, BLOCK), BLOCK)
            dqkv[spot, pl.ds(WIDTH, 2 * WIDTH)] = (
                a[rows, :].astype(jnp.float32) + b[rows, :].astype(jnp.float32)
            ).astype(jnp.bfloat16)

        row_blocks(add)

    join(0, mine.at[0], theirs.at[1])
    to_norm.wait_recv()
    left_t[0, :, other] = transposed(got_left[0])
    to_query.wait_recv()
    to_own.wait_recv()
    join(GROUP, theirs.at[0], mine.at[1])
    grads(0, 3)
    query.first()
    branch.second()
    grads(1536, 3)
    value.first()
    back(1024, 4)
    query.second()
    for load in loads[7:]:
        load.wait()
    sums[...] = jnp.zeros_like(sums)

    def norm_back(rows, _):
        n, inverse = normed(x[rows, :].astype(jnp.float32))
        u = acc[rows, :]
        scaled = u * vec[0:1, :]
        average = jnp.mean(scaled, -1, keepdims=True)
        project = jnp.mean(scaled * n, -1, keepdims=True)
        grad_tokens[rows, :] = d_res[rows, :] + inverse * (scaled - average - n * project)
        sums[0] += jnp.sum((u * n).reshape(BLOCK // 8, 8, WIDTH), 0)
        sums[1] += jnp.sum(u.reshape(BLOCK // 8, 8, WIDTH), 0)

    row_blocks(norm_back)
    ids = row_ids(8, WIDTH)
    vector_grads = jnp.where(
        ids == 0,
        jnp.sum(sums[0], 0, keepdims=True),
        jnp.where(ids == 1, jnp.sum(sums[1], 0, keepdims=True), norms[...]),
    )
    for half in range(2):
        rows = router[half * 512 : (half + 1) * 512, :]
        side[half, :, :, :, :, pl.ds(0, 128)] = rows.reshape(SIDE, SIDE, SIDE, 8, 128)
        for at in range(SIDE):
            block = vector_grads[:, (half * SIDE + at) * 128 : (half * SIDE + at + 1) * 128]
            side[half, at, :, :, :, pl.ds(128, 128)] = jnp.broadcast_to(block[None, None], (SIDE, SIDE, 8, 128))
    small.open(core, side)
    value.second()
    branch.third()
    small.first()
    query.third()
    value.third()
    small.third()
    branch.fourth()
    query.fourth()
    value.fourth()
    small.fourth()
    branch.last()
    query.last()
    value.last()
    small.last()
    send.close()


def finish(tokens, norm1, attended, vectors, d_resid, dq, dkv_own, dkv_other, d_branch, grad_router, norm_grads,
           layer):
    low, wide = jnp.bfloat16, jnp.float32
    anywhere = pl.BlockSpec(memory_space=pl.ANY)
    vmem = pl.BlockSpec(memory_space=pltpu.VMEM)
    lead = (SIDE, SIDE, SIDE, 8)
    scratch, copies = SmallReduction.scratch(SMALL), 6 + SmallReduction.COPIES
    for piece in RS_PIECES[::-1]:
        scratch, copies = Reduction.scratch(piece) + scratch, copies + Reduction.COPIES
    return pl.pallas_call(
        finish_kernel,
        out_shape=tuple(jax.ShapeDtypeStruct((8, c), wide) for c in RS_COLS)
        + (jax.ShapeDtypeStruct((GROUP, WIDTH), wide),),
        in_specs=[anywhere] * 12,
        out_specs=(vmem,) * 4,
        scratch_shapes=[
            pltpu.VMEM((WIDTH, 3 * WIDTH), low),
            pltpu.VMEM((GROUP, WIDTH), low),
            pltpu.VMEM((GROUP, WIDTH), wide),
            pltpu.VMEM((2, GROUP, HALF), low),
            pltpu.VMEM((2, HALF, 2 * GROUP), low),
            pltpu.VMEM((2, GROUP, 2 * WIDTH), low),
            pltpu.VMEM((2, GROUP, 2 * WIDTH), low),
            pltpu.VMEM((2, GROUP, HALF), low),
            pltpu.VMEM((2 * GROUP, 3 * WIDTH), low),
            pltpu.VMEM((2 * GROUP, WIDTH), low),
            pltpu.VMEM((GROUP, WIDTH), wide),
            pltpu.VMEM((2, 8, WIDTH), wide),
            pltpu.VMEM(lead + (3 * WIDTH,), wide),
            pltpu.VMEM(lead + (WIDTH,), wide),
            pltpu.VMEM((WIDTH, 128), wide),
            pltpu.VMEM((8, WIDTH), wide),
            pltpu.VMEM((8, WIDTH), wide),
            pltpu.VMEM((2,) + lead + (256,), wide),
            pltpu.SemaphoreType.DMA((12,)),
            *scratch,
            pltpu.SemaphoreType.DMA((copies,)),
            pltpu.SemaphoreType.DMA((copies,)),
        ],
        compiler_params=pltpu.CompilerParams(
            collective_id=1, has_side_effects=True, vmem_limit_bytes=60 * 1024 * 1024
        ),
        name="finish",
    )(tokens, norm1, attended, vectors, d_resid, dq, dkv_own, dkv_other, d_branch, grad_router, norm_grads, layer)


def results_kernel(sum_qkv, sum_out, side, given_tokens, qkv, out, router, vectors, loss, tokens):
    place = (lax.axis_index("dp") * 64 + lax.axis_index("expert")) % 16
    qkv[...] = sum_qkv[...]
    out[...] = sum_out[...]
    tokens[...] = given_tokens[...]
    router[...] = side[:, :64]
    sums = side[:, 128:256]
    vectors[...] = pltpu.roll(sums, (16 - place) * 8 % 128, 1)
    loss[...] = sums[4:5, 0:1] / (sums[5:6, 0:1] * WIDTH)


def results(*sums):
    wide = jnp.float32
    shapes = ((8, 3072), (8, 1024), (8, 64), (8, 128), (1, 1), (GROUP, WIDTH))
    vmem = pl.BlockSpec(memory_space=pltpu.VMEM)
    return pl.pallas_call(
        results_kernel,
        out_shape=tuple(jax.ShapeDtypeStruct(s, wide) for s in shapes),
        in_specs=[vmem] * 4,
        out_specs=(vmem,) * 6,
        name="results",
    )(*sums)


def per_device(
    tokens,
    teacher,
    lengths,
    routes,
    ln1_gain,
    ln1_bias,
    query_key_value_weight,
    output_weight,
    ln2_gain,
    ln2_bias,
    router_weight,
    w_in,
    w_down,
):
    device = lax.axis_index("dp") * 64 + lax.axis_index("expert")
    vectors = jnp.tile(jnp.stack([ln1_gain, ln1_bias, ln2_gain, ln2_bias] * 2).astype(jnp.float32), (1, 8))
    vectors = jnp.where(jnp.arange(64)[None, :] // 8 == device % 8, vectors, 0)
    layer, in_other, down_other = gather_layer(
        query_key_value_weight, output_weight, router_weight, vectors, w_in[0], w_down[0]
    )
    x, parting, qkv, kv_other, attended, norm1, norm2, residual, lse, probs, placing, vectors = forward(
        tokens[0], teacher[0], routes.reshape(1, GROUP), lengths, layer
    )
    y_back, d_back, g1, g2 = experts(x, parting, w_in[0], in_other, w_down[0], down_other)
    mixed, d_resid, dq, dkv_own, dkv_other, d_branch, grad_router, norm_grads, g1, g2 = backward(
        y_back, d_back, teacher[0], lengths, layer, qkv, kv_other, norm2, residual, lse, probs, placing, vectors,
        g1, g2,
    )
    sums = finish(
        tokens[0], norm1, attended, vectors, d_resid, dq, dkv_own, dkv_other, d_branch, grad_router, norm_grads,
        layer,
    )
    grad_qkv, grad_out, grad_router, vector_grads, loss_value, grad_tokens = results(*sums)
    return (
        mixed[None],
        loss_value[0, 0],
        grad_tokens[None],
        vector_grads[0, :8],
        vector_grads[1, :8],
        grad_qkv,
        grad_out,
        vector_grads[2, :8],
        vector_grads[3, :8],
        grad_router,
        g1[None],
        g2[None],
    )


def solution(mesh):
    placed = (
        P("expert", "dp", None),
        P("expert", "dp", None),
        P("expert"),
        P("expert", "dp", None),
        P(("dp", "expert")),
        P(("dp", "expert")),
        P(("dp", "expert"), None),
        P(("dp", "expert"), None),
        P(("dp", "expert")),
        P(("dp", "expert")),
        P(("dp", "expert"), None),
        P("expert", "dp", None),
        P("expert", "dp", None),
    )
    return jax.shard_map(
        per_device,
        mesh=mesh,
        in_specs=placed,
        out_specs=(
            P("expert", "dp", None),
            P(),
            P("expert", "dp", None),
            P(("dp", "expert")),
            P(("dp", "expert")),
            P(("dp", "expert"), None),
            P(("dp", "expert"), None),
            P(("dp", "expert")),
            P(("dp", "expert")),
            P(("dp", "expert"), None),
            P("expert", "dp", None),
            P("expert", "dp", None),
        ),
        check_vma=False,
    )
```

```python
import jax
import jax.numpy as jnp
from jax import lax
from jax.experimental import pallas as pl
from jax.experimental.pallas import tpu as pltpu
from jax.sharding import PartitionSpec as P

MESH = pl.DeviceIdType.MESH
SIDE = 4
FULL = slice(None)

AG_COLS = 4224
AG_PIECES = ((0, 768, 1408), (1408, 2176, 2816), (2816, 3584, 4224))


def coords():
    e = lax.axis_index("expert")
    return [e // 16, (e // 4) % 4, e % 4]


def shifted(pos, axis, by):
    out = list(pos)
    out[axis] = (pos[axis] + by) % SIDE
    return out


def chip(pos):
    return {"expert": pos[0] * 16 + pos[1] * 4 + pos[2]}


def greet(pos, core):
    barrier = pltpu.get_barrier_semaphore()
    for axis in range(3):
        for by in range(1, SIDE):
            pl.semaphore_signal(barrier, inc=1, device_id=chip(shifted(pos, axis, by)), device_id_type=MESH)
    pl.semaphore_signal(barrier, inc=1, device_id={"dp": 1 - core}, device_id_type=MESH)
    pl.semaphore_wait(barrier, 10)


class Sender:
    def __init__(self, send_sems, recv_sems):
        self.send_sems, self.recv_sems, self.count, self.sent = send_sems, recv_sems, 0, []

    def __call__(self, src, dst, device):
        copy = pltpu.make_async_remote_copy(
            src_ref=src,
            dst_ref=dst,
            send_sem=self.send_sems.at[self.count],
            recv_sem=self.recv_sems.at[self.count],
            device_id=device,
            device_id_type=MESH,
        )
        copy.start()
        self.count += 1
        self.sent.append(copy)
        return copy

    def close(self):
        for copy in self.sent:
            copy.wait_send()


def gather_kernel(
    q, o, r, vectors, w_in, w_down, whole, in_other, down_other, shard, own_sem, send_sems, recv_sems
):
    pos = coords()
    core = lax.axis_index("dp")
    partner = {"dp": 1 - core}
    shard[:, :3072] = q[...]
    shard[:, 3072:4096] = o[...]
    shard[:, 4096:] = jnp.concatenate([r[...].astype(jnp.float32), vectors[...]], 1).astype(jnp.bfloat16)
    own = pltpu.make_async_copy(shard, whole.at[(core, *pos)], own_sem)
    own.start()
    greet(pos, core)
    send = Sender(send_sems, recv_sems)

    def share(region, c0, c1, device):
        spot = whole.at[(core, *region, FULL, pl.ds(c0, c1 - c0))]
        return send(spot, spot, device)

    plans = []
    for piece, (c0, mid, c1) in enumerate(AG_PIECES):
        axes = [(piece + step) % 3 for step in range(3)]
        spot = whole.at[(core, *pos, FULL, pl.ds(c0, c1 - c0))]
        first = [send(shard.at[:, pl.ds(c0, c1 - c0)], spot, chip(shifted(pos, axes[0], by))) for by in (1, 3, 2)]
        plans.append((axes, c0, mid, c1, first))
    across = [send(w_in, in_other, partner), send(w_down, down_other, partner)]
    own.wait()

    def line(axes, second, third):
        region = [None] * 3
        region[axes[0]], region[axes[1]], region[axes[2]] = FULL, second, third
        return region

    def at(axis, by):
        return (pos[axis] + by) % SIDE

    seconds, lines = [], [{} for _ in plans]

    def onward(piece, by):
        axes, c0, mid, c1, _ = plans[piece]
        region = line(axes, at(axes[1], by), pos[axes[2]])
        lines[piece][by] = (
            share(region, c0, c1, chip(shifted(pos, axes[2], 1))),
            share(region, c0, c1, chip(shifted(pos, axes[2], 3))),
        )
        across.append(share(region, c0, c1, partner))

    def relay(piece, by):
        axes, c0, mid, c1, _ = plans[piece]
        up, down = lines[piece][by]
        up.wait_recv()
        below = line(axes, at(axes[1], by), at(axes[2], 3))
        on_up = share(below, c0, mid, chip(shifted(pos, axes[2], 1)))
        down.wait_recv()
        above = line(axes, at(axes[1], by), at(axes[2], 1))
        on_down = share(above, mid, c1, chip(shifted(pos, axes[2], 3)))
        across.append(share(below, c0, c1, partner))
        across.append(share(above, c0, c1, partner))
        lines[piece][by] = (on_up, on_down)

    def end(piece, by):
        axes, c0, mid, c1, _ = plans[piece]
        for copy in lines[piece][by]:
            copy.wait_recv()
        across.append(share(line(axes, at(axes[1], by), at(axes[2], 2)), c0, c1, partner))

    for piece, (axes, c0, mid, c1, first) in enumerate(plans):
        for copy in first:
            copy.wait_recv()
        region = line(axes, pos[axes[1]], pos[axes[2]])
        seconds.append([share(region, c0, c1, chip(shifted(pos, axes[1], by))) for by in (1, 3, 2)])
        onward(piece, 0)
    for n, by in enumerate((3, 1)):
        for piece in range(3):
            seconds[piece][n].wait_recv()
            onward(piece, by)
    for piece in range(3):
        relay(piece, 0)
    for piece in range(3):
        seconds[piece][2].wait_recv()
        onward(piece, 2)
    for by in (3, 1, 2):
        for piece in range(3):
            relay(piece, by)
    for by in (0, 3, 1, 2):
        for piece in range(3):
            end(piece, by)
    for copy in across:
        copy.wait_recv()
    send.close()


def gather_layer(q, o, r, vectors, w_in, w_down):
    copies = 3 * (3 + 3 + 4 * 4 + 4 * 4) + 2
    anywhere, vmem = pl.BlockSpec(memory_space=pl.ANY), pl.BlockSpec(memory_space=pltpu.VMEM)
    whole, in_other, down_other = pl.pallas_call(
        gather_kernel,
        out_shape=(
            jax.ShapeDtypeStruct((2, SIDE, SIDE, SIDE, 8, AG_COLS), jnp.bfloat16),
            jax.ShapeDtypeStruct(w_in.shape, w_in.dtype),
            jax.ShapeDtypeStruct(w_down.shape, w_down.dtype),
        ),
        in_specs=[vmem] * 4 + [anywhere] * 2,
        out_specs=(anywhere,) * 3,
        scratch_shapes=[
            pltpu.VMEM((8, AG_COLS), jnp.bfloat16),
            pltpu.SemaphoreType.DMA,
            pltpu.SemaphoreType.DMA((copies,)),
            pltpu.SemaphoreType.DMA((copies,)),
        ],
        compiler_params=pltpu.CompilerParams(collective_id=0, has_side_effects=True),
        name="gather_layer",
    )(q, o, r, vectors, w_in, w_down)
    return whole.reshape(1024, AG_COLS), in_other, down_other


RS_COLS = (3072, 1024, 256)
RS_PIECES = ((0, 0, 768, 1536, 0), (0, 1536, 2304, 3072, 1), (1, 0, 512, 1024, 2))
ORDER = (2, 1, 3, 0)


class Reduction:
    low = jnp.bfloat16
    COPIES = 8 + 8 + 3 + 3

    def __init__(self, piece, pos, send, source, out, bufs):
        _, self.c0, self.mid, self.c1, first = piece
        self.axes = [(first + step) % 3 for step in range(3)]
        self.pos, self.send, self.source, self.out = pos, send, source, out
        (self.total, self.send_2, self.recv_2, self.mine, self.send_3, self.recv_3) = bufs[:6]
        self.take(bufs[6:])

    def take(self, bufs):
        self.send_a, self.recv_a, self.send_b, self.recv_b = bufs

    @classmethod
    def scratch(cls, piece):
        _, c0, mid, c1, _ = piece
        width, low, wide = c1 - c0, cls.low, jnp.float32
        return [
            pltpu.VMEM((SIDE, 8, width), wide),
            pltpu.VMEM((3, SIDE, 8, width), low),
            pltpu.VMEM((3, SIDE, 8, width), low),
            pltpu.VMEM((8, width), wide),
            pltpu.VMEM((3, 8, width), low),
            pltpu.VMEM((3, 8, width), low),
        ] + cls.more(mid - c0, width)

    @classmethod
    def more(cls, half, width):
        return [pltpu.VMEM((2, SIDE, SIDE, 8, half), cls.low)] * 2 + [pltpu.VMEM((2, SIDE, SIDE, 8, width), cls.low)] * 2

    def to(self, step, by):
        return chip(shifted(self.pos, self.axes[step], by))

    def term(self, first, second, third, c0, c1):
        spot = [None] * 3
        spot[self.axes[0]] = (self.pos[self.axes[0]] + first) % SIDE
        spot[self.axes[1]] = (self.pos[self.axes[1]] + second) % SIDE
        spot[self.axes[2]] = third
        return self.source[(*spot, FULL, pl.ds(c0, c1 - c0))]

    def first(self):
        self.firsts = []
        for group in ORDER:
            @pl.loop(0, SIDE)
            def _(s):
                self.send_a[0, group, s] = self.term(2, group, s, self.c0, self.mid).astype(self.low)
                self.send_a[1, group, s] = self.term(2, group, s, self.mid, self.c1).astype(self.low)

            self.firsts.append([
                self.send(self.send_a.at[way, group], self.recv_a.at[way, group], self.to(0, (1, 3)[way]))
                for way in range(2)
            ])

    def second(self):
        self.seconds = []
        half = self.mid - self.c0
        for n, group in enumerate(ORDER):
            for copy in self.firsts[n]:
                copy.wait_recv()

            @pl.loop(0, SIDE)
            def _(s):
                for way, by in enumerate((1, 3)):
                    for part, (c0, c1) in enumerate(((self.c0, self.mid), (self.mid, self.c1))):
                        block = self.term(by, group, s, c0, c1)
                        if part == way:
                            block = block + self.recv_a[way, group, s].astype(jnp.float32)
                        self.send_b[way, group, s, :, pl.ds(part * half, half)] = block.astype(self.low)

            self.seconds.append([
                self.send(self.send_b.at[way, group], self.recv_b.at[way, group], self.to(0, (1, 3)[way]))
                for way in range(2)
            ])

    def arrived(self, n, group, s):
        block = self.term(0, group, s, self.c0, self.c1)
        for way in range(2):
            block = block + self.recv_b[way, group, s].astype(jnp.float32)
        return block

    def third(self):
        self.thirds = []
        for n, group in enumerate(ORDER):
            for copy in self.seconds[n]:
                copy.wait_recv()

            @pl.loop(0, SIDE)
            def _(s):
                block = self.arrived(n, group, s)
                if group:
                    self.send_2[group - 1, s] = block.astype(self.low)
                else:
                    self.total[s] = block

            if group:
                self.thirds.append(self.send(self.send_2.at[group - 1], self.recv_2.at[group - 1], self.to(1, group)))

    def fourth(self):
        for copy in self.thirds:
            copy.wait_recv()
        self.fourths = []
        for by in ORDER:
            s = (self.pos[self.axes[2]] + by) % SIDE
            block = self.total[s]
            for n in range(3):
                block = block + self.recv_2[n, s].astype(jnp.float32)
            if by:
                self.send_3[by - 1] = block.astype(self.low)
                self.fourths.append(self.send(self.send_3.at[by - 1], self.recv_3.at[by - 1], self.to(2, by)))
            else:
                self.mine[...] = block

    def last(self):
        for copy in self.fourths:
            copy.wait_recv()
        block = self.mine[...]
        for n in range(3):
            block = block + self.recv_3[n].astype(jnp.float32)
        self.out[:, pl.ds(self.c0, self.c1 - self.c0)] = block


class SmallReduction(Reduction):
    low = jnp.float32
    COPIES = 1 + 3 + 3 + 3

    def take(self, bufs):
        self.landed, self.send_1, self.recv_1 = bufs

    @classmethod
    def more(cls, half, width):
        return [pltpu.VMEM((SIDE, SIDE, SIDE, 8, width), cls.low)] + [
            pltpu.VMEM((3, SIDE, SIDE, 8, width), cls.low)
        ] * 2

    def open(self, core, both):
        self.source = both.at[core]
        self.opening = self.send(both.at[1 - core], self.landed, {"dp": 1 - core})

    def term(self, *spot):
        kept = self.source
        mine = super().term(*spot)
        self.source = self.landed
        theirs = super().term(*spot)
        self.source = kept
        return mine + theirs

    def first(self):
        self.opening.wait_recv()
        self.seconds = [[]] * SIDE
        copies = []
        for by in (2, 1, 3):
            @pl.loop(0, SIDE)
            def _(s):
                for group in range(SIDE):
                    self.send_1[by - 1, group, s] = self.term(by, group, s, self.c0, self.c1)

            copies.append(self.send(self.send_1.at[by - 1], self.recv_1.at[by - 1], self.to(0, by)))
        self.seconds = [copies] + [[]] * 3

    def arrived(self, n, group, s):
        block = self.term(0, group, s, self.c0, self.c1)
        for way in range(3):
            block = block + self.recv_1[way, group, s]
        return block


SMALL = (2, 0, 128, 256, 2)


ROWS = 512
WIDTH = 1024
HIDDEN = 4096
HALF_IN = WIDTH // 2
HALF_FF = HIDDEN // 2
EXTRA = 128
TILE = 512
N_TILES = HIDDEN // TILE
HALF_TILES = N_TILES // 2
CURVE = 0.7978845608028654


def dot_nt(a, b):
    return lax.dot_general(a, b, (((1,), (1,)), ((), ())), preferred_element_type=jnp.float32)


def dot_nn(a, b):
    return lax.dot_general(a, b, (((1,), (0,)), ((), ())), preferred_element_type=jnp.float32)


def dot_tn(a, b):
    return lax.dot_general(a, b, (((0,), (0,)), ((), ())), preferred_element_type=jnp.float32)


ALL_STEPS = [((2 + n // 16) % 4, (2 + n // 4 % 4) % 4, (2 + n % 4) % 4) for n in range(64)]
STEPS = [steps for steps in ALL_STEPS if sum(steps) % 2] + [steps for steps in ALL_STEPS if sum(steps) % 2 == 0]
OWN = STEPS.index((0, 0, 0))


def ring_places(pos):
    return [[(pos[axis] + step) % 4 * scale for step in range(4)] for axis, scale in enumerate((16, 4, 1))]


def away(places, n, sign):
    return sum(places[axis][sign * step % 4] for axis, step in enumerate(STEPS[n]))


def spread(places, source, target, send_sem, recv_sems):
    for n in range(64):
        if n != OWN:
            d = away(places, n, 1)
            pltpu.make_async_remote_copy(
                src_ref=source.at[d],
                dst_ref=target.at[n],
                send_sem=send_sem,
                recv_sem=recv_sems.at[n // 32],
                device_id={"expert": d},
                device_id_type=MESH,
            ).start()


def bring_back(places, me, source, target, send_sem, recv_sem):
    for n in range(64):
        if n != OWN:
            pltpu.make_async_remote_copy(
                src_ref=source.at[n],
                dst_ref=target.at[me],
                send_sem=send_sem,
                recv_sem=recv_sem,
                device_id={"expert": away(places, n, -1)},
                device_id_type=MESH,
            ).start()


def blocks(ref, count, sem):
    pltpu.make_async_copy(ref.at[pl.ds(0, count)], ref.at[pl.ds(0, count)], sem).wait()


def all_but_one(ref, sem):
    blocks(ref, 63, sem)


def in_turn(count, make, use, first, second):
    make(0, first)

    @pl.loop(0, count // 2 - 1)
    def _(i):
        make(2 * i + 1, second)
        use(2 * i, first)
        make(2 * i + 2, first)
        use(2 * i + 1, second)

    make(count - 1, second)
    use(count - 2, first)
    use(count - 1, second)


def expert_kernel(
    x, r, w1_own, w1_other, w2_own, w2_other,
    y_back, d_back, g1, g2,
    w1, w2, x_in, r_in, xb, xt, act, slope, d_pre, acc, d_exp, out_rows,
    sent1, sent2, got1, got2, stage,
    w_sems, x_sems, r_sems, y_sems, d_sems, own_sems, pass_s, pass_r, out_sems,
):
    pos = coords()
    me = lax.axis_index("expert")
    core = lax.axis_index("dp")
    loads = [
        pltpu.make_async_copy(w1_own, w1.at[core], w_sems.at[0]),
        pltpu.make_async_copy(w1_other, w1.at[1 - core], w_sems.at[1]),
        pltpu.make_async_copy(w2_own, w2.at[core], w_sems.at[2]),
        pltpu.make_async_copy(w2_other, w2.at[1 - core], w_sems.at[3]),
    ]
    barrier = pltpu.get_barrier_semaphore()

    places = ring_places(pos)
    for n in range(64):
        if n != OWN:
            pl.semaphore_signal(barrier, inc=1, device_id={"expert": away(places, n, 1)}, device_id_type=MESH)

    pl.semaphore_signal(barrier, inc=1, device_id={"dp": 1 - core}, device_id_type=MESH)
    own_x = pltpu.make_async_copy(x.at[me], x_in.at[OWN], own_sems.at[0])
    own_r = pltpu.make_async_copy(r.at[me], r_in.at[OWN], own_sems.at[1])
    own_x.start()
    own_r.start()
    for load in loads:
        load.start()
    pl.semaphore_wait(barrier, 64)
    spread(places, x, x_in, x_sems.at[0], x_sems.at[pl.ds(1, 2)])
    spread(places, r, r_in, r_sems.at[0], r_sems.at[pl.ds(1, 2)])
    acc[...] = jnp.zeros_like(acc)
    spare = [stage.at[n] for n in range(2)]
    for part in range(2):
        rows = pl.ds(part * 256, 256)
        if part == 0:
            blocks(x_in, 32, x_sems.at[1])
        else:
            own_x.wait()
            blocks(x_in, 31, x_sems.at[2])

        @pl.loop(0, 4)
        def _(i):
            block = x_in[pl.ds(part * 32 + i * 8, 8)].astype(jnp.float32).reshape(64, WIDTH)
            xb[pl.ds(pl.multiple_of(part * 256 + i * 64, 64), 64), :] = block.astype(jnp.bfloat16)

        if part == 0:
            loads[0].wait()
            loads[1].wait()

        def make(c, to):
            cols = pl.ds(pl.multiple_of(c * TILE, TILE), TILE)
            to[:256, :] = dot_nn(xb[rows, :HALF_IN], w1[0, :, cols]) + dot_nn(xb[rows, HALF_IN:], w1[1, :, cols])

        def use(c, pre_ref):
            cols = pl.ds(pl.multiple_of(c * TILE, TILE), TILE)
            pre = pre_ref[:256, :]
            square = pre * pre
            t = jnp.tanh(CURVE * pre * (1.0 + 0.044715 * square))
            low = (0.5 * pre * (1.0 + t)).astype(jnp.bfloat16)
            act[rows, cols] = low
            slope[rows, cols] = 0.5 * (1.0 + t) + (0.5 * CURVE) * pre * (1.0 - t * t) * (1.0 + (3 * 0.044715) * square)
            half = c // HALF_TILES
            ff = pl.ds(pl.multiple_of((c % HALF_TILES) * TILE, TILE), TILE)
            acc[rows, :] += dot_nn(low, w2[half, ff, :])

        if part == 0:
            loads[2].wait()
            loads[3].wait()
        in_turn(N_TILES, make, use, *spare)

    own_r.wait()
    blocks(r_in, 32, r_sems.at[1])
    blocks(r_in, 31, r_sems.at[2])

    @pl.loop(0, 8)
    def _(i):
        rows = pl.ds(pl.multiple_of(i * 64, 64), 64)
        low = acc[rows, :].astype(jnp.bfloat16)
        out = low.astype(jnp.float32)
        out_rows[pl.ds(i * 8, 8)] = out.reshape(8, 8, WIDTH).astype(jnp.bfloat16)
        parted = r_in[pl.ds(i * 8, 8)].astype(jnp.float32).reshape(64, WIDTH + EXTRA)
        gate = parted[:, WIDTH : WIDTH + 1] + parted[:, WIDTH + 1 : WIDTH + 2]
        valid = parted[:, WIDTH + 2 : WIDTH + 3]
        d_exp[rows, :] = (gate * valid * (parted[:, :WIDTH] + gate * out)).astype(jnp.bfloat16)

    own_y = pltpu.make_async_copy(out_rows.at[OWN], y_back.at[me], own_sems.at[2])
    own_y.start()
    bring_back(places, me, out_rows, y_back, y_sems.at[0], y_sems.at[1])
    acc[...] = jnp.zeros_like(acc)

    def make_back(c, to):
        ff = pl.ds(pl.multiple_of((c % HALF_TILES) * TILE, TILE), TILE)
        to[...] = dot_nt(d_exp[...], w2[c // HALF_TILES, ff, :])

    def use_back(c, d_act):
        cols = pl.ds(pl.multiple_of(c * TILE, TILE), TILE)
        low = (slope[:, cols] * d_act[...]).astype(jnp.bfloat16)
        d_pre[:, cols] = low
        acc[:, :HALF_IN] += dot_nt(low, w1[0, :, cols])
        acc[:, HALF_IN:] += dot_nt(low, w1[1, :, cols])

    in_turn(N_TILES, make_back, use_back, *spare)

    own_y.wait()
    all_but_one(out_rows, y_sems.at[0])

    @pl.loop(0, 8)
    def _(i):
        rows = pl.ds(pl.multiple_of(i * 64, 64), 64)
        out_rows[pl.ds(i * 8, 8)] = acc[rows, :].reshape(8, 8, WIDTH).astype(jnp.bfloat16)

    own_d = pltpu.make_async_copy(out_rows.at[OWN], d_back.at[me], own_sems.at[3])
    own_d.start()
    bring_back(places, me, out_rows, d_back, d_sems.at[0], d_sems.at[1])

    xt[...] = xb[...].astype(jnp.float32).T.astype(jnp.bfloat16)

    def passed(buf, got, c, base):
        return pltpu.make_async_remote_copy(
            src_ref=buf.at[c],
            dst_ref=got.at[c],
            send_sem=pass_s.at[base + c],
            recv_sem=pass_r.at[base + c],
            device_id={"dp": 1 - core},
            device_id_type=MESH,
        )

    def in_rows(half):
        return xt[pl.ds(pl.multiple_of(half * HALF_IN, HALF_IN), HALF_IN), :]

    @pl.loop(0, N_TILES)
    def _(c):
        cols = pl.ds(pl.multiple_of(c * TILE, TILE), TILE)
        sent1[c] = dot_nn(in_rows(1 - core), d_pre[:, cols]).astype(jnp.bfloat16)
        passed(sent1, got1, c, 0).start()

    @pl.loop(0, HALF_TILES)
    def _(c):
        cols = pl.ds(pl.multiple_of((1 - core) * HALF_FF + c * TILE, TILE), TILE)
        sent2[c] = dot_tn(act[:, cols], d_exp[...]).astype(jnp.bfloat16)
        passed(sent2, got2, c, N_TILES).start()

    def made(slot, columns):
        return slope.at[:, pl.ds(pl.multiple_of(slot * WIDTH, WIDTH), columns)]

    def out1(c, slot):
        cols = pl.ds(pl.multiple_of(c * TILE, TILE), TILE)
        return pltpu.make_async_copy(made(slot, TILE), g1.at[:, cols], out_sems.at[slot])

    def out2(c, slot):
        rows = pl.ds(pl.multiple_of(c * TILE, TILE), TILE)
        return pltpu.make_async_copy(made(slot, WIDTH), g2.at[rows, :], out_sems.at[slot])

    @pl.loop(0, N_TILES)
    def _(c):
        slot = c % 2
        cols = pl.ds(pl.multiple_of(c * TILE, TILE), TILE)

        @pl.when(c >= 2)
        def _():
            out1(c - 2, slot).wait()

        passed(sent1, got1, c, 0).wait_recv()
        made(slot, TILE)[...] = dot_nn(in_rows(core), d_pre[:, cols]) + got1[c].astype(jnp.float32)
        out1(c, slot).start()

    out1(N_TILES - 2, 0).wait()
    out1(N_TILES - 1, 1).wait()

    @pl.loop(0, HALF_TILES)
    def _(c):
        slot = c % 2
        cols = pl.ds(pl.multiple_of(core * HALF_FF + c * TILE, TILE), TILE)

        @pl.when(c >= 2)
        def _():
            out2(c - 2, slot).wait()

        passed(sent2, got2, c, N_TILES).wait_recv()
        made(slot, WIDTH)[...] = dot_tn(act[:, cols], d_exp[...]) + got2[c].astype(jnp.float32)
        out2(c, slot).start()

    out2(HALF_TILES - 2, 0).wait()
    out2(HALF_TILES - 1, 1).wait()

    @pl.loop(0, N_TILES)
    def _(c):
        passed(sent1, got1, c, 0).wait_send()

    @pl.loop(0, HALF_TILES)
    def _(c):
        passed(sent2, got2, c, N_TILES).wait_send()

    own_d.wait()
    all_but_one(x_in, x_sems.at[0])
    all_but_one(r_in, r_sems.at[0])
    all_but_one(out_rows, d_sems.at[0])
    all_but_one(out_rows, y_sems.at[1])
    all_but_one(out_rows, d_sems.at[1])


def experts(x, r, w1_own, w1_other, w2_own, w2_other):
    low, wide = jnp.bfloat16, jnp.float32
    anywhere = pl.BlockSpec(memory_space=pl.ANY)
    return pl.pallas_call(
        expert_kernel,
        out_shape=(
            jax.ShapeDtypeStruct((64, 8, WIDTH), low),
            jax.ShapeDtypeStruct((64, 8, WIDTH), low),
            jax.ShapeDtypeStruct((HALF_IN, HIDDEN), wide),
            jax.ShapeDtypeStruct((HALF_FF, WIDTH), wide),
        ),
        in_specs=[anywhere] * 6,
        out_specs=(anywhere,) * 4,
        scratch_shapes=[
            pltpu.VMEM((2, HALF_IN, HIDDEN), low),
            pltpu.VMEM((2, HALF_FF, WIDTH), low),
            pltpu.VMEM((64, 8, WIDTH), low),
            pltpu.VMEM((64, 8, WIDTH + EXTRA), low),
            pltpu.VMEM((ROWS, WIDTH), low),
            pltpu.VMEM((WIDTH, ROWS), low),
            pltpu.VMEM((ROWS, HIDDEN), low),
            pltpu.VMEM((ROWS, HIDDEN), wide),
            pltpu.VMEM((ROWS, HIDDEN), low),
            pltpu.VMEM((ROWS, WIDTH), wide),
            pltpu.VMEM((ROWS, WIDTH), low),
            pltpu.VMEM((64, 8, WIDTH), low),
            pltpu.VMEM((N_TILES, HALF_IN, TILE), low),
            pltpu.VMEM((HALF_TILES, TILE, WIDTH), low),
            pltpu.VMEM((N_TILES, HALF_IN, TILE), low),
            pltpu.VMEM((HALF_TILES, TILE, WIDTH), low),
            pltpu.VMEM((2, ROWS, TILE), wide),
            pltpu.SemaphoreType.DMA((4,)),
            pltpu.SemaphoreType.DMA((3,)),
            pltpu.SemaphoreType.DMA((3,)),
            pltpu.SemaphoreType.DMA((2,)),
            pltpu.SemaphoreType.DMA((2,)),
            pltpu.SemaphoreType.DMA((4,)),
            pltpu.SemaphoreType.DMA((N_TILES + HALF_TILES,)),
            pltpu.SemaphoreType.DMA((N_TILES + HALF_TILES,)),
            pltpu.SemaphoreType.DMA((2,)),
        ],
        compiler_params=pltpu.CompilerParams(
            collective_id=2, has_side_effects=True, vmem_limit_bytes=63 * 1024 * 1024
        ),
        name="experts",
    )(x, r, w1_own, w1_other, w2_own, w2_other)


GROUP = 256
HEADS = 16
PAIRS = HEADS // 2
SLOTS = 512
BLOCK = 32
EPS = 1e-05
MASKED = -1e30


def lanes(start, size):
    return pl.ds(pl.multiple_of(start, 128), size)


def row_blocks(body, size=BLOCK):
    @pl.loop(0, GROUP // size)
    def _(i):
        body(pl.ds(pl.multiple_of(i * size, size), size), i * size)


def normed(v):
    centred = v - jnp.mean(v, -1, keepdims=True)
    inverse = lax.rsqrt(jnp.mean(centred * centred, -1, keepdims=True) + EPS)
    return centred * inverse, inverse


def lane_ids(rows, columns):
    return lax.broadcasted_iota(jnp.int32, (rows, columns), 1)


def row_ids(rows, columns):
    return lax.broadcasted_iota(jnp.int32, (rows, columns), 0)


def allowed_keys(core, length):
    query, key = row_ids(GROUP, GROUP), lane_ids(GROUP, GROUP)
    own = (key <= query) & (key + core * GROUP < length)
    other = (key < length) & (core == 1)
    return own, other


def head_scores(q, k_own, k_other, own, other):
    s_own = jnp.where(own, dot_nt(q, k_own) * 0.125, MASKED)
    s_other = jnp.where(other, dot_nt(q, k_other) * 0.125, MASKED)
    return s_own, s_other


def forward_kernel(
    tokens, teacher, routes_row, lengths, layer,
    x_out, parting_out, qkv_out, kv_other_out, attended_out, norm1_out, norm2_out, residual_out,
    lse_out, probs_out, placing_out, vectors_out,
    weights, norm1, qkv, kv_other, attended, norm2, residual, lse, probs, placing, vectors, parted, packed_x, packed_r,
    load_sems, out_sems, kv_sems,
):
    core = lax.axis_index("dp")
    length = lengths[0]
    spans = ((4096, 128), (1024, 1024), (2048, 1024), (0, 1024), (3072, 1024))
    loads = [
        pltpu.make_async_copy(layer.at[:, pl.ds(c, n)], weights.at[:, pl.ds(c, n)], load_sems.at[i])
        for i, (c, n) in enumerate(spans)
    ]
    for load in loads:
        load.start()
    outs = []

    def save(src, dst):
        copy = pltpu.make_async_copy(src, dst, out_sems.at[len(outs)])
        copy.start()
        outs.append(copy)

    barrier = pltpu.get_barrier_semaphore()
    pl.semaphore_signal(barrier, inc=1, device_id={"dp": 1 - core}, device_id_type=MESH)

    loads[0].wait()
    for g in range(16):
        part = weights[pl.ds(g * 64, 64), pl.ds(4096, 128)].astype(jnp.float32)
        part = jnp.sum(part.reshape(8, 8, 128), 0)
        vectors[:, g * 64 : (g + 1) * 64] = part[:, 64:]
    save(vectors, vectors_out)

    routes = jnp.where(row_ids(GROUP, GROUP) == lane_ids(GROUP, GROUP), routes_row[...], 0)
    route = jnp.sum(routes.astype(jnp.float32), -1, keepdims=True)

    def first_norm(rows, _):
        n, _ = normed(tokens[rows, :].astype(jnp.float32))
        norm1[rows, :] = (n * vectors[0:1, :] + vectors[1:2, :]).astype(jnp.bfloat16)

    row_blocks(first_norm, 64)
    save(norm1, norm1_out)

    def project(block):
        @pl.loop(0, 2)
        def _(i):
            cols = lanes(block * 1024 + i * 512, 512)
            qkv[:, cols] = dot_nn(norm1[...], weights[:, cols]).astype(jnp.bfloat16)

    loads[1].wait()
    project(1)
    loads[2].wait()
    project(2)
    pl.semaphore_wait(barrier, 1)
    passed = pltpu.make_async_remote_copy(
        src_ref=qkv.at[:, pl.ds(1024, 2048)],
        dst_ref=kv_other,
        send_sem=kv_sems.at[0],
        recv_sem=kv_sems.at[1],
        device_id={"dp": 1 - core},
        device_id_type=MESH,
    )
    passed.start()
    loads[3].wait()
    project(0)
    save(qkv, qkv_out)
    passed.wait_recv()
    save(kv_other, kv_other_out)

    own, other = allowed_keys(core, length)
    lse[...] = jnp.zeros_like(lse)

    @pl.loop(0, PAIRS)
    def _(pair):
        q = qkv[:, lanes(pair * 128, 128)]
        k_own, v_own = qkv[:, lanes(1024 + pair * 128, 128)], qkv[:, lanes(2048 + pair * 128, 128)]
        k_other, v_other = kv_other[:, lanes(pair * 128, 128)], kv_other[:, lanes(1024 + pair * 128, 128)]
        left = lane_ids(GROUP, 128) < 64
        results = []
        for h in range(2):
            qh = jnp.where(left == (h == 0), q, jnp.zeros_like(q))
            s_own, s_other = head_scores(qh, k_own, k_other, own, other)
            top = jnp.max(jnp.maximum(s_own, s_other), -1, keepdims=True)
            e_own, e_other = jnp.exp(s_own - top), jnp.exp(s_other - top)
            total = jnp.sum(e_own + e_other, -1, keepdims=True)
            scale = 1.0 / total
            p_own, p_other = (e_own * scale).astype(jnp.bfloat16), (e_other * scale).astype(jnp.bfloat16)
            results.append(dot_nn(p_own, v_own) + dot_nn(p_other, v_other))
            lse[...] = jnp.where(lane_ids(GROUP, 128) == pair * 2 + h, top + jnp.log(total), lse[...])
        attended[:, lanes(pair * 128, 128)] = jnp.where(left, results[0], results[1]).astype(jnp.bfloat16)

    save(attended, attended_out)
    save(lse, lse_out)
    loads[4].wait()

    @pl.loop(0, 2)
    def _(i):
        cols = lanes(i * 512, 512)
        branch = dot_nn(attended[...], weights[:, lanes(3072 + i * 512, 512)])
        residual[:, cols] = tokens[:, cols].astype(jnp.float32) + branch

    save(residual, residual_out)

    def second_norm(rows, _):
        n, _ = normed(residual[rows, :])
        norm2[rows, :] = (n * vectors[2:3, :] + vectors[3:4, :]).astype(jnp.bfloat16)
        parted[rows, :WIDTH] = (residual[rows, :] - teacher[rows, :].astype(jnp.float32)).astype(jnp.bfloat16)

    row_blocks(second_norm, 64)
    save(norm2, norm2_out)
    logits = dot_nn(norm2[...], weights[:, pl.ds(4096, 128)])
    ids = lane_ids(GROUP, 128)
    logits = jnp.where(ids < 64, logits, MASKED)
    e = jnp.exp(logits - jnp.max(logits, -1, keepdims=True))
    share = e / jnp.sum(e, -1, keepdims=True)
    chosen = ids.astype(jnp.float32) == route
    gate = jnp.sum(jnp.where(chosen, share, 0.0), -1, keepdims=True)
    probs[...] = jnp.where(ids == 64, gate, jnp.where(ids == 65, route, share))
    save(probs, probs_out)
    low_gate = gate.astype(jnp.bfloat16).astype(jnp.float32)
    valid = (row_ids(GROUP, 128) + core * GROUP < length).astype(jnp.float32)
    extras = jnp.where(ids == 0, low_gate, jnp.where(ids == 1, gate - low_gate, jnp.where(ids == 2, valid, 0.0)))
    parted[:, WIDTH:] = extras.astype(jnp.bfloat16)
    marks = chosen.astype(jnp.float32).astype(jnp.bfloat16)
    before = (lane_ids(GROUP, GROUP) < row_ids(GROUP, GROUP)).astype(jnp.float32).astype(jnp.bfloat16)
    rank = jnp.sum(jnp.where(chosen, dot_nn(before, marks), 0.0), -1, keepdims=True)
    slot = route * 8.0 + rank
    placing[...] = (lane_ids(GROUP, SLOTS).astype(jnp.float32) == slot).astype(jnp.float32).astype(jnp.bfloat16)
    save(placing, placing_out)
    for half in range(2):
        to_slots = placing[:, half * 256 : (half + 1) * 256].astype(jnp.float32).T.astype(jnp.bfloat16)
        sent = dot_nn(to_slots, norm2[...])
        packed_x[half * 32 : (half + 1) * 32] = sent.reshape(32, 8, WIDTH).astype(jnp.bfloat16)
        sent = dot_nn(to_slots, parted[...])
        packed_r[half * 32 : (half + 1) * 32] = sent.reshape(32, 8, WIDTH + EXTRA).astype(jnp.bfloat16)
    save(packed_x, x_out)
    save(packed_r, parting_out)
    passed.wait_send()
    for copy in outs:
        copy.wait()


def forward(tokens, teacher, routes, lengths, layer):
    low, wide = jnp.bfloat16, jnp.float32
    anywhere = pl.BlockSpec(memory_space=pl.ANY)
    vmem = pl.BlockSpec(memory_space=pltpu.VMEM)
    saved = [
        ((64, 8, WIDTH), low),
        ((64, 8, WIDTH + EXTRA), low),
        ((GROUP, 3 * WIDTH), low),
        ((GROUP, 2 * WIDTH), low),
        ((GROUP, WIDTH), low),
        ((GROUP, WIDTH), low),
        ((GROUP, WIDTH), low),
        ((GROUP, WIDTH), wide),
        ((GROUP, 128), wide),
        ((GROUP, 128), wide),
        ((GROUP, SLOTS), low),
        ((8, WIDTH), wide),
    ]
    return pl.pallas_call(
        forward_kernel,
        out_shape=tuple(jax.ShapeDtypeStruct(s, t) for s, t in saved),
        in_specs=[vmem, vmem, vmem, pl.BlockSpec(memory_space=pltpu.SMEM), anywhere],
        out_specs=(anywhere,) * len(saved),
        scratch_shapes=[
            pltpu.VMEM((WIDTH, AG_COLS), low),
            pltpu.VMEM((GROUP, WIDTH), low),
            pltpu.VMEM((GROUP, 3 * WIDTH), low),
            pltpu.VMEM((GROUP, 2 * WIDTH), low),
            pltpu.VMEM((GROUP, WIDTH), low),
            pltpu.VMEM((GROUP, WIDTH), low),
            pltpu.VMEM((GROUP, WIDTH), wide),
            pltpu.VMEM((GROUP, 128), wide),
            pltpu.VMEM((GROUP, 128), wide),
            pltpu.VMEM((GROUP, SLOTS), low),
            pltpu.VMEM((8, WIDTH), wide),
            pltpu.VMEM((GROUP, WIDTH + EXTRA), low),
            pltpu.VMEM((64, 8, WIDTH), low),
            pltpu.VMEM((64, 8, WIDTH + EXTRA), low),
            pltpu.SemaphoreType.DMA((5,)),
            pltpu.SemaphoreType.DMA((len(saved),)),
            pltpu.SemaphoreType.DMA((2,)),
        ],
        compiler_params=pltpu.CompilerParams(
            collective_id=3, has_side_effects=True, vmem_limit_bytes=56 * 1024 * 1024
        ),
        name="forward",
    )(tokens, teacher, routes, lengths, layer)


def backward_kernel(
    y_back, d_back, teacher_in, lengths, layer, qkv_in, kv_other_in, norm2_in, residual_in, lse_in, probs_in,
    placing_in, vectors_in, g1, g2,
    mixed_to, d_resid_to, dq_to, dkv_own_to, dkv_other_to, d_branch_to, grad_router_to, norm_grads_to, g1_out, g2_out,
    y_in, d_in, teacher, qkv, kv_other, norm2, residual, lse, probs, placing, vectors,
    mixed_out, d_resid, dq, dkv_own, dkv_other, d_branch, grad_router, norm_grads,
    w_out, w_router, eo, dn, sums, d_attended, logit_parts,
    held1, held2, pass_sems, load_sems, out_sems,
):
    core = lax.axis_index("dp")
    length = lengths[0]
    spans = (
        (y_back, y_in),
        (placing_in, placing),
        (d_back, d_in),
        (probs_in, probs),
        (residual_in, residual),
        (teacher_in, teacher),
        (layer.at[:, pl.ds(4096, 128)], w_router),
        (norm2_in, norm2),
        (vectors_in, vectors),
        (layer.at[:, pl.ds(3072, 1024)], w_out),
        (qkv_in, qkv),
        (kv_other_in, kv_other),
        (lse_in, lse),
    )
    loads = [pltpu.make_async_copy(src, dst, load_sems.at[n]) for n, (src, dst) in enumerate(spans)]
    for load in loads:
        load.start()
    passing = [
        pltpu.make_async_copy(g1, held1, pass_sems.at[0]),
        pltpu.make_async_copy(g2, held2, pass_sems.at[1]),
    ]
    passed_on = [
        pltpu.make_async_copy(held1, g1_out, pass_sems.at[2]),
        pltpu.make_async_copy(held2, g2_out, pass_sems.at[3]),
    ]
    outs = []

    def save(src, dst):
        copy = pltpu.make_async_copy(src, dst, out_sems.at[len(outs)])
        copy.start()
        outs.append(copy)

    loads[0].wait()
    loads[1].wait()
    rows_back = y_in[...].astype(jnp.float32).reshape(SLOTS, WIDTH).astype(jnp.bfloat16)
    eo[...] = dot_nn(placing[...], rows_back)
    loads[2].wait()
    rows_back = d_in[...].astype(jnp.float32).reshape(SLOTS, WIDTH).astype(jnp.bfloat16)
    dn[...] = dot_nn(placing[...], rows_back)
    sums[...] = jnp.zeros_like(sums)
    for load in loads[3:6]:
        load.wait()

    def loss(rows, first):
        ids = lane_ids(BLOCK, 128)
        share = probs[rows, :]
        gate = share[:, 64:65]
        chosen = ids.astype(jnp.float32) == share[:, 65:66]
        share = jnp.where(ids < 64, share, 0.0)
        out = eo[rows, :]
        mixed = (residual[rows, :] + gate * out).astype(jnp.bfloat16)
        mixed_out[rows, :] = mixed
        valid = (row_ids(BLOCK, 1) + first + core * GROUP < length).astype(jnp.float32)
        d_mixed = valid * (mixed.astype(jnp.float32) - teacher[rows, :].astype(jnp.float32))
        d_resid[rows, :] = d_mixed
        d_gate = jnp.sum(d_mixed * out, -1, keepdims=True)
        d_logits = d_gate * gate * (chosen.astype(jnp.float32) - share)
        high = d_logits.astype(jnp.bfloat16)
        logit_parts[rows, :128] = high
        logit_parts[rows, 128:] = (d_logits - high.astype(jnp.float32)).astype(jnp.bfloat16)
        square = jnp.sum((d_mixed * d_mixed).reshape(BLOCK // 8, 8, WIDTH), 0)
        sums[0] += square

    row_blocks(loss)
    save(mixed_out, mixed_to)
    for load in loads[6:9]:
        load.wait()
    for copy in passing:
        copy.start()
    dn[...] += dot_nt(logit_parts[:, :128], w_router[...]) + dot_nt(logit_parts[:, 128:], w_router[...])
    both = dot_tn(norm2[...], logit_parts[...])
    grad_router[...] = both[:, :128] + both[:, 128:]

    def norm_back(rows, _):
        n, inverse = normed(residual[rows, :])
        u = dn[rows, :]
        scaled = u * vectors[2:3, :]
        average = jnp.mean(scaled, -1, keepdims=True)
        project = jnp.mean(scaled * n, -1, keepdims=True)
        d = d_resid[rows, :] + inverse * (scaled - average - n * project)
        d_resid[rows, :] = d
        d_branch[rows, :] = d.astype(jnp.bfloat16)
        sums[1] += jnp.sum((u * n).reshape(BLOCK // 8, 8, WIDTH), 0)
        sums[2] += jnp.sum(u.reshape(BLOCK // 8, 8, WIDTH), 0)

    row_blocks(norm_back)
    save(grad_router, grad_router_to)
    save(d_resid, d_resid_to)
    save(d_branch, d_branch_to)
    valid_all = jnp.clip(length - core * GROUP, 0, GROUP).astype(jnp.float32)
    ids = row_ids(8, WIDTH)
    square = jnp.sum(sums[0])
    norm_grads[...] = jnp.where(
        ids == 2,
        jnp.sum(sums[1], 0, keepdims=True),
        jnp.where(
            ids == 3,
            jnp.sum(sums[2], 0, keepdims=True),
            jnp.where(ids == 4, square, jnp.where(ids == 5, valid_all, 0.0)),
        ),
    )
    save(norm_grads, norm_grads_to)
    loads[9].wait()

    @pl.loop(0, 2)
    def _(i):
        cols = lanes(i * 512, 512)
        rows = pl.ds(pl.multiple_of(i * 512, 512), 512)
        d_attended[:, cols] = dot_nt(d_branch[...], w_out[rows, :]).astype(jnp.bfloat16)

    own, other = allowed_keys(core, length)
    for load in loads[10:]:
        load.wait()

    @pl.loop(0, PAIRS)
    def _(pair):
        @pl.when(pair == 3)
        def _():
            for copy, onward in zip(passing, passed_on):
                copy.wait()
                onward.start()

        q, do = qkv[:, lanes(pair * 128, 128)], d_attended[:, lanes(pair * 128, 128)]
        k_own, v_own = qkv[:, lanes(1024 + pair * 128, 128)], qkv[:, lanes(2048 + pair * 128, 128)]
        k_other, v_other = kv_other[:, lanes(pair * 128, 128)], kv_other[:, lanes(1024 + pair * 128, 128)]
        left = lane_ids(GROUP, 128) < 64
        zero = jnp.zeros_like(q)
        parts = []
        for h in range(2):
            qh = jnp.where(left == (h == 0), q, zero)
            doh = jnp.where(left == (h == 0), do, zero)
            s_own, s_other = head_scores(qh, k_own, k_other, own, other)
            log_total = jnp.sum(jnp.where(lane_ids(GROUP, 128) == pair * 2 + h, lse[...], 0.0), -1, keepdims=True)
            p_own, p_other = jnp.exp(s_own - log_total), jnp.exp(s_other - log_total)
            dp_own, dp_other = dot_nt(doh, v_own), dot_nt(doh, v_other)
            total = jnp.sum(p_own * dp_own + p_other * dp_other, -1, keepdims=True)
            ds_own = (p_own * (dp_own - total)).astype(jnp.bfloat16)
            ds_other = (p_other * (dp_other - total)).astype(jnp.bfloat16)
            p_own, p_other = p_own.astype(jnp.bfloat16), p_other.astype(jnp.bfloat16)
            parts.append((
                dot_nn(ds_own, k_own) + dot_nn(ds_other, k_other),
                dot_tn(ds_own, q),
                dot_tn(ds_other, q),
                dot_tn(p_own, do),
                dot_tn(p_other, do),
            ))
        d_q, d_k, d_k_other, d_v, d_v_other = [jnp.where(left, a, b) for a, b in zip(*parts)]
        dq[:, lanes(pair * 128, 128)] = (d_q * 0.125).astype(jnp.bfloat16)
        dkv_own[:, lanes(pair * 128, 128)] = (d_k * 0.125).astype(jnp.bfloat16)
        dkv_own[:, lanes(1024 + pair * 128, 128)] = d_v.astype(jnp.bfloat16)
        dkv_other[:, lanes(pair * 128, 128)] = (d_k_other * 0.125).astype(jnp.bfloat16)
        dkv_other[:, lanes(1024 + pair * 128, 128)] = d_v_other.astype(jnp.bfloat16)

    save(dkv_other, dkv_other_to)
    save(dkv_own, dkv_own_to)
    save(dq, dq_to)
    for copy in passed_on + outs:
        copy.wait()


def backward(y_back, d_back, teacher, lengths, layer, qkv, kv_other, norm2, residual, lse, probs,
             placing, vectors, g1, g2):
    low, wide = jnp.bfloat16, jnp.float32
    anywhere = pl.BlockSpec(memory_space=pl.ANY)
    made = [
        ((GROUP, WIDTH), low),
        ((GROUP, WIDTH), wide),
        ((GROUP, WIDTH), low),
        ((GROUP, 2 * WIDTH), low),
        ((GROUP, 2 * WIDTH), low),
        ((GROUP, WIDTH), low),
        ((WIDTH, 128), wide),
        ((8, WIDTH), wide),
        (g1.shape, wide),
        (g2.shape, wide),
    ]
    return pl.pallas_call(
        backward_kernel,
        out_shape=tuple(jax.ShapeDtypeStruct(s, t) for s, t in made),
        in_specs=[anywhere] * 3 + [pl.BlockSpec(memory_space=pltpu.SMEM)] + [anywhere] * 11,
        out_specs=(anywhere,) * 10,
        scratch_shapes=[
            *[pltpu.VMEM(t.shape, t.dtype) for t in (y_back, d_back, teacher, qkv, kv_other, norm2, residual)],
            *[pltpu.VMEM(t.shape, t.dtype) for t in (lse, probs, placing, vectors)],
            *[pltpu.VMEM(shape, kind) for shape, kind in made[:8]],
            pltpu.VMEM((WIDTH, WIDTH), low),
            pltpu.VMEM((WIDTH, 128), low),
            pltpu.VMEM((GROUP, WIDTH), wide),
            pltpu.VMEM((GROUP, WIDTH), wide),
            pltpu.VMEM((3, 8, WIDTH), wide),
            pltpu.VMEM((GROUP, WIDTH), low),
            pltpu.VMEM((GROUP, 256), low),
            pltpu.VMEM(g1.shape, wide),
            pltpu.VMEM(g2.shape, wide),
            pltpu.SemaphoreType.DMA((4,)),
            pltpu.SemaphoreType.DMA((13,)),
            pltpu.SemaphoreType.DMA((8,)),
        ],
        compiler_params=pltpu.CompilerParams(vmem_limit_bytes=56 * 1024 * 1024),
        name="backward",
    )(y_back, d_back, teacher, lengths, layer, qkv, kv_other, norm2, residual, lse, probs,
      placing, vectors, g1, g2)


HALF = WIDTH // 2


def transposed(block):
    return block.astype(jnp.float32).T.astype(jnp.bfloat16)


def finish_kernel(
    tokens, norm1, attended, vectors, d_resid, dq, dkv_own, dkv_other, d_branch, grad_router, norm_grads, layer,
    sum_qkv, sum_out, sum_side, grad_tokens,
    weights, x, d_res, left, left_t, mine, theirs, got_left, dqkv, d_both, acc, sums, grad_qkv, grad_out,
    router, vec, norms, side, load_sems, *rest,
):
    pos = coords()
    core = lax.axis_index("dp")
    partner = {"dp": 1 - core}
    keep, give = pl.ds(core * HALF, HALF), pl.ds((1 - core) * HALF, HALF)
    own, other = pl.ds(0, GROUP), pl.ds(GROUP, GROUP)
    spans = (
        (norm1.at[:, keep], left.at[0]),
        (attended.at[:, keep], left.at[1]),
        (d_branch, d_both.at[own, :]),
        (layer.at[:, pl.ds(0, 3072)], weights),
        (dq, dqkv.at[own, pl.ds(0, WIDTH)]),
        (dkv_own, mine.at[0]),
        (dkv_other, mine.at[1]),
        (tokens, x),
        (vectors, vec),
        (d_resid, d_res),
        (grad_router, router),
        (norm_grads, norms),
    )
    loads = [pltpu.make_async_copy(src, dst, load_sems.at[n]) for n, (src, dst) in enumerate(spans)]
    for load in loads:
        load.start()
    greet(pos, core)
    send = Sender(*rest[-2:])
    to_left = send(attended.at[:, give], got_left.at[1], partner)
    to_branch = send(d_branch, d_both.at[other, :], partner)
    to_other = send(dkv_other, theirs.at[1], partner)
    to_norm = send(norm1.at[:, give], got_left.at[0], partner)
    to_query = send(dq, dqkv.at[other, pl.ds(0, WIDTH)], partner)
    to_own = send(dkv_own, theirs.at[0], partner)
    bufs, groups = list(rest[:-2]), []
    for piece in RS_PIECES + (SMALL,):
        kind = Reduction if piece is not SMALL else SmallReduction
        count = len(kind.scratch(piece))
        source, out = ((grad_qkv, sum_qkv), (grad_out, sum_out), (side, sum_side))[piece[0]]
        groups.append(kind(piece, pos, send, source, out, bufs[:count]))
        bufs = bufs[count:]
    query, value, branch, small = groups

    loads[0].wait()
    left_t[0, :, own] = transposed(left[0])
    loads[1].wait()
    left_t[1, :, own] = transposed(left[1])
    loads[2].wait()
    to_left.wait_recv()
    left_t[1, :, other] = transposed(got_left[1])
    to_branch.wait_recv()

    @pl.loop(0, 2)
    def _(i):
        cols = lanes(i * 512, 512)
        grad_out[:, :, :, :, cols] = dot_nn(left_t[1], d_both[:, cols]).reshape(SIDE, SIDE, SIDE, 8, 512)

    branch.first()
    loads[3].wait()
    loads[4].wait()
    acc[...] = jnp.zeros_like(acc)

    def back(first, count):
        @pl.loop(0, count)
        def _(i):
            cols = lanes(first + i * 512, 512)
            acc[...] += dot_nt(dqkv[own, cols], weights[:, cols])

    def grads(first, count):
        @pl.loop(0, count)
        def _(i):
            cols = lanes(first + i * 512, 512)
            grad_qkv[:, :, :, :, cols] = dot_nn(left_t[0], dqkv[:, cols]).reshape(SIDE, SIDE, SIDE, 8, 512)

    back(0, 2)
    loads[5].wait()
    loads[6].wait()
    to_other.wait_recv()

    def join(first, a, b):
        def add(rows, start):
            spot = pl.ds(pl.multiple_of(first + start, BLOCK), BLOCK)
            dqkv[spot, pl.ds(WIDTH, 2 * WIDTH)] = (
                a[rows, :].astype(jnp.float32) + b[rows, :].astype(jnp.float32)
            ).astype(jnp.bfloat16)

        row_blocks(add)

    join(0, mine.at[0], theirs.at[1])
    to_norm.wait_recv()
    left_t[0, :, other] = transposed(got_left[0])
    to_query.wait_recv()
    to_own.wait_recv()
    join(GROUP, theirs.at[0], mine.at[1])
    grads(0, 3)
    query.first()
    branch.second()
    grads(1536, 3)
    value.first()
    back(1024, 4)
    query.second()
    for load in loads[7:]:
        load.wait()
    sums[...] = jnp.zeros_like(sums)

    def norm_back(rows, _):
        n, inverse = normed(x[rows, :].astype(jnp.float32))
        u = acc[rows, :]
        scaled = u * vec[0:1, :]
        average = jnp.mean(scaled, -1, keepdims=True)
        project = jnp.mean(scaled * n, -1, keepdims=True)
        grad_tokens[rows, :] = d_res[rows, :] + inverse * (scaled - average - n * project)
        sums[0] += jnp.sum((u * n).reshape(BLOCK // 8, 8, WIDTH), 0)
        sums[1] += jnp.sum(u.reshape(BLOCK // 8, 8, WIDTH), 0)

    row_blocks(norm_back)
    ids = row_ids(8, WIDTH)
    vector_grads = jnp.where(
        ids == 0,
        jnp.sum(sums[0], 0, keepdims=True),
        jnp.where(ids == 1, jnp.sum(sums[1], 0, keepdims=True), norms[...]),
    )
    for half in range(2):
        rows = router[half * 512 : (half + 1) * 512, :]
        side[half, :, :, :, :, pl.ds(0, 128)] = rows.reshape(SIDE, SIDE, SIDE, 8, 128)
        for at in range(SIDE):
            block = vector_grads[:, (half * SIDE + at) * 128 : (half * SIDE + at + 1) * 128]
            side[half, at, :, :, :, pl.ds(128, 128)] = jnp.broadcast_to(block[None, None], (SIDE, SIDE, 8, 128))
    small.open(core, side)
    value.second()
    branch.third()
    small.first()
    query.third()
    value.third()
    small.third()
    branch.fourth()
    query.fourth()
    value.fourth()
    small.fourth()
    branch.last()
    query.last()
    value.last()
    small.last()
    send.close()


def finish(tokens, norm1, attended, vectors, d_resid, dq, dkv_own, dkv_other, d_branch, grad_router, norm_grads,
           layer):
    low, wide = jnp.bfloat16, jnp.float32
    anywhere = pl.BlockSpec(memory_space=pl.ANY)
    vmem = pl.BlockSpec(memory_space=pltpu.VMEM)
    lead = (SIDE, SIDE, SIDE, 8)
    scratch, copies = SmallReduction.scratch(SMALL), 6 + SmallReduction.COPIES
    for piece in RS_PIECES[::-1]:
        scratch, copies = Reduction.scratch(piece) + scratch, copies + Reduction.COPIES
    return pl.pallas_call(
        finish_kernel,
        out_shape=tuple(jax.ShapeDtypeStruct((8, c), wide) for c in RS_COLS)
        + (jax.ShapeDtypeStruct((GROUP, WIDTH), wide),),
        in_specs=[anywhere] * 12,
        out_specs=(vmem,) * 4,
        scratch_shapes=[
            pltpu.VMEM((WIDTH, 3 * WIDTH), low),
            pltpu.VMEM((GROUP, WIDTH), low),
            pltpu.VMEM((GROUP, WIDTH), wide),
            pltpu.VMEM((2, GROUP, HALF), low),
            pltpu.VMEM((2, HALF, 2 * GROUP), low),
            pltpu.VMEM((2, GROUP, 2 * WIDTH), low),
            pltpu.VMEM((2, GROUP, 2 * WIDTH), low),
            pltpu.VMEM((2, GROUP, HALF), low),
            pltpu.VMEM((2 * GROUP, 3 * WIDTH), low),
            pltpu.VMEM((2 * GROUP, WIDTH), low),
            pltpu.VMEM((GROUP, WIDTH), wide),
            pltpu.VMEM((2, 8, WIDTH), wide),
            pltpu.VMEM(lead + (3 * WIDTH,), wide),
            pltpu.VMEM(lead + (WIDTH,), wide),
            pltpu.VMEM((WIDTH, 128), wide),
            pltpu.VMEM((8, WIDTH), wide),
            pltpu.VMEM((8, WIDTH), wide),
            pltpu.VMEM((2,) + lead + (256,), wide),
            pltpu.SemaphoreType.DMA((12,)),
            *scratch,
            pltpu.SemaphoreType.DMA((copies,)),
            pltpu.SemaphoreType.DMA((copies,)),
        ],
        compiler_params=pltpu.CompilerParams(
            collective_id=1, has_side_effects=True, vmem_limit_bytes=60 * 1024 * 1024
        ),
        name="finish",
    )(tokens, norm1, attended, vectors, d_resid, dq, dkv_own, dkv_other, d_branch, grad_router, norm_grads, layer)


def results_kernel(sum_qkv, sum_out, side, given_tokens, qkv, out, router, vectors, loss, tokens):
    place = (lax.axis_index("dp") * 64 + lax.axis_index("expert")) % 16
    qkv[...] = sum_qkv[...]
    out[...] = sum_out[...]
    tokens[...] = given_tokens[...]
    router[...] = side[:, :64]
    sums = side[:, 128:256]
    vectors[...] = pltpu.roll(sums, (16 - place) * 8 % 128, 1)
    loss[...] = sums[4:5, 0:1] / (sums[5:6, 0:1] * WIDTH)


def results(*sums):
    wide = jnp.float32
    shapes = ((8, 3072), (8, 1024), (8, 64), (8, 128), (1, 1), (GROUP, WIDTH))
    vmem = pl.BlockSpec(memory_space=pltpu.VMEM)
    return pl.pallas_call(
        results_kernel,
        out_shape=tuple(jax.ShapeDtypeStruct(s, wide) for s in shapes),
        in_specs=[vmem] * 4,
        out_specs=(vmem,) * 6,
        name="results",
    )(*sums)


def per_device(
    tokens,
    teacher,
    lengths,
    routes,
    ln1_gain,
    ln1_bias,
    query_key_value_weight,
    output_weight,
    ln2_gain,
    ln2_bias,
    router_weight,
    w_in,
    w_down,
):
    device = lax.axis_index("dp") * 64 + lax.axis_index("expert")
    vectors = jnp.tile(jnp.stack([ln1_gain, ln1_bias, ln2_gain, ln2_bias] * 2).astype(jnp.float32), (1, 8))
    vectors = jnp.where(jnp.arange(64)[None, :] // 8 == device % 8, vectors, 0)
    layer, in_other, down_other = gather_layer(
        query_key_value_weight, output_weight, router_weight, vectors, w_in[0], w_down[0]
    )
    x, parting, qkv, kv_other, attended, norm1, norm2, residual, lse, probs, placing, vectors = forward(
        tokens[0], teacher[0], routes.reshape(1, GROUP), lengths, layer
    )
    y_back, d_back, g1, g2 = experts(x, parting, w_in[0], in_other, w_down[0], down_other)
    mixed, d_resid, dq, dkv_own, dkv_other, d_branch, grad_router, norm_grads, g1, g2 = backward(
        y_back, d_back, teacher[0], lengths, layer, qkv, kv_other, norm2, residual, lse, probs, placing, vectors,
        g1, g2,
    )
    sums = finish(
        tokens[0], norm1, attended, vectors, d_resid, dq, dkv_own, dkv_other, d_branch, grad_router, norm_grads,
        layer,
    )
    grad_qkv, grad_out, grad_router, vector_grads, loss_value, grad_tokens = results(*sums)
    return (
        mixed[None],
        loss_value[0, 0],
        grad_tokens[None],
        vector_grads[0, :8],
        vector_grads[1, :8],
        grad_qkv,
        grad_out,
        vector_grads[2, :8],
        vector_grads[3, :8],
        grad_router,
        g1[None],
        g2[None],
    )


def solution(mesh):
    placed = (
        P("expert", "dp", None),
        P("expert", "dp", None),
        P("expert"),
        P("expert", "dp", None),
        P(("dp", "expert")),
        P(("dp", "expert")),
        P(("dp", "expert"), None),
        P(("dp", "expert"), None),
        P(("dp", "expert")),
        P(("dp", "expert")),
        P(("dp", "expert"), None),
        P("expert", "dp", None),
        P("expert", "dp", None),
    )
    return jax.shard_map(
        per_device,
        mesh=mesh,
        in_specs=placed,
        out_specs=(
            P("expert", "dp", None),
            P(),
            P("expert", "dp", None),
            P(("dp", "expert")),
            P(("dp", "expert")),
            P(("dp", "expert"), None),
            P(("dp", "expert"), None),
            P(("dp", "expert")),
            P(("dp", "expert")),
            P(("dp", "expert"), None),
            P("expert", "dp", None),
            P("expert", "dp", None),
        ),
        check_vma=False,
    )
```

```python
import jax
import jax.numpy as jnp
from jax import lax
from jax.experimental import pallas as pl
from jax.experimental.pallas import tpu as pltpu
from jax.sharding import PartitionSpec as P

MESH = pl.DeviceIdType.MESH
SIDE = 4
FULL = slice(None)

AG_COLS = 4224
AG_PIECES = ((0, 768, 1408), (1408, 2176, 2816), (2816, 3584, 4224))


def coords():
    e = lax.axis_index("expert")
    return [e // 16, (e // 4) % 4, e % 4]


def shifted(pos, axis, by):
    out = list(pos)
    out[axis] = (pos[axis] + by) % SIDE
    return out


def chip(pos):
    return {"expert": pos[0] * 16 + pos[1] * 4 + pos[2]}


def greet(pos, core):
    barrier = pltpu.get_barrier_semaphore()
    for axis in range(3):
        for by in range(1, SIDE):
            pl.semaphore_signal(barrier, inc=1, device_id=chip(shifted(pos, axis, by)), device_id_type=MESH)
    pl.semaphore_signal(barrier, inc=1, device_id={"dp": 1 - core}, device_id_type=MESH)
    pl.semaphore_wait(barrier, 10)


class Sender:
    def __init__(self, send_sems, recv_sems):
        self.send_sems, self.recv_sems, self.count, self.sent = send_sems, recv_sems, 0, []

    def __call__(self, src, dst, device):
        copy = pltpu.make_async_remote_copy(
            src_ref=src,
            dst_ref=dst,
            send_sem=self.send_sems.at[self.count],
            recv_sem=self.recv_sems.at[self.count],
            device_id=device,
            device_id_type=MESH,
        )
        copy.start()
        self.count += 1
        self.sent.append(copy)
        return copy

    def close(self):
        for copy in self.sent:
            copy.wait_send()


def gather_kernel(
    q, o, r, gain_one, bias_one, gain_two, bias_two, w_in, w_down, whole, in_other, down_other, shard, own_sem, send_sems, recv_sems
):
    pos = coords()
    core = lax.axis_index("dp")
    partner = {"dp": 1 - core}
    shard[:, :3072] = q[...]
    shard[:, 3072:4096] = o[...]
    lane = lax.broadcasted_iota(jnp.int32, (8, 64), 1)
    row = lax.broadcasted_iota(jnp.int32, (8, 64), 0)
    here = (lane == row + lax.axis_index("expert") % 8 * 8).astype(jnp.float32)
    vectors = jnp.zeros((8, 64), jnp.float32)
    same = (lax.broadcasted_iota(jnp.int32, (8, 8), 0) == lax.broadcasted_iota(jnp.int32, (8, 8), 1)).astype(jnp.float32)
    for n, vector in enumerate((gain_one, bias_one, gain_two, bias_two)):
        column = jnp.sum(same * vector[...].astype(jnp.float32), 1, keepdims=True)
        spread_out = jnp.sum(here * column, 0, keepdims=True)
        vectors = jnp.where(row == n, spread_out, vectors)
    shard[:, 4096:] = jnp.concatenate([r[...].astype(jnp.float32), vectors], 1).astype(jnp.bfloat16)
    own = pltpu.make_async_copy(shard, whole.at[(core, *pos)], own_sem)
    own.start()
    greet(pos, core)
    send = Sender(send_sems, recv_sems)

    def share(region, c0, c1, device):
        spot = whole.at[(core, *region, FULL, pl.ds(c0, c1 - c0))]
        return send(spot, spot, device)

    plans = []
    for piece, (c0, mid, c1) in enumerate(AG_PIECES):
        axes = [(piece + step) % 3 for step in range(3)]
        spot = whole.at[(core, *pos, FULL, pl.ds(c0, c1 - c0))]
        first = [send(shard.at[:, pl.ds(c0, c1 - c0)], spot, chip(shifted(pos, axes[0], by))) for by in (1, 3, 2)]
        plans.append((axes, c0, mid, c1, first))
    across = [send(w_in, in_other, partner), send(w_down, down_other, partner)]
    own.wait()

    def line(axes, second, third):
        region = [None] * 3
        region[axes[0]], region[axes[1]], region[axes[2]] = FULL, second, third
        return region

    def at(axis, by):
        return (pos[axis] + by) % SIDE

    seconds, lines = [], [{} for _ in plans]

    def onward(piece, by):
        axes, c0, mid, c1, _ = plans[piece]
        region = line(axes, at(axes[1], by), pos[axes[2]])
        lines[piece][by] = (
            share(region, c0, c1, chip(shifted(pos, axes[2], 1))),
            share(region, c0, c1, chip(shifted(pos, axes[2], 3))),
        )
        across.append(share(region, c0, c1, partner))

    def relay(piece, by):
        axes, c0, mid, c1, _ = plans[piece]
        up, down = lines[piece][by]
        up.wait_recv()
        below = line(axes, at(axes[1], by), at(axes[2], 3))
        on_up = share(below, c0, mid, chip(shifted(pos, axes[2], 1)))
        down.wait_recv()
        above = line(axes, at(axes[1], by), at(axes[2], 1))
        on_down = share(above, mid, c1, chip(shifted(pos, axes[2], 3)))
        across.append(share(below, c0, c1, partner))
        across.append(share(above, c0, c1, partner))
        lines[piece][by] = (on_up, on_down)

    def end(piece, by):
        axes, c0, mid, c1, _ = plans[piece]
        for copy in lines[piece][by]:
            copy.wait_recv()
        across.append(share(line(axes, at(axes[1], by), at(axes[2], 2)), c0, c1, partner))

    for piece, (axes, c0, mid, c1, first) in enumerate(plans):
        for copy in first:
            copy.wait_recv()
        region = line(axes, pos[axes[1]], pos[axes[2]])
        seconds.append([share(region, c0, c1, chip(shifted(pos, axes[1], by))) for by in (1, 3, 2)])
        onward(piece, 0)
    for n, by in enumerate((3, 1)):
        for piece in range(3):
            seconds[piece][n].wait_recv()
            onward(piece, by)
    for piece in range(3):
        relay(piece, 0)
    for piece in range(3):
        seconds[piece][2].wait_recv()
        onward(piece, 2)
    for by in (3, 1, 2):
        for piece in range(3):
            relay(piece, by)
    for by in (0, 3, 1, 2):
        for piece in range(3):
            end(piece, by)
    for copy in across:
        copy.wait_recv()
    send.close()


def gather_layer(q, o, r, vectors, w_in, w_down):
    copies = 3 * (3 + 3 + 4 * 4 + 4 * 4) + 2
    anywhere, vmem = pl.BlockSpec(memory_space=pl.ANY), pl.BlockSpec(memory_space=pltpu.VMEM)
    whole, in_other, down_other = pl.pallas_call(
        gather_kernel,
        out_shape=(
            jax.ShapeDtypeStruct((2, SIDE, SIDE, SIDE, 8, AG_COLS), jnp.bfloat16),
            jax.ShapeDtypeStruct(w_in.shape, w_in.dtype),
            jax.ShapeDtypeStruct(w_down.shape, w_down.dtype),
        ),
        in_specs=[vmem] * 7 + [anywhere] * 2,
        out_specs=(anywhere,) * 3,
        scratch_shapes=[
            pltpu.VMEM((8, AG_COLS), jnp.bfloat16),
            pltpu.SemaphoreType.DMA,
            pltpu.SemaphoreType.DMA((copies,)),
            pltpu.SemaphoreType.DMA((copies,)),
        ],
        compiler_params=pltpu.CompilerParams(collective_id=0, has_side_effects=True),
        name="gather_layer",
    )(q, o, r, *vectors, w_in, w_down)
    return whole.reshape(1024, AG_COLS), in_other, down_other


RS_COLS = (3072, 1024, 256)
RS_PIECES = ((0, 0, 768, 1536, 0), (0, 1536, 2304, 3072, 1), (1, 0, 512, 1024, 2))
ORDER = (2, 1, 3, 0)


class Reduction:
    low = jnp.bfloat16
    COPIES = 8 + 8 + 3 + 3

    def __init__(self, piece, pos, send, source, out, bufs):
        _, self.c0, self.mid, self.c1, first = piece
        self.axes = [(first + step) % 3 for step in range(3)]
        self.pos, self.send, self.source, self.out = pos, send, source, out
        (self.total, self.send_2, self.recv_2, self.mine, self.send_3, self.recv_3) = bufs[:6]
        self.take(bufs[6:])

    def take(self, bufs):
        self.send_a, self.recv_a, self.send_b, self.recv_b = bufs

    @classmethod
    def scratch(cls, piece):
        _, c0, mid, c1, _ = piece
        width, low, wide = c1 - c0, cls.low, jnp.float32
        return [
            pltpu.VMEM((SIDE, 8, width), wide),
            pltpu.VMEM((3, SIDE, 8, width), low),
            pltpu.VMEM((3, SIDE, 8, width), low),
            pltpu.VMEM((8, width), wide),
            pltpu.VMEM((3, 8, width), low),
            pltpu.VMEM((3, 8, width), low),
        ] + cls.more(mid - c0, width)

    @classmethod
    def more(cls, half, width):
        return [pltpu.VMEM((2, SIDE, SIDE, 8, half), cls.low)] * 2 + [pltpu.VMEM((2, SIDE, SIDE, 8, width), cls.low)] * 2

    def to(self, step, by):
        return chip(shifted(self.pos, self.axes[step], by))

    def term(self, first, second, third, c0, c1):
        spot = [None] * 3
        spot[self.axes[0]] = (self.pos[self.axes[0]] + first) % SIDE
        spot[self.axes[1]] = (self.pos[self.axes[1]] + second) % SIDE
        spot[self.axes[2]] = third
        return self.source[(*spot, FULL, pl.ds(c0, c1 - c0))]

    def first(self):
        self.firsts = []
        for group in ORDER:
            @pl.loop(0, SIDE)
            def _(s):
                self.send_a[0, group, s] = self.term(2, group, s, self.c0, self.mid).astype(self.low)
                self.send_a[1, group, s] = self.term(2, group, s, self.mid, self.c1).astype(self.low)

            self.firsts.append([
                self.send(self.send_a.at[way, group], self.recv_a.at[way, group], self.to(0, (1, 3)[way]))
                for way in range(2)
            ])

    def second(self):
        self.seconds = []
        half = self.mid - self.c0
        for n, group in enumerate(ORDER):
            for copy in self.firsts[n]:
                copy.wait_recv()

            @pl.loop(0, SIDE)
            def _(s):
                for way, by in enumerate((1, 3)):
                    for part, (c0, c1) in enumerate(((self.c0, self.mid), (self.mid, self.c1))):
                        block = self.term(by, group, s, c0, c1)
                        if part == way:
                            block = block + self.recv_a[way, group, s].astype(jnp.float32)
                        self.send_b[way, group, s, :, pl.ds(part * half, half)] = block.astype(self.low)

            self.seconds.append([
                self.send(self.send_b.at[way, group], self.recv_b.at[way, group], self.to(0, (1, 3)[way]))
                for way in range(2)
            ])

    def arrived(self, n, group, s):
        block = self.term(0, group, s, self.c0, self.c1)
        for way in range(2):
            block = block + self.recv_b[way, group, s].astype(jnp.float32)
        return block

    def third(self):
        self.thirds = []
        for n, group in enumerate(ORDER):
            for copy in self.seconds[n]:
                copy.wait_recv()

            @pl.loop(0, SIDE)
            def _(s):
                block = self.arrived(n, group, s)
                if group:
                    self.send_2[group - 1, s] = block.astype(self.low)
                else:
                    self.total[s] = block

            if group:
                self.thirds.append(self.send(self.send_2.at[group - 1], self.recv_2.at[group - 1], self.to(1, group)))

    def fourth(self):
        for copy in self.thirds:
            copy.wait_recv()
        self.fourths = []
        for by in ORDER:
            s = (self.pos[self.axes[2]] + by) % SIDE
            block = self.total[s]
            for n in range(3):
                block = block + self.recv_2[n, s].astype(jnp.float32)
            if by:
                self.send_3[by - 1] = block.astype(self.low)
                self.fourths.append(self.send(self.send_3.at[by - 1], self.recv_3.at[by - 1], self.to(2, by)))
            else:
                self.mine[...] = block

    def last(self):
        for copy in self.fourths:
            copy.wait_recv()
        block = self.mine[...]
        for n in range(3):
            block = block + self.recv_3[n].astype(jnp.float32)
        self.out[:, pl.ds(self.c0, self.c1 - self.c0)] = block


class SmallReduction(Reduction):
    low = jnp.float32
    COPIES = 1 + 3 + 3 + 3

    def take(self, bufs):
        self.landed, self.send_1, self.recv_1 = bufs

    @classmethod
    def more(cls, half, width):
        return [pltpu.VMEM((SIDE, SIDE, SIDE, 8, width), cls.low)] + [
            pltpu.VMEM((3, SIDE, SIDE, 8, width), cls.low)
        ] * 2

    def open(self, core, both):
        self.source = both.at[core]
        self.opening = self.send(both.at[1 - core], self.landed, {"dp": 1 - core})

    def term(self, *spot):
        kept = self.source
        mine = super().term(*spot)
        self.source = self.landed
        theirs = super().term(*spot)
        self.source = kept
        return mine + theirs

    def first(self):
        self.opening.wait_recv()
        self.seconds = [[]] * SIDE
        copies = []
        for by in (2, 1, 3):
            @pl.loop(0, SIDE)
            def _(s):
                for group in range(SIDE):
                    self.send_1[by - 1, group, s] = self.term(by, group, s, self.c0, self.c1)

            copies.append(self.send(self.send_1.at[by - 1], self.recv_1.at[by - 1], self.to(0, by)))
        self.seconds = [copies] + [[]] * 3

    def arrived(self, n, group, s):
        block = self.term(0, group, s, self.c0, self.c1)
        for way in range(3):
            block = block + self.recv_1[way, group, s]
        return block


SMALL = (2, 0, 128, 256, 2)


ROWS = 512
WIDTH = 1024
HIDDEN = 4096
HALF_IN = WIDTH // 2
HALF_FF = HIDDEN // 2
EXTRA = 128
TILE = 512
N_TILES = HIDDEN // TILE
HALF_TILES = N_TILES // 2
CURVE = 0.7978845608028654


def dot_nt(a, b):
    return lax.dot_general(a, b, (((1,), (1,)), ((), ())), preferred_element_type=jnp.float32)


def dot_nn(a, b):
    return lax.dot_general(a, b, (((1,), (0,)), ((), ())), preferred_element_type=jnp.float32)


def dot_tn(a, b):
    return lax.dot_general(a, b, (((0,), (0,)), ((), ())), preferred_element_type=jnp.float32)


ALL_STEPS = [((2 + n // 16) % 4, (2 + n // 4 % 4) % 4, (2 + n % 4) % 4) for n in range(64)]
STEPS = [steps for steps in ALL_STEPS if sum(steps) % 2] + [steps for steps in ALL_STEPS if sum(steps) % 2 == 0]
OWN = STEPS.index((0, 0, 0))


def ring_places(pos):
    return [[(pos[axis] + step) % 4 * scale for step in range(4)] for axis, scale in enumerate((16, 4, 1))]


def away(places, n, sign):
    return sum(places[axis][sign * step % 4] for axis, step in enumerate(STEPS[n]))


def spread(places, source, target, send_sem, recv_sems):
    for n in range(64):
        if n != OWN:
            d = away(places, n, 1)
            pltpu.make_async_remote_copy(
                src_ref=source.at[d],
                dst_ref=target.at[n],
                send_sem=send_sem,
                recv_sem=recv_sems.at[n // 32],
                device_id={"expert": d},
                device_id_type=MESH,
            ).start()


def bring_back(places, me, source, target, send_sem, recv_sem):
    for n in range(64):
        if n != OWN:
            pltpu.make_async_remote_copy(
                src_ref=source.at[n],
                dst_ref=target.at[me],
                send_sem=send_sem,
                recv_sem=recv_sem,
                device_id={"expert": away(places, n, -1)},
                device_id_type=MESH,
            ).start()


def blocks(ref, count, sem):
    pltpu.make_async_copy(ref.at[pl.ds(0, count)], ref.at[pl.ds(0, count)], sem).wait()


def all_but_one(ref, sem):
    blocks(ref, 63, sem)


def in_turn(count, make, use, first, second):
    make(0, first)

    @pl.loop(0, count // 2 - 1)
    def _(i):
        make(2 * i + 1, second)
        use(2 * i, first)
        make(2 * i + 2, first)
        use(2 * i + 1, second)

    make(count - 1, second)
    use(count - 2, first)
    use(count - 1, second)


def expert_kernel(
    x, r, w1_own, w1_other, w2_own, w2_other,
    y_back, d_back, g1, g2,
    w1, w2, x_in, r_in, xb, xt, act, slope, d_pre, acc, d_exp, out_rows,
    sent1, sent2, got1, got2, stage,
    w_sems, x_sems, r_sems, y_sems, d_sems, own_sems, pass_s, pass_r, out_sems,
):
    pos = coords()
    me = lax.axis_index("expert")
    core = lax.axis_index("dp")
    loads = [
        pltpu.make_async_copy(w1_own, w1.at[core], w_sems.at[0]),
        pltpu.make_async_copy(w1_other, w1.at[1 - core], w_sems.at[1]),
        pltpu.make_async_copy(w2_own, w2.at[core], w_sems.at[2]),
        pltpu.make_async_copy(w2_other, w2.at[1 - core], w_sems.at[3]),
    ]
    barrier = pltpu.get_barrier_semaphore()

    places = ring_places(pos)
    for n in range(64):
        if n != OWN:
            pl.semaphore_signal(barrier, inc=1, device_id={"expert": away(places, n, 1)}, device_id_type=MESH)

    pl.semaphore_signal(barrier, inc=1, device_id={"dp": 1 - core}, device_id_type=MESH)
    own_x = pltpu.make_async_copy(x.at[me], x_in.at[OWN], own_sems.at[0])
    own_r = pltpu.make_async_copy(r.at[me], r_in.at[OWN], own_sems.at[1])
    own_x.start()
    own_r.start()
    for load in loads:
        load.start()
    pl.semaphore_wait(barrier, 64)
    spread(places, x, x_in, x_sems.at[0], x_sems.at[pl.ds(1, 2)])
    spread(places, r, r_in, r_sems.at[0], r_sems.at[pl.ds(1, 2)])
    acc[...] = jnp.zeros_like(acc)
    spare = [stage.at[n] for n in range(2)]
    for part in range(2):
        rows = pl.ds(part * 256, 256)
        if part == 0:
            blocks(x_in, 32, x_sems.at[1])
        else:
            own_x.wait()
            blocks(x_in, 31, x_sems.at[2])

        @pl.loop(0, 4)
        def _(i):
            block = x_in[pl.ds(part * 32 + i * 8, 8)].astype(jnp.float32).reshape(64, WIDTH)
            xb[pl.ds(pl.multiple_of(part * 256 + i * 64, 64), 64), :] = block.astype(jnp.bfloat16)

        if part == 0:
            loads[0].wait()
            loads[1].wait()

        def make(c, to):
            cols = pl.ds(pl.multiple_of(c * TILE, TILE), TILE)
            to[:256, :] = dot_nn(xb[rows, :HALF_IN], w1[0, :, cols]) + dot_nn(xb[rows, HALF_IN:], w1[1, :, cols])

        def use(c, pre_ref):
            cols = pl.ds(pl.multiple_of(c * TILE, TILE), TILE)
            pre = pre_ref[:256, :]
            square = pre * pre
            t = jnp.tanh(CURVE * pre * (1.0 + 0.044715 * square))
            low = (0.5 * pre * (1.0 + t)).astype(jnp.bfloat16)
            act[rows, cols] = low
            slope[rows, cols] = 0.5 * (1.0 + t) + (0.5 * CURVE) * pre * (1.0 - t * t) * (1.0 + (3 * 0.044715) * square)
            half = c // HALF_TILES
            ff = pl.ds(pl.multiple_of((c % HALF_TILES) * TILE, TILE), TILE)
            acc[rows, :] += dot_nn(low, w2[half, ff, :])

        if part == 0:
            loads[2].wait()
            loads[3].wait()
        in_turn(N_TILES, make, use, *spare)

    own_r.wait()
    blocks(r_in, 32, r_sems.at[1])
    blocks(r_in, 31, r_sems.at[2])

    @pl.loop(0, 8)
    def _(i):
        rows = pl.ds(pl.multiple_of(i * 64, 64), 64)
        low = acc[rows, :].astype(jnp.bfloat16)
        out = low.astype(jnp.float32)
        out_rows[pl.ds(i * 8, 8)] = out.reshape(8, 8, WIDTH).astype(jnp.bfloat16)
        parted = r_in[pl.ds(i * 8, 8)].astype(jnp.float32).reshape(64, WIDTH + EXTRA)
        gate = parted[:, WIDTH : WIDTH + 1] + parted[:, WIDTH + 1 : WIDTH + 2]
        valid = parted[:, WIDTH + 2 : WIDTH + 3]
        d_exp[rows, :] = (gate * valid * (parted[:, :WIDTH] + gate * out)).astype(jnp.bfloat16)

    own_y = pltpu.make_async_copy(out_rows.at[OWN], y_back.at[me], own_sems.at[2])
    own_y.start()
    bring_back(places, me, out_rows, y_back, y_sems.at[0], y_sems.at[1])
    acc[...] = jnp.zeros_like(acc)

    def make_back(c, to):
        ff = pl.ds(pl.multiple_of((c % HALF_TILES) * TILE, TILE), TILE)
        to[...] = dot_nt(d_exp[...], w2[c // HALF_TILES, ff, :])

    def use_back(c, d_act):
        cols = pl.ds(pl.multiple_of(c * TILE, TILE), TILE)
        low = (slope[:, cols] * d_act[...]).astype(jnp.bfloat16)
        d_pre[:, cols] = low
        acc[:, :HALF_IN] += dot_nt(low, w1[0, :, cols])
        acc[:, HALF_IN:] += dot_nt(low, w1[1, :, cols])

    in_turn(N_TILES, make_back, use_back, *spare)

    own_y.wait()
    all_but_one(out_rows, y_sems.at[0])

    @pl.loop(0, 8)
    def _(i):
        rows = pl.ds(pl.multiple_of(i * 64, 64), 64)
        out_rows[pl.ds(i * 8, 8)] = acc[rows, :].reshape(8, 8, WIDTH).astype(jnp.bfloat16)

    own_d = pltpu.make_async_copy(out_rows.at[OWN], d_back.at[me], own_sems.at[3])
    own_d.start()
    bring_back(places, me, out_rows, d_back, d_sems.at[0], d_sems.at[1])

    xt[...] = xb[...].astype(jnp.float32).T.astype(jnp.bfloat16)

    def passed(buf, got, c, base):
        return pltpu.make_async_remote_copy(
            src_ref=buf.at[c],
            dst_ref=got.at[c],
            send_sem=pass_s.at[base + c],
            recv_sem=pass_r.at[base + c],
            device_id={"dp": 1 - core},
            device_id_type=MESH,
        )

    def in_rows(half):
        return xt[pl.ds(pl.multiple_of(half * HALF_IN, HALF_IN), HALF_IN), :]

    @pl.loop(0, N_TILES)
    def _(c):
        cols = pl.ds(pl.multiple_of(c * TILE, TILE), TILE)
        sent1[c] = dot_nn(in_rows(1 - core), d_pre[:, cols]).astype(jnp.bfloat16)
        passed(sent1, got1, c, 0).start()

    @pl.loop(0, HALF_TILES)
    def _(c):
        cols = pl.ds(pl.multiple_of((1 - core) * HALF_FF + c * TILE, TILE), TILE)
        sent2[c] = dot_tn(act[:, cols], d_exp[...]).astype(jnp.bfloat16)
        passed(sent2, got2, c, N_TILES).start()

    def made(slot, columns):
        return slope.at[:, pl.ds(pl.multiple_of(slot * WIDTH, WIDTH), columns)]

    def out1(c, slot):
        cols = pl.ds(pl.multiple_of(c * TILE, TILE), TILE)
        return pltpu.make_async_copy(made(slot, TILE), g1.at[:, cols], out_sems.at[slot])

    def out2(c, slot):
        rows = pl.ds(pl.multiple_of(c * TILE, TILE), TILE)
        return pltpu.make_async_copy(made(slot, WIDTH), g2.at[rows, :], out_sems.at[slot])

    @pl.loop(0, N_TILES)
    def _(c):
        slot = c % 2
        cols = pl.ds(pl.multiple_of(c * TILE, TILE), TILE)

        @pl.when(c >= 2)
        def _():
            out1(c - 2, slot).wait()

        passed(sent1, got1, c, 0).wait_recv()
        made(slot, TILE)[...] = dot_nn(in_rows(core), d_pre[:, cols]) + got1[c].astype(jnp.float32)
        out1(c, slot).start()

    out1(N_TILES - 2, 0).wait()
    out1(N_TILES - 1, 1).wait()

    @pl.loop(0, HALF_TILES)
    def _(c):
        slot = c % 2
        cols = pl.ds(pl.multiple_of(core * HALF_FF + c * TILE, TILE), TILE)

        @pl.when(c >= 2)
        def _():
            out2(c - 2, slot).wait()

        passed(sent2, got2, c, N_TILES).wait_recv()
        made(slot, WIDTH)[...] = dot_tn(act[:, cols], d_exp[...]) + got2[c].astype(jnp.float32)
        out2(c, slot).start()

    out2(HALF_TILES - 2, 0).wait()
    out2(HALF_TILES - 1, 1).wait()

    @pl.loop(0, N_TILES)
    def _(c):
        passed(sent1, got1, c, 0).wait_send()

    @pl.loop(0, HALF_TILES)
    def _(c):
        passed(sent2, got2, c, N_TILES).wait_send()

    own_d.wait()
    all_but_one(x_in, x_sems.at[0])
    all_but_one(r_in, r_sems.at[0])
    all_but_one(out_rows, d_sems.at[0])
    all_but_one(out_rows, y_sems.at[1])
    all_but_one(out_rows, d_sems.at[1])


def experts(x, r, w1_own, w1_other, w2_own, w2_other):
    low, wide = jnp.bfloat16, jnp.float32
    anywhere = pl.BlockSpec(memory_space=pl.ANY)
    return pl.pallas_call(
        expert_kernel,
        out_shape=(
            jax.ShapeDtypeStruct((64, 8, WIDTH), low),
            jax.ShapeDtypeStruct((64, 8, WIDTH), low),
            jax.ShapeDtypeStruct((HALF_IN, HIDDEN), wide),
            jax.ShapeDtypeStruct((HALF_FF, WIDTH), wide),
        ),
        in_specs=[anywhere] * 6,
        out_specs=(anywhere,) * 4,
        scratch_shapes=[
            pltpu.VMEM((2, HALF_IN, HIDDEN), low),
            pltpu.VMEM((2, HALF_FF, WIDTH), low),
            pltpu.VMEM((64, 8, WIDTH), low),
            pltpu.VMEM((64, 8, WIDTH + EXTRA), low),
            pltpu.VMEM((ROWS, WIDTH), low),
            pltpu.VMEM((WIDTH, ROWS), low),
            pltpu.VMEM((ROWS, HIDDEN), low),
            pltpu.VMEM((ROWS, HIDDEN), wide),
            pltpu.VMEM((ROWS, HIDDEN), low),
            pltpu.VMEM((ROWS, WIDTH), wide),
            pltpu.VMEM((ROWS, WIDTH), low),
            pltpu.VMEM((64, 8, WIDTH), low),
            pltpu.VMEM((N_TILES, HALF_IN, TILE), low),
            pltpu.VMEM((HALF_TILES, TILE, WIDTH), low),
            pltpu.VMEM((N_TILES, HALF_IN, TILE), low),
            pltpu.VMEM((HALF_TILES, TILE, WIDTH), low),
            pltpu.VMEM((2, ROWS, TILE), wide),
            pltpu.SemaphoreType.DMA((4,)),
            pltpu.SemaphoreType.DMA((3,)),
            pltpu.SemaphoreType.DMA((3,)),
            pltpu.SemaphoreType.DMA((2,)),
            pltpu.SemaphoreType.DMA((2,)),
            pltpu.SemaphoreType.DMA((4,)),
            pltpu.SemaphoreType.DMA((N_TILES + HALF_TILES,)),
            pltpu.SemaphoreType.DMA((N_TILES + HALF_TILES,)),
            pltpu.SemaphoreType.DMA((2,)),
        ],
        compiler_params=pltpu.CompilerParams(
            collective_id=2, has_side_effects=True, vmem_limit_bytes=63 * 1024 * 1024
        ),
        name="experts",
    )(x, r, w1_own, w1_other, w2_own, w2_other)


GROUP = 256
HEADS = 16
PAIRS = HEADS // 2
SLOTS = 512
BLOCK = 32
EPS = 1e-05
MASKED = -1e30


def lanes(start, size):
    return pl.ds(pl.multiple_of(start, 128), size)


def row_blocks(body, size=BLOCK):
    @pl.loop(0, GROUP // size)
    def _(i):
        body(pl.ds(pl.multiple_of(i * size, size), size), i * size)


def normed(v):
    centred = v - jnp.mean(v, -1, keepdims=True)
    inverse = lax.rsqrt(jnp.mean(centred * centred, -1, keepdims=True) + EPS)
    return centred * inverse, inverse


def lane_ids(rows, columns):
    return lax.broadcasted_iota(jnp.int32, (rows, columns), 1)


def row_ids(rows, columns):
    return lax.broadcasted_iota(jnp.int32, (rows, columns), 0)


def allowed_keys(core, length):
    query, key = row_ids(GROUP, GROUP), lane_ids(GROUP, GROUP)
    own = (key <= query) & (key + core * GROUP < length)
    other = (key < length) & (core == 1)
    return own, other


def head_scores(q, k_own, k_other, own, other):
    s_own = jnp.where(own, dot_nt(q, k_own), MASKED)
    s_other = jnp.where(other, dot_nt(q, k_other), MASKED)
    return s_own, s_other


def forward_kernel(
    tokens, teacher, routes_row, lengths, layer,
    x_out, parting_out, qkv_out, kv_other_out, attended_out, norm1_out, norm2_out, residual_out,
    lse_out, probs_out, placing_out, vectors_out,
    weights, norm1, qkv, kv_other, attended, norm2, residual, lse, probs, placing, vectors, parted, packed_x, packed_r,
    load_sems, out_sems, kv_sems,
):
    core = lax.axis_index("dp")
    length = lengths[0]
    spans = ((4096, 128), (1024, 1024), (2048, 1024), (0, 1024), (3072, 1024))
    loads = [
        pltpu.make_async_copy(layer.at[:, pl.ds(c, n)], weights.at[:, pl.ds(c, n)], load_sems.at[i])
        for i, (c, n) in enumerate(spans)
    ]
    for load in loads:
        load.start()
    outs = []

    def save(src, dst):
        copy = pltpu.make_async_copy(src, dst, out_sems.at[len(outs)])
        copy.start()
        outs.append(copy)

    barrier = pltpu.get_barrier_semaphore()
    pl.semaphore_signal(barrier, inc=1, device_id={"dp": 1 - core}, device_id_type=MESH)

    def statistics(rows, _):
        n, _ = normed(tokens[rows, :].astype(jnp.float32))
        residual[rows, :] = n

    row_blocks(statistics, 64)
    loads[0].wait()
    for g in range(16):
        part = weights[pl.ds(g * 64, 64), pl.ds(4096, 128)].astype(jnp.float32)
        part = jnp.sum(part.reshape(8, 8, 128), 0)
        vectors[:, g * 64 : (g + 1) * 64] = part[:, 64:]
    save(vectors, vectors_out)

    routes = jnp.where(row_ids(GROUP, GROUP) == lane_ids(GROUP, GROUP), routes_row[...], 0)
    route = jnp.sum(routes.astype(jnp.float32), -1, keepdims=True)

    def first_norm(rows, _):
        norm1[rows, :] = (residual[rows, :] * vectors[0:1, :] + vectors[1:2, :]).astype(jnp.bfloat16)

    row_blocks(first_norm, 64)
    save(norm1, norm1_out)

    def project(block):
        @pl.loop(0, 2)
        def _(i):
            cols = lanes(block * 1024 + i * 512, 512)
            qkv[:, cols] = dot_nn(norm1[...], weights[:, cols]).astype(jnp.bfloat16)

    loads[1].wait()
    project(1)
    loads[2].wait()
    project(2)
    pl.semaphore_wait(barrier, 1)
    passed = pltpu.make_async_remote_copy(
        src_ref=qkv.at[:, pl.ds(1024, 2048)],
        dst_ref=kv_other,
        send_sem=kv_sems.at[0],
        recv_sem=kv_sems.at[1],
        device_id={"dp": 1 - core},
        device_id_type=MESH,
    )
    passed.start()
    loads[3].wait()
    project(0)
    save(qkv, qkv_out)
    passed.wait_recv()
    save(kv_other, kv_other_out)

    own, other = allowed_keys(core, length)
    lse[...] = jnp.zeros_like(lse)

    @pl.loop(0, PAIRS)
    def _(pair):
        q = qkv[:, lanes(pair * 128, 128)] * 0.125
        k_own, v_own = qkv[:, lanes(1024 + pair * 128, 128)], qkv[:, lanes(2048 + pair * 128, 128)]
        k_other, v_other = kv_other[:, lanes(pair * 128, 128)], kv_other[:, lanes(1024 + pair * 128, 128)]
        left = lane_ids(GROUP, 128) < 64
        results = []
        for h in range(2):
            qh = jnp.where(left == (h == 0), q, jnp.zeros_like(q))
            s_own, s_other = head_scores(qh, k_own, k_other, own, other)
            top = jnp.max(jnp.maximum(s_own, s_other), -1, keepdims=True)
            e_own, e_other = jnp.exp(s_own - top), jnp.exp(s_other - top)
            total = jnp.sum(e_own + e_other, -1, keepdims=True)
            e_own, e_other = e_own.astype(jnp.bfloat16), e_other.astype(jnp.bfloat16)
            results.append((dot_nn(e_own, v_own) + dot_nn(e_other, v_other)) * (1.0 / total))
            lse[...] = jnp.where(lane_ids(GROUP, 128) == pair * 2 + h, top + jnp.log(total), lse[...])
        attended[:, lanes(pair * 128, 128)] = jnp.where(left, results[0], results[1]).astype(jnp.bfloat16)

    save(attended, attended_out)
    save(lse, lse_out)
    loads[4].wait()

    @pl.loop(0, 2)
    def _(i):
        cols = lanes(i * 512, 512)
        branch = dot_nn(attended[...], weights[:, lanes(3072 + i * 512, 512)])
        residual[:, cols] = tokens[:, cols].astype(jnp.float32) + branch

    save(residual, residual_out)

    def second_norm(rows, _):
        n, _ = normed(residual[rows, :])
        norm2[rows, :] = (n * vectors[2:3, :] + vectors[3:4, :]).astype(jnp.bfloat16)
        parted[rows, :WIDTH] = (residual[rows, :] - teacher[rows, :].astype(jnp.float32)).astype(jnp.bfloat16)

    row_blocks(second_norm, 64)
    save(norm2, norm2_out)
    logits = dot_nn(norm2[...], weights[:, pl.ds(4096, 128)])
    ids = lane_ids(GROUP, 128)
    logits = jnp.where(ids < 64, logits, MASKED)
    e = jnp.exp(logits - jnp.max(logits, -1, keepdims=True))
    share = e / jnp.sum(e, -1, keepdims=True)
    chosen = ids.astype(jnp.float32) == route
    gate = jnp.sum(jnp.where(chosen, share, 0.0), -1, keepdims=True)
    probs[...] = jnp.where(ids == 64, gate, jnp.where(ids == 65, route, share))
    save(probs, probs_out)
    low_gate = gate.astype(jnp.bfloat16).astype(jnp.float32)
    valid = (row_ids(GROUP, 128) + core * GROUP < length).astype(jnp.float32)
    extras = jnp.where(ids == 0, low_gate, jnp.where(ids == 1, gate - low_gate, jnp.where(ids == 2, valid, 0.0)))
    parted[:, WIDTH:] = extras.astype(jnp.bfloat16)
    marks = chosen.astype(jnp.float32).astype(jnp.bfloat16)
    before = (lane_ids(GROUP, GROUP) < row_ids(GROUP, GROUP)).astype(jnp.float32).astype(jnp.bfloat16)
    rank = jnp.sum(jnp.where(chosen, dot_nn(before, marks), 0.0), -1, keepdims=True)
    slot = route * 8.0 + rank
    placing[...] = (lane_ids(GROUP, SLOTS).astype(jnp.float32) == slot).astype(jnp.float32).astype(jnp.bfloat16)
    save(placing, placing_out)
    for half in range(2):
        to_slots = placing[:, half * 256 : (half + 1) * 256].astype(jnp.float32).T.astype(jnp.bfloat16)
        sent = dot_nn(to_slots, norm2[...])
        packed_x[half * 32 : (half + 1) * 32] = sent.reshape(32, 8, WIDTH).astype(jnp.bfloat16)
        sent = dot_nn(to_slots, parted[...])
        packed_r[half * 32 : (half + 1) * 32] = sent.reshape(32, 8, WIDTH + EXTRA).astype(jnp.bfloat16)
    save(packed_x, x_out)
    save(packed_r, parting_out)
    passed.wait_send()
    for copy in outs:
        copy.wait()


def forward(tokens, teacher, routes, lengths, layer):
    low, wide = jnp.bfloat16, jnp.float32
    anywhere = pl.BlockSpec(memory_space=pl.ANY)
    vmem = pl.BlockSpec(memory_space=pltpu.VMEM)
    saved = [
        ((64, 8, WIDTH), low),
        ((64, 8, WIDTH + EXTRA), low),
        ((GROUP, 3 * WIDTH), low),
        ((GROUP, 2 * WIDTH), low),
        ((GROUP, WIDTH), low),
        ((GROUP, WIDTH), low),
        ((GROUP, WIDTH), low),
        ((GROUP, WIDTH), wide),
        ((GROUP, 128), wide),
        ((GROUP, 128), wide),
        ((GROUP, SLOTS), low),
        ((8, WIDTH), wide),
    ]
    return pl.pallas_call(
        forward_kernel,
        out_shape=tuple(jax.ShapeDtypeStruct(s, t) for s, t in saved),
        in_specs=[vmem, vmem, vmem, pl.BlockSpec(memory_space=pltpu.SMEM), anywhere],
        out_specs=(anywhere,) * len(saved),
        scratch_shapes=[
            pltpu.VMEM((WIDTH, AG_COLS), low),
            pltpu.VMEM((GROUP, WIDTH), low),
            pltpu.VMEM((GROUP, 3 * WIDTH), low),
            pltpu.VMEM((GROUP, 2 * WIDTH), low),
            pltpu.VMEM((GROUP, WIDTH), low),
            pltpu.VMEM((GROUP, WIDTH), low),
            pltpu.VMEM((GROUP, WIDTH), wide),
            pltpu.VMEM((GROUP, 128), wide),
            pltpu.VMEM((GROUP, 128), wide),
            pltpu.VMEM((GROUP, SLOTS), low),
            pltpu.VMEM((8, WIDTH), wide),
            pltpu.VMEM((GROUP, WIDTH + EXTRA), low),
            pltpu.VMEM((64, 8, WIDTH), low),
            pltpu.VMEM((64, 8, WIDTH + EXTRA), low),
            pltpu.SemaphoreType.DMA((5,)),
            pltpu.SemaphoreType.DMA((len(saved),)),
            pltpu.SemaphoreType.DMA((2,)),
        ],
        compiler_params=pltpu.CompilerParams(
            collective_id=3, has_side_effects=True, vmem_limit_bytes=56 * 1024 * 1024
        ),
        name="forward",
    )(tokens, teacher, routes, lengths, layer)


def backward_kernel(
    y_back, d_back, teacher_in, lengths, layer, qkv_in, kv_other_in, norm2_in, residual_in, lse_in, probs_in,
    placing_in, vectors_in, g1, g2,
    mixed_to, d_resid_to, dq_to, dkv_own_to, dkv_other_to, d_branch_to, grad_router_to, norm_grads_to, g1_out, g2_out,
    y_in, d_in, teacher, qkv, kv_other, norm2, residual, lse, probs, placing, vectors,
    mixed_out, d_resid, dq, dkv_own, dkv_other, d_branch, grad_router, norm_grads,
    w_out, w_router, eo, dn, sums, d_attended, logit_parts,
    held1, held2, pass_sems, load_sems, out_sems,
):
    core = lax.axis_index("dp")
    length = lengths[0]
    spans = (
        (y_back, y_in),
        (placing_in, placing),
        (d_back, d_in),
        (probs_in, probs),
        (residual_in, residual),
        (teacher_in, teacher),
        (layer.at[:, pl.ds(4096, 128)], w_router),
        (norm2_in, norm2),
        (vectors_in, vectors),
        (layer.at[:, pl.ds(3072, 1024)], w_out),
        (qkv_in, qkv),
        (kv_other_in, kv_other),
        (lse_in, lse),
    )
    loads = [pltpu.make_async_copy(src, dst, load_sems.at[n]) for n, (src, dst) in enumerate(spans)]
    for load in loads:
        load.start()
    passing = [
        pltpu.make_async_copy(g1, held1, pass_sems.at[0]),
        pltpu.make_async_copy(g2, held2, pass_sems.at[1]),
    ]
    passed_on = [
        pltpu.make_async_copy(held1, g1_out, pass_sems.at[2]),
        pltpu.make_async_copy(held2, g2_out, pass_sems.at[3]),
    ]
    outs = []

    def save(src, dst):
        copy = pltpu.make_async_copy(src, dst, out_sems.at[len(outs)])
        copy.start()
        outs.append(copy)

    loads[0].wait()
    loads[1].wait()
    rows_back = y_in[...].astype(jnp.float32).reshape(SLOTS, WIDTH).astype(jnp.bfloat16)
    eo[...] = dot_nn(placing[...], rows_back)
    loads[2].wait()
    rows_back = d_in[...].astype(jnp.float32).reshape(SLOTS, WIDTH).astype(jnp.bfloat16)
    dn[...] = dot_nn(placing[...], rows_back)
    sums[...] = jnp.zeros_like(sums)
    for load in loads[3:6]:
        load.wait()

    def loss(rows, first):
        ids = lane_ids(BLOCK, 128)
        share = probs[rows, :]
        gate = share[:, 64:65]
        chosen = ids.astype(jnp.float32) == share[:, 65:66]
        share = jnp.where(ids < 64, share, 0.0)
        out = eo[rows, :]
        mixed = (residual[rows, :] + gate * out).astype(jnp.bfloat16)
        mixed_out[rows, :] = mixed
        valid = (row_ids(BLOCK, 1) + first + core * GROUP < length).astype(jnp.float32)
        d_mixed = valid * (mixed.astype(jnp.float32) - teacher[rows, :].astype(jnp.float32))
        d_resid[rows, :] = d_mixed
        d_gate = jnp.sum(d_mixed * out, -1, keepdims=True)
        d_logits = d_gate * gate * (chosen.astype(jnp.float32) - share)
        high = d_logits.astype(jnp.bfloat16)
        logit_parts[rows, :128] = high
        logit_parts[rows, 128:] = (d_logits - high.astype(jnp.float32)).astype(jnp.bfloat16)
        square = jnp.sum((d_mixed * d_mixed).reshape(BLOCK // 8, 8, WIDTH), 0)
        sums[0] += square

    row_blocks(loss)
    save(mixed_out, mixed_to)
    for load in loads[6:9]:
        load.wait()
    for copy in passing:
        copy.start()
    dn[...] += dot_nt(logit_parts[:, :128], w_router[...]) + dot_nt(logit_parts[:, 128:], w_router[...])
    both = dot_tn(norm2[...], logit_parts[...])
    grad_router[...] = both[:, :128] + both[:, 128:]

    def norm_back(rows, _):
        n, inverse = normed(residual[rows, :])
        u = dn[rows, :]
        scaled = u * vectors[2:3, :]
        average = jnp.mean(scaled, -1, keepdims=True)
        project = jnp.mean(scaled * n, -1, keepdims=True)
        d = d_resid[rows, :] + inverse * (scaled - average - n * project)
        d_resid[rows, :] = d
        d_branch[rows, :] = d.astype(jnp.bfloat16)
        sums[1] += jnp.sum((u * n).reshape(BLOCK // 8, 8, WIDTH), 0)
        sums[2] += jnp.sum(u.reshape(BLOCK // 8, 8, WIDTH), 0)

    row_blocks(norm_back)
    save(grad_router, grad_router_to)
    save(d_resid, d_resid_to)
    save(d_branch, d_branch_to)
    valid_all = jnp.clip(length - core * GROUP, 0, GROUP).astype(jnp.float32)
    ids = row_ids(8, WIDTH)
    square = jnp.sum(sums[0])
    norm_grads[...] = jnp.where(
        ids == 2,
        jnp.sum(sums[1], 0, keepdims=True),
        jnp.where(
            ids == 3,
            jnp.sum(sums[2], 0, keepdims=True),
            jnp.where(ids == 4, square, jnp.where(ids == 5, valid_all, 0.0)),
        ),
    )
    save(norm_grads, norm_grads_to)
    loads[9].wait()

    @pl.loop(0, 2)
    def _(i):
        cols = lanes(i * 512, 512)
        rows = pl.ds(pl.multiple_of(i * 512, 512), 512)
        d_attended[:, cols] = dot_nt(d_branch[...], w_out[rows, :]).astype(jnp.bfloat16)

    own, other = allowed_keys(core, length)
    for load in loads[10:]:
        load.wait()

    @pl.loop(0, PAIRS)
    def _(pair):
        @pl.when(pair == 3)
        def _():
            for copy, onward in zip(passing, passed_on):
                copy.wait()
                onward.start()

        q, do = qkv[:, lanes(pair * 128, 128)], d_attended[:, lanes(pair * 128, 128)]
        k_own, v_own = qkv[:, lanes(1024 + pair * 128, 128)], qkv[:, lanes(2048 + pair * 128, 128)]
        k_other, v_other = kv_other[:, lanes(pair * 128, 128)], kv_other[:, lanes(1024 + pair * 128, 128)]
        left = lane_ids(GROUP, 128) < 64
        zero = jnp.zeros_like(q)
        parts = []
        for h in range(2):
            qh = jnp.where(left == (h == 0), q * 0.125, zero)
            doh = jnp.where(left == (h == 0), do, zero)
            s_own, s_other = head_scores(qh, k_own, k_other, own, other)
            log_total = jnp.sum(jnp.where(lane_ids(GROUP, 128) == pair * 2 + h, lse[...], 0.0), -1, keepdims=True)
            p_own, p_other = jnp.exp(s_own - log_total), jnp.exp(s_other - log_total)
            dp_own, dp_other = dot_nt(doh, v_own), dot_nt(doh, v_other)
            total = jnp.sum(p_own * dp_own + p_other * dp_other, -1, keepdims=True)
            ds_own = (p_own * (dp_own - total)).astype(jnp.bfloat16)
            ds_other = (p_other * (dp_other - total)).astype(jnp.bfloat16)
            p_own, p_other = p_own.astype(jnp.bfloat16), p_other.astype(jnp.bfloat16)
            parts.append((
                dot_nn(ds_own, k_own) + dot_nn(ds_other, k_other),
                dot_tn(ds_own, q),
                dot_tn(ds_other, q),
                dot_tn(p_own, do),
                dot_tn(p_other, do),
            ))
        d_q, d_k, d_k_other, d_v, d_v_other = [jnp.where(left, a, b) for a, b in zip(*parts)]
        dq[:, lanes(pair * 128, 128)] = (d_q * 0.125).astype(jnp.bfloat16)
        dkv_own[:, lanes(pair * 128, 128)] = (d_k * 0.125).astype(jnp.bfloat16)
        dkv_own[:, lanes(1024 + pair * 128, 128)] = d_v.astype(jnp.bfloat16)
        dkv_other[:, lanes(pair * 128, 128)] = (d_k_other * 0.125).astype(jnp.bfloat16)
        dkv_other[:, lanes(1024 + pair * 128, 128)] = d_v_other.astype(jnp.bfloat16)

    save(dkv_other, dkv_other_to)
    save(dkv_own, dkv_own_to)
    save(dq, dq_to)
    for copy in passed_on + outs:
        copy.wait()


def backward(y_back, d_back, teacher, lengths, layer, qkv, kv_other, norm2, residual, lse, probs,
             placing, vectors, g1, g2):
    low, wide = jnp.bfloat16, jnp.float32
    anywhere = pl.BlockSpec(memory_space=pl.ANY)
    made = [
        ((GROUP, WIDTH), low),
        ((GROUP, WIDTH), wide),
        ((GROUP, WIDTH), low),
        ((GROUP, 2 * WIDTH), low),
        ((GROUP, 2 * WIDTH), low),
        ((GROUP, WIDTH), low),
        ((WIDTH, 128), wide),
        ((8, WIDTH), wide),
        (g1.shape, wide),
        (g2.shape, wide),
    ]
    return pl.pallas_call(
        backward_kernel,
        out_shape=tuple(jax.ShapeDtypeStruct(s, t) for s, t in made),
        in_specs=[anywhere] * 3 + [pl.BlockSpec(memory_space=pltpu.SMEM)] + [anywhere] * 11,
        out_specs=(anywhere,) * 10,
        scratch_shapes=[
            *[pltpu.VMEM(t.shape, t.dtype) for t in (y_back, d_back, teacher, qkv, kv_other, norm2, residual)],
            *[pltpu.VMEM(t.shape, t.dtype) for t in (lse, probs, placing, vectors)],
            *[pltpu.VMEM(shape, kind) for shape, kind in made[:8]],
            pltpu.VMEM((WIDTH, WIDTH), low),
            pltpu.VMEM((WIDTH, 128), low),
            pltpu.VMEM((GROUP, WIDTH), wide),
            pltpu.VMEM((GROUP, WIDTH), wide),
            pltpu.VMEM((3, 8, WIDTH), wide),
            pltpu.VMEM((GROUP, WIDTH), low),
            pltpu.VMEM((GROUP, 256), low),
            pltpu.VMEM(g1.shape, wide),
            pltpu.VMEM(g2.shape, wide),
            pltpu.SemaphoreType.DMA((4,)),
            pltpu.SemaphoreType.DMA((13,)),
            pltpu.SemaphoreType.DMA((8,)),
        ],
        compiler_params=pltpu.CompilerParams(vmem_limit_bytes=56 * 1024 * 1024),
        name="backward",
    )(y_back, d_back, teacher, lengths, layer, qkv, kv_other, norm2, residual, lse, probs,
      placing, vectors, g1, g2)


HALF = WIDTH // 2


def transposed(block):
    return block.astype(jnp.float32).T.astype(jnp.bfloat16)


def finish_kernel(
    tokens, norm1, attended, vectors, d_resid, dq, dkv_own, dkv_other, d_branch, grad_router, norm_grads, layer,
    sum_qkv, sum_out, sum_side, grad_tokens,
    weights, x, d_res, left, left_t, mine, theirs, got_left, dqkv, d_both, acc, sums, grad_qkv, grad_out,
    router, vec, norms, side, load_sems, *rest,
):
    pos = coords()
    core = lax.axis_index("dp")
    partner = {"dp": 1 - core}
    keep, give = pl.ds(core * HALF, HALF), pl.ds((1 - core) * HALF, HALF)
    own, other = pl.ds(0, GROUP), pl.ds(GROUP, GROUP)
    spans = (
        (norm1.at[:, keep], left.at[0]),
        (attended.at[:, keep], left.at[1]),
        (d_branch, d_both.at[own, :]),
        (layer.at[:, pl.ds(0, 3072)], weights),
        (dq, dqkv.at[own, pl.ds(0, WIDTH)]),
        (dkv_own, mine.at[0]),
        (dkv_other, mine.at[1]),
        (tokens, x),
        (vectors, vec),
        (d_resid, d_res),
        (grad_router, router),
        (norm_grads, norms),
    )
    loads = [pltpu.make_async_copy(src, dst, load_sems.at[n]) for n, (src, dst) in enumerate(spans)]
    for load in loads:
        load.start()
    greet(pos, core)
    send = Sender(*rest[-2:])
    to_left = send(attended.at[:, give], got_left.at[1], partner)
    to_branch = send(d_branch, d_both.at[other, :], partner)
    to_norm = send(norm1.at[:, give], got_left.at[0], partner)
    to_query = send(dq, dqkv.at[other, pl.ds(0, WIDTH)], partner)
    to_other = send(dkv_other, theirs.at[1], partner)
    to_own = send(dkv_own, theirs.at[0], partner)
    bufs, groups = list(rest[:-2]), []
    for piece in RS_PIECES + (SMALL,):
        kind = Reduction if piece is not SMALL else SmallReduction
        count = len(kind.scratch(piece))
        source, out = ((grad_qkv, sum_qkv), (grad_out, sum_out), (side, sum_side))[piece[0]]
        groups.append(kind(piece, pos, send, source, out, bufs[:count]))
        bufs = bufs[count:]
    query, value, branch, small = groups

    loads[0].wait()
    left_t[0, :, own] = transposed(left[0])
    loads[1].wait()
    left_t[1, :, own] = transposed(left[1])
    loads[2].wait()
    to_left.wait_recv()
    left_t[1, :, other] = transposed(got_left[1])
    to_branch.wait_recv()

    @pl.loop(0, 2)
    def _(i):
        cols = lanes(i * 512, 512)
        grad_out[:, :, :, :, cols] = dot_nn(left_t[1], d_both[:, cols]).reshape(SIDE, SIDE, SIDE, 8, 512)

    branch.first()
    loads[3].wait()
    loads[4].wait()
    acc[...] = jnp.zeros_like(acc)

    def back(first, count):
        @pl.loop(0, count)
        def _(i):
            cols = lanes(first + i * 512, 512)
            acc[...] += dot_nt(dqkv[own, cols], weights[:, cols])

    def grads(first, count):
        @pl.loop(0, count)
        def _(i):
            cols = lanes(first + i * 512, 512)
            grad_qkv[:, :, :, :, cols] = dot_nn(left_t[0], dqkv[:, cols]).reshape(SIDE, SIDE, SIDE, 8, 512)

    loads[5].wait()
    loads[6].wait()

    def join(first, a, b):
        def add(rows, start):
            spot = pl.ds(pl.multiple_of(first + start, BLOCK), BLOCK)
            dqkv[spot, pl.ds(WIDTH, 2 * WIDTH)] = (
                a[rows, :].astype(jnp.float32) + b[rows, :].astype(jnp.float32)
            ).astype(jnp.bfloat16)

        row_blocks(add)

    to_norm.wait_recv()
    left_t[0, :, other] = transposed(got_left[0])
    to_query.wait_recv()
    to_other.wait_recv()
    join(0, mine.at[0], theirs.at[1])
    to_own.wait_recv()
    join(GROUP, theirs.at[0], mine.at[1])
    grads(0, 3)
    query.first()
    branch.second()
    grads(1536, 3)
    value.first()
    back(0, 6)
    query.second()
    for load in loads[7:]:
        load.wait()
    sums[...] = jnp.zeros_like(sums)

    def norm_back(rows, _):
        n, inverse = normed(x[rows, :].astype(jnp.float32))
        u = acc[rows, :]
        scaled = u * vec[0:1, :]
        average = jnp.mean(scaled, -1, keepdims=True)
        project = jnp.mean(scaled * n, -1, keepdims=True)
        grad_tokens[rows, :] = d_res[rows, :] + inverse * (scaled - average - n * project)
        sums[0] += jnp.sum((u * n).reshape(BLOCK // 8, 8, WIDTH), 0)
        sums[1] += jnp.sum(u.reshape(BLOCK // 8, 8, WIDTH), 0)

    row_blocks(norm_back)
    ids = row_ids(8, WIDTH)
    vector_grads = jnp.where(
        ids == 0,
        jnp.sum(sums[0], 0, keepdims=True),
        jnp.where(ids == 1, jnp.sum(sums[1], 0, keepdims=True), norms[...]),
    )
    for half in range(2):
        rows = router[half * 512 : (half + 1) * 512, :]
        side[half, :, :, :, :, pl.ds(0, 128)] = rows.reshape(SIDE, SIDE, SIDE, 8, 128)
        for at in range(SIDE):
            block = vector_grads[:, (half * SIDE + at) * 128 : (half * SIDE + at + 1) * 128]
            side[half, at, :, :, :, pl.ds(128, 128)] = jnp.broadcast_to(block[None, None], (SIDE, SIDE, 8, 128))
    small.open(core, side)
    value.second()
    branch.third()
    small.first()
    query.third()
    value.third()
    small.third()
    branch.fourth()
    query.fourth()
    value.fourth()
    small.fourth()
    branch.last()
    query.last()
    value.last()
    small.last()
    send.close()


def finish(tokens, norm1, attended, vectors, d_resid, dq, dkv_own, dkv_other, d_branch, grad_router, norm_grads,
           layer):
    low, wide = jnp.bfloat16, jnp.float32
    anywhere = pl.BlockSpec(memory_space=pl.ANY)
    vmem = pl.BlockSpec(memory_space=pltpu.VMEM)
    lead = (SIDE, SIDE, SIDE, 8)
    scratch, copies = SmallReduction.scratch(SMALL), 6 + SmallReduction.COPIES
    for piece in RS_PIECES[::-1]:
        scratch, copies = Reduction.scratch(piece) + scratch, copies + Reduction.COPIES
    return pl.pallas_call(
        finish_kernel,
        out_shape=tuple(jax.ShapeDtypeStruct((8, c), wide) for c in RS_COLS)
        + (jax.ShapeDtypeStruct((GROUP, WIDTH), wide),),
        in_specs=[anywhere] * 12,
        out_specs=(vmem,) * 4,
        scratch_shapes=[
            pltpu.VMEM((WIDTH, 3 * WIDTH), low),
            pltpu.VMEM((GROUP, WIDTH), low),
            pltpu.VMEM((GROUP, WIDTH), wide),
            pltpu.VMEM((2, GROUP, HALF), low),
            pltpu.VMEM((2, HALF, 2 * GROUP), low),
            pltpu.VMEM((2, GROUP, 2 * WIDTH), low),
            pltpu.VMEM((2, GROUP, 2 * WIDTH), low),
            pltpu.VMEM((2, GROUP, HALF), low),
            pltpu.VMEM((2 * GROUP, 3 * WIDTH), low),
            pltpu.VMEM((2 * GROUP, WIDTH), low),
            pltpu.VMEM((GROUP, WIDTH), wide),
            pltpu.VMEM((2, 8, WIDTH), wide),
            pltpu.VMEM(lead + (3 * WIDTH,), wide),
            pltpu.VMEM(lead + (WIDTH,), wide),
            pltpu.VMEM((WIDTH, 128), wide),
            pltpu.VMEM((8, WIDTH), wide),
            pltpu.VMEM((8, WIDTH), wide),
            pltpu.VMEM((2,) + lead + (256,), wide),
            pltpu.SemaphoreType.DMA((12,)),
            *scratch,
            pltpu.SemaphoreType.DMA((copies,)),
            pltpu.SemaphoreType.DMA((copies,)),
        ],
        compiler_params=pltpu.CompilerParams(
            collective_id=1, has_side_effects=True, vmem_limit_bytes=60 * 1024 * 1024
        ),
        name="finish",
    )(tokens, norm1, attended, vectors, d_resid, dq, dkv_own, dkv_other, d_branch, grad_router, norm_grads, layer)


def results_kernel(sum_qkv, sum_out, side, given_tokens, qkv, out, router, *rest):
    vectors, (loss, tokens) = rest[:4], rest[4:]
    place = (lax.axis_index("dp") * 64 + lax.axis_index("expert")) % 16
    qkv[...] = sum_qkv[...]
    out[...] = sum_out[...]
    tokens[...] = given_tokens[...]
    router[...] = side[:, :64]
    sums = side[:, 128:256]
    sums_here = pltpu.roll(sums, (16 - place) * 8 % 128, 1)
    for n in range(4):
        vectors[n][...] = sums_here[n : n + 1, :8]
    loss[...] = sums[4:5, 0:1] / (sums[5:6, 0:1] * WIDTH)


def results(*sums):
    wide = jnp.float32
    shapes = ((8, 3072), (8, 1024), (8, 64), (1, 8), (1, 8), (1, 8), (1, 8), (1, 1), (GROUP, WIDTH))
    vmem = pl.BlockSpec(memory_space=pltpu.VMEM)
    return pl.pallas_call(
        results_kernel,
        out_shape=tuple(jax.ShapeDtypeStruct(s, wide) for s in shapes),
        in_specs=[vmem] * 4,
        out_specs=(vmem,) * 9,
        name="results",
    )(*sums)


def per_device(
    tokens,
    teacher,
    lengths,
    routes,
    ln1_gain,
    ln1_bias,
    query_key_value_weight,
    output_weight,
    ln2_gain,
    ln2_bias,
    router_weight,
    w_in,
    w_down,
):
    vectors = [vector.reshape(1, 8) for vector in (ln1_gain, ln1_bias, ln2_gain, ln2_bias)]
    layer, in_other, down_other = gather_layer(
        query_key_value_weight, output_weight, router_weight, vectors, w_in[0], w_down[0]
    )
    x, parting, qkv, kv_other, attended, norm1, norm2, residual, lse, probs, placing, vectors = forward(
        tokens[0], teacher[0], routes.reshape(1, GROUP), lengths, layer
    )
    y_back, d_back, g1, g2 = experts(x, parting, w_in[0], in_other, w_down[0], down_other)
    mixed, d_resid, dq, dkv_own, dkv_other, d_branch, grad_router, norm_grads, g1, g2 = backward(
        y_back, d_back, teacher[0], lengths, layer, qkv, kv_other, norm2, residual, lse, probs, placing, vectors,
        g1, g2,
    )
    sums = finish(
        tokens[0], norm1, attended, vectors, d_resid, dq, dkv_own, dkv_other, d_branch, grad_router, norm_grads,
        layer,
    )
    grad_qkv, grad_out, grad_router, *vector_grads, loss_value, grad_tokens = results(*sums)
    return (
        mixed[None],
        loss_value[0, 0],
        grad_tokens[None],
        vector_grads[0][0],
        vector_grads[1][0],
        grad_qkv,
        grad_out,
        vector_grads[2][0],
        vector_grads[3][0],
        grad_router,
        g1[None],
        g2[None],
    )


def solution(mesh):
    placed = (
        P("expert", "dp", None),
        P("expert", "dp", None),
        P("expert"),
        P("expert", "dp", None),
        P(("dp", "expert")),
        P(("dp", "expert")),
        P(("dp", "expert"), None),
        P(("dp", "expert"), None),
        P(("dp", "expert")),
        P(("dp", "expert")),
        P(("dp", "expert"), None),
        P("expert", "dp", None),
        P("expert", "dp", None),
    )
    return jax.shard_map(
        per_device,
        mesh=mesh,
        in_specs=placed,
        out_specs=(
            P("expert", "dp", None),
            P(),
            P("expert", "dp", None),
            P(("dp", "expert")),
            P(("dp", "expert")),
            P(("dp", "expert"), None),
            P(("dp", "expert"), None),
            P(("dp", "expert")),
            P(("dp", "expert")),
            P(("dp", "expert"), None),
            P("expert", "dp", None),
            P("expert", "dp", None),
        ),
        check_vma=False,
    )
```

```python
import jax
import jax.numpy as jnp
from jax import lax
from jax.experimental import pallas as pl
from jax.experimental.pallas import tpu as pltpu
from jax.sharding import PartitionSpec as P

MESH = pl.DeviceIdType.MESH
SIDE = 4
FULL = slice(None)

AG_COLS = 4224
AG_PIECES = ((0, 768, 1408), (1408, 2176, 2816), (2816, 3584, 4224))


def coords():
    e = lax.axis_index("expert")
    return [e // 16, (e // 4) % 4, e % 4]


def shifted(pos, axis, by):
    out = list(pos)
    out[axis] = (pos[axis] + by) % SIDE
    return out


def chip(pos):
    return {"expert": pos[0] * 16 + pos[1] * 4 + pos[2]}


def greet(pos, core):
    barrier = pltpu.get_barrier_semaphore()
    for axis in range(3):
        for by in range(1, SIDE):
            pl.semaphore_signal(barrier, inc=1, device_id=chip(shifted(pos, axis, by)), device_id_type=MESH)
    pl.semaphore_signal(barrier, inc=1, device_id={"dp": 1 - core}, device_id_type=MESH)
    pl.semaphore_wait(barrier, 10)


class Sender:
    def __init__(self, send_sems, recv_sems):
        self.send_sems, self.recv_sems, self.count, self.sent = send_sems, recv_sems, 0, []

    def __call__(self, src, dst, device):
        copy = pltpu.make_async_remote_copy(
            src_ref=src,
            dst_ref=dst,
            send_sem=self.send_sems.at[self.count],
            recv_sem=self.recv_sems.at[self.count],
            device_id=device,
            device_id_type=MESH,
        )
        copy.start()
        self.count += 1
        self.sent.append(copy)
        return copy

    def close(self):
        for copy in self.sent:
            copy.wait_send()


def gather_kernel(
    q, o, r, gain_one, bias_one, gain_two, bias_two, w_in, w_down, whole, in_other, down_other, shard, own_sem, send_sems, recv_sems
):
    pos = coords()
    core = lax.axis_index("dp")
    partner = {"dp": 1 - core}
    shard[:, :3072] = q[...]
    shard[:, 3072:4096] = o[...]
    lane = lax.broadcasted_iota(jnp.int32, (8, 64), 1)
    row = lax.broadcasted_iota(jnp.int32, (8, 64), 0)
    here = (lane == row + lax.axis_index("expert") % 8 * 8).astype(jnp.float32)
    vectors = jnp.zeros((8, 64), jnp.float32)
    same = (lax.broadcasted_iota(jnp.int32, (8, 8), 0) == lax.broadcasted_iota(jnp.int32, (8, 8), 1)).astype(jnp.float32)
    for n, vector in enumerate((gain_one, bias_one, gain_two, bias_two)):
        column = jnp.sum(same * vector[...].astype(jnp.float32), 1, keepdims=True)
        spread_out = jnp.sum(here * column, 0, keepdims=True)
        vectors = jnp.where(row == n, spread_out, vectors)
    shard[:, 4096:] = jnp.concatenate([r[...].astype(jnp.float32), vectors], 1).astype(jnp.bfloat16)
    own = pltpu.make_async_copy(shard, whole.at[(core, *pos)], own_sem)
    own.start()
    greet(pos, core)
    send = Sender(send_sems, recv_sems)

    def share(region, c0, c1, device):
        spot = whole.at[(core, *region, FULL, pl.ds(c0, c1 - c0))]
        return send(spot, spot, device)

    plans = []
    for piece, (c0, mid, c1) in enumerate(AG_PIECES):
        axes = [(piece + step) % 3 for step in range(3)]
        spot = whole.at[(core, *pos, FULL, pl.ds(c0, c1 - c0))]
        first = [send(shard.at[:, pl.ds(c0, c1 - c0)], spot, chip(shifted(pos, axes[0], by))) for by in (1, 3, 2)]
        plans.append((axes, c0, mid, c1, first))
    across = [send(w_in, in_other, partner), send(w_down, down_other, partner)]
    own.wait()

    def line(axes, second, third):
        region = [None] * 3
        region[axes[0]], region[axes[1]], region[axes[2]] = FULL, second, third
        return region

    def at(axis, by):
        return (pos[axis] + by) % SIDE

    seconds, lines = [], [{} for _ in plans]

    def onward(piece, by):
        axes, c0, mid, c1, _ = plans[piece]
        region = line(axes, at(axes[1], by), pos[axes[2]])
        lines[piece][by] = (
            share(region, c0, c1, chip(shifted(pos, axes[2], 1))),
            share(region, c0, c1, chip(shifted(pos, axes[2], 3))),
        )
        across.append(share(region, c0, c1, partner))

    def relay(piece, by):
        axes, c0, mid, c1, _ = plans[piece]
        up, down = lines[piece][by]
        up.wait_recv()
        below = line(axes, at(axes[1], by), at(axes[2], 3))
        on_up = share(below, c0, mid, chip(shifted(pos, axes[2], 1)))
        down.wait_recv()
        above = line(axes, at(axes[1], by), at(axes[2], 1))
        on_down = share(above, mid, c1, chip(shifted(pos, axes[2], 3)))
        across.append(share(below, c0, c1, partner))
        across.append(share(above, c0, c1, partner))
        lines[piece][by] = (on_up, on_down)

    def end(piece, by):
        axes, c0, mid, c1, _ = plans[piece]
        for copy in lines[piece][by]:
            copy.wait_recv()
        across.append(share(line(axes, at(axes[1], by), at(axes[2], 2)), c0, c1, partner))

    for piece, (axes, c0, mid, c1, first) in enumerate(plans):
        for copy in first:
            copy.wait_recv()
        region = line(axes, pos[axes[1]], pos[axes[2]])
        seconds.append([share(region, c0, c1, chip(shifted(pos, axes[1], by))) for by in (1, 3, 2)])
        onward(piece, 0)
    for n, by in enumerate((3, 1)):
        for piece in range(3):
            seconds[piece][n].wait_recv()
            onward(piece, by)
    for piece in range(3):
        relay(piece, 0)
    for piece in range(3):
        seconds[piece][2].wait_recv()
        onward(piece, 2)
    for by in (3, 1, 2):
        for piece in range(3):
            relay(piece, by)
    for by in (0, 3, 1, 2):
        for piece in range(3):
            end(piece, by)
    for copy in across:
        copy.wait_recv()
    send.close()


def gather_layer(q, o, r, vectors, w_in, w_down):
    copies = 3 * (3 + 3 + 4 * 4 + 4 * 4) + 2
    anywhere, vmem = pl.BlockSpec(memory_space=pl.ANY), pl.BlockSpec(memory_space=pltpu.VMEM)
    whole, in_other, down_other = pl.pallas_call(
        gather_kernel,
        out_shape=(
            jax.ShapeDtypeStruct((2, SIDE, SIDE, SIDE, 8, AG_COLS), jnp.bfloat16),
            jax.ShapeDtypeStruct(w_in.shape, w_in.dtype),
            jax.ShapeDtypeStruct(w_down.shape, w_down.dtype),
        ),
        in_specs=[vmem] * 7 + [anywhere] * 2,
        out_specs=(anywhere,) * 3,
        scratch_shapes=[
            pltpu.VMEM((8, AG_COLS), jnp.bfloat16),
            pltpu.SemaphoreType.DMA,
            pltpu.SemaphoreType.DMA((copies,)),
            pltpu.SemaphoreType.DMA((copies,)),
        ],
        compiler_params=pltpu.CompilerParams(collective_id=0, has_side_effects=True),
        name="gather_layer",
    )(q, o, r, *vectors, w_in, w_down)
    return whole.reshape(1024, AG_COLS), in_other, down_other


RS_COLS = (3072, 1024, 256)
RS_PIECES = ((0, 0, 768, 1536, 0), (0, 1536, 2304, 3072, 1), (1, 0, 512, 1024, 2))
ORDER = (2, 1, 3, 0)


class Reduction:
    low = jnp.bfloat16
    COPIES = 8 + 8 + 3 + 3

    def __init__(self, piece, pos, send, source, out, bufs):
        _, self.c0, self.mid, self.c1, first = piece
        self.axes = [(first + step) % 3 for step in range(3)]
        self.pos, self.send, self.source, self.out = pos, send, source, out
        (self.total, self.send_2, self.recv_2, self.mine, self.send_3, self.recv_3) = bufs[:6]
        self.take(bufs[6:])

    def take(self, bufs):
        self.send_a, self.recv_a, self.send_b, self.recv_b = bufs

    @classmethod
    def scratch(cls, piece):
        _, c0, mid, c1, _ = piece
        width, low, wide = c1 - c0, cls.low, jnp.float32
        return [
            pltpu.VMEM((SIDE, 8, width), wide),
            pltpu.VMEM((3, SIDE, 8, width), low),
            pltpu.VMEM((3, SIDE, 8, width), low),
            pltpu.VMEM((8, width), wide),
            pltpu.VMEM((3, 8, width), low),
            pltpu.VMEM((3, 8, width), low),
        ] + cls.more(mid - c0, width)

    @classmethod
    def more(cls, half, width):
        return [pltpu.VMEM((2, SIDE, SIDE, 8, half), cls.low)] * 2 + [pltpu.VMEM((2, SIDE, SIDE, 8, width), cls.low)] * 2

    def to(self, step, by):
        return chip(shifted(self.pos, self.axes[step], by))

    def term(self, first, second, third, c0, c1):
        spot = [None] * 3
        spot[self.axes[0]] = (self.pos[self.axes[0]] + first) % SIDE
        spot[self.axes[1]] = (self.pos[self.axes[1]] + second) % SIDE
        spot[self.axes[2]] = third
        return self.source[(*spot, FULL, pl.ds(c0, c1 - c0))]

    def first(self):
        self.firsts = []
        for group in ORDER:
            @pl.loop(0, SIDE)
            def _(s):
                self.send_a[0, group, s] = self.term(2, group, s, self.c0, self.mid).astype(self.low)
                self.send_a[1, group, s] = self.term(2, group, s, self.mid, self.c1).astype(self.low)

            self.firsts.append([
                self.send(self.send_a.at[way, group], self.recv_a.at[way, group], self.to(0, (1, 3)[way]))
                for way in range(2)
            ])

    def second(self):
        self.seconds = []
        half = self.mid - self.c0
        for n, group in enumerate(ORDER):
            for copy in self.firsts[n]:
                copy.wait_recv()

            @pl.loop(0, SIDE)
            def _(s):
                for way, by in enumerate((1, 3)):
                    for part, (c0, c1) in enumerate(((self.c0, self.mid), (self.mid, self.c1))):
                        block = self.term(by, group, s, c0, c1)
                        if part == way:
                            block = block + self.recv_a[way, group, s].astype(jnp.float32)
                        self.send_b[way, group, s, :, pl.ds(part * half, half)] = block.astype(self.low)

            self.seconds.append([
                self.send(self.send_b.at[way, group], self.recv_b.at[way, group], self.to(0, (1, 3)[way]))
                for way in range(2)
            ])

    def arrived(self, n, group, s):
        block = self.term(0, group, s, self.c0, self.c1)
        for way in range(2):
            block = block + self.recv_b[way, group, s].astype(jnp.float32)
        return block

    def third(self):
        self.thirds = []
        for n, group in enumerate(ORDER):
            for copy in self.seconds[n]:
                copy.wait_recv()

            @pl.loop(0, SIDE)
            def _(s):
                block = self.arrived(n, group, s)
                if group:
                    self.send_2[group - 1, s] = block.astype(self.low)
                else:
                    self.total[s] = block

            if group:
                self.thirds.append(self.send(self.send_2.at[group - 1], self.recv_2.at[group - 1], self.to(1, group)))

    def fourth(self):
        for copy in self.thirds:
            copy.wait_recv()
        self.fourths = []
        for by in ORDER:
            s = (self.pos[self.axes[2]] + by) % SIDE
            block = self.total[s]
            for n in range(3):
                block = block + self.recv_2[n, s].astype(jnp.float32)
            if by:
                self.send_3[by - 1] = block.astype(self.low)
                self.fourths.append(self.send(self.send_3.at[by - 1], self.recv_3.at[by - 1], self.to(2, by)))
            else:
                self.mine[...] = block

    def last(self):
        for copy in self.fourths:
            copy.wait_recv()
        block = self.mine[...]
        for n in range(3):
            block = block + self.recv_3[n].astype(jnp.float32)
        self.out[:, pl.ds(self.c0, self.c1 - self.c0)] = block


class SmallReduction(Reduction):
    low = jnp.float32
    COPIES = 1 + 3 + 3 + 3

    def take(self, bufs):
        self.landed, self.send_1, self.recv_1 = bufs

    @classmethod
    def more(cls, half, width):
        return [pltpu.VMEM((SIDE, SIDE, SIDE, 8, width), cls.low)] + [
            pltpu.VMEM((3, SIDE, SIDE, 8, width), cls.low)
        ] * 2

    def open(self, core, both):
        self.source = both.at[core]
        self.opening = self.send(both.at[1 - core], self.landed, {"dp": 1 - core})

    def term(self, *spot):
        kept = self.source
        mine = super().term(*spot)
        self.source = self.landed
        theirs = super().term(*spot)
        self.source = kept
        return mine + theirs

    def first(self):
        self.opening.wait_recv()
        self.seconds = [[]] * SIDE
        copies = []
        for by in (2, 1, 3):
            @pl.loop(0, SIDE)
            def _(s):
                for group in range(SIDE):
                    self.send_1[by - 1, group, s] = self.term(by, group, s, self.c0, self.c1)

            copies.append(self.send(self.send_1.at[by - 1], self.recv_1.at[by - 1], self.to(0, by)))
        self.seconds = [copies] + [[]] * 3

    def arrived(self, n, group, s):
        block = self.term(0, group, s, self.c0, self.c1)
        for way in range(3):
            block = block + self.recv_1[way, group, s]
        return block


SMALL = (2, 0, 128, 256, 2)


ROWS = 512
WIDTH = 1024
HIDDEN = 4096
HALF_IN = WIDTH // 2
HALF_FF = HIDDEN // 2
EXTRA = 128
TILE = 512
N_TILES = HIDDEN // TILE
HALF_TILES = N_TILES // 2
CURVE = 0.7978845608028654


def dot_nt(a, b):
    return lax.dot_general(a, b, (((1,), (1,)), ((), ())), preferred_element_type=jnp.float32)


def dot_nn(a, b):
    return lax.dot_general(a, b, (((1,), (0,)), ((), ())), preferred_element_type=jnp.float32)


def dot_tn(a, b):
    return lax.dot_general(a, b, (((0,), (0,)), ((), ())), preferred_element_type=jnp.float32)


ALL_STEPS = [((2 + n // 16) % 4, (2 + n // 4 % 4) % 4, (2 + n % 4) % 4) for n in range(64)]
STEPS = [steps for steps in ALL_STEPS if sum(steps) % 2] + [steps for steps in ALL_STEPS if sum(steps) % 2 == 0]
OWN = STEPS.index((0, 0, 0))


def ring_places(pos):
    return [[(pos[axis] + step) % 4 * scale for step in range(4)] for axis, scale in enumerate((16, 4, 1))]


def away(places, n, sign):
    return sum(places[axis][sign * step % 4] for axis, step in enumerate(STEPS[n]))


def spread(places, source, target, send_sem, recv_sems):
    for n in range(64):
        if n != OWN:
            d = away(places, n, 1)
            pltpu.make_async_remote_copy(
                src_ref=source.at[d],
                dst_ref=target.at[n],
                send_sem=send_sem,
                recv_sem=recv_sems.at[n // 32],
                device_id={"expert": d},
                device_id_type=MESH,
            ).start()


def bring_back(places, me, source, target, send_sem, recv_sem):
    for n in range(64):
        if n != OWN:
            pltpu.make_async_remote_copy(
                src_ref=source.at[n],
                dst_ref=target.at[me],
                send_sem=send_sem,
                recv_sem=recv_sem,
                device_id={"expert": away(places, n, -1)},
                device_id_type=MESH,
            ).start()


def blocks(ref, count, sem):
    pltpu.make_async_copy(ref.at[pl.ds(0, count)], ref.at[pl.ds(0, count)], sem).wait()


def all_but_one(ref, sem):
    blocks(ref, 63, sem)


def in_turn(count, make, use, first, second):
    make(0, first)

    @pl.loop(0, count // 2 - 1)
    def _(i):
        make(2 * i + 1, second)
        use(2 * i, first)
        make(2 * i + 2, first)
        use(2 * i + 1, second)

    make(count - 1, second)
    use(count - 2, first)
    use(count - 1, second)


def expert_kernel(
    x, r, w1_own, w1_other, w2_own, w2_other,
    y_back, d_back, g1, g2,
    w1, w2, x_in, r_in, xb, xt, act, slope, d_pre, acc, d_exp, out_rows,
    sent1, sent2, got1, got2, stage,
    w_sems, x_sems, r_sems, y_sems, d_sems, own_sems, pass_s, pass_r, out_sems,
):
    pos = coords()
    me = lax.axis_index("expert")
    core = lax.axis_index("dp")
    loads = [
        pltpu.make_async_copy(w1_own, w1.at[core], w_sems.at[0]),
        pltpu.make_async_copy(w1_other, w1.at[1 - core], w_sems.at[1]),
        pltpu.make_async_copy(w2_own, w2.at[core], w_sems.at[2]),
        pltpu.make_async_copy(w2_other, w2.at[1 - core], w_sems.at[3]),
    ]
    barrier = pltpu.get_barrier_semaphore()

    places = ring_places(pos)
    for n in range(64):
        if n != OWN:
            pl.semaphore_signal(barrier, inc=1, device_id={"expert": away(places, n, 1)}, device_id_type=MESH)

    pl.semaphore_signal(barrier, inc=1, device_id={"dp": 1 - core}, device_id_type=MESH)
    own_x = pltpu.make_async_copy(x.at[me], x_in.at[OWN], own_sems.at[0])
    own_r = pltpu.make_async_copy(r.at[me], r_in.at[OWN], own_sems.at[1])
    own_x.start()
    own_r.start()
    for load in loads:
        load.start()
    pl.semaphore_wait(barrier, 64)
    spread(places, x, x_in, x_sems.at[0], x_sems.at[pl.ds(1, 2)])
    spread(places, r, r_in, r_sems.at[0], r_sems.at[pl.ds(1, 2)])
    acc[...] = jnp.zeros_like(acc)
    spare = [stage.at[n] for n in range(2)]
    for part in range(2):
        rows = pl.ds(part * 256, 256)
        if part == 0:
            blocks(x_in, 32, x_sems.at[1])
        else:
            own_x.wait()
            blocks(x_in, 31, x_sems.at[2])

        @pl.loop(0, 4)
        def _(i):
            block = x_in[pl.ds(part * 32 + i * 8, 8)].astype(jnp.float32).reshape(64, WIDTH)
            xb[pl.ds(pl.multiple_of(part * 256 + i * 64, 64), 64), :] = block.astype(jnp.bfloat16)

        if part == 0:
            loads[0].wait()
            loads[1].wait()

        def make(c, to):
            cols = pl.ds(pl.multiple_of(c * TILE, TILE), TILE)
            to[:256, :] = dot_nn(xb[rows, :HALF_IN], w1[0, :, cols]) + dot_nn(xb[rows, HALF_IN:], w1[1, :, cols])

        def use(c, pre_ref):
            cols = pl.ds(pl.multiple_of(c * TILE, TILE), TILE)
            pre = pre_ref[:256, :]
            square = pre * pre
            t = jnp.tanh(CURVE * pre * (1.0 + 0.044715 * square))
            low = (0.5 * pre * (1.0 + t)).astype(jnp.bfloat16)
            act[rows, cols] = low
            slope[rows, cols] = 0.5 * (1.0 + t) + (0.5 * CURVE) * pre * (1.0 - t * t) * (1.0 + (3 * 0.044715) * square)
            half = c // HALF_TILES
            ff = pl.ds(pl.multiple_of((c % HALF_TILES) * TILE, TILE), TILE)
            acc[rows, :] += dot_nn(low, w2[half, ff, :])

        if part == 0:
            loads[2].wait()
            loads[3].wait()
        in_turn(N_TILES, make, use, *spare)

    own_r.wait()
    blocks(r_in, 32, r_sems.at[1])
    blocks(r_in, 31, r_sems.at[2])

    @pl.loop(0, 8)
    def _(i):
        rows = pl.ds(pl.multiple_of(i * 64, 64), 64)
        low = acc[rows, :].astype(jnp.bfloat16)
        out = low.astype(jnp.float32)
        out_rows[pl.ds(i * 8, 8)] = out.reshape(8, 8, WIDTH).astype(jnp.bfloat16)
        parted = r_in[pl.ds(i * 8, 8)].astype(jnp.float32).reshape(64, WIDTH + EXTRA)
        gate = parted[:, WIDTH : WIDTH + 1] + parted[:, WIDTH + 1 : WIDTH + 2]
        valid = parted[:, WIDTH + 2 : WIDTH + 3]
        d_exp[rows, :] = (gate * valid * (parted[:, :WIDTH] + gate * out)).astype(jnp.bfloat16)

    own_y = pltpu.make_async_copy(out_rows.at[OWN], y_back.at[me], own_sems.at[2])
    own_y.start()
    bring_back(places, me, out_rows, y_back, y_sems.at[0], y_sems.at[1])
    acc[...] = jnp.zeros_like(acc)

    def make_back(c, to):
        ff = pl.ds(pl.multiple_of((c % HALF_TILES) * TILE, TILE), TILE)
        to[...] = dot_nt(d_exp[...], w2[c // HALF_TILES, ff, :])

    def use_back(c, d_act):
        cols = pl.ds(pl.multiple_of(c * TILE, TILE), TILE)
        low = (slope[:, cols] * d_act[...]).astype(jnp.bfloat16)
        d_pre[:, cols] = low
        acc[:, :HALF_IN] += dot_nt(low, w1[0, :, cols])
        acc[:, HALF_IN:] += dot_nt(low, w1[1, :, cols])

    in_turn(N_TILES, make_back, use_back, *spare)

    own_y.wait()
    all_but_one(out_rows, y_sems.at[0])

    @pl.loop(0, 8)
    def _(i):
        rows = pl.ds(pl.multiple_of(i * 64, 64), 64)
        out_rows[pl.ds(i * 8, 8)] = acc[rows, :].reshape(8, 8, WIDTH).astype(jnp.bfloat16)

    own_d = pltpu.make_async_copy(out_rows.at[OWN], d_back.at[me], own_sems.at[3])
    own_d.start()
    bring_back(places, me, out_rows, d_back, d_sems.at[0], d_sems.at[1])

    xt[...] = xb[...].astype(jnp.float32).T.astype(jnp.bfloat16)

    def passed(buf, got, c, base):
        return pltpu.make_async_remote_copy(
            src_ref=buf.at[c],
            dst_ref=got.at[c],
            send_sem=pass_s.at[base + c],
            recv_sem=pass_r.at[base + c],
            device_id={"dp": 1 - core},
            device_id_type=MESH,
        )

    def in_rows(half):
        return xt[pl.ds(pl.multiple_of(half * HALF_IN, HALF_IN), HALF_IN), :]

    @pl.loop(0, N_TILES)
    def _(c):
        cols = pl.ds(pl.multiple_of(c * TILE, TILE), TILE)
        sent1[c] = dot_nn(in_rows(1 - core), d_pre[:, cols]).astype(jnp.bfloat16)
        passed(sent1, got1, c, 0).start()

    @pl.loop(0, HALF_TILES)
    def _(c):
        cols = pl.ds(pl.multiple_of((1 - core) * HALF_FF + c * TILE, TILE), TILE)
        sent2[c] = dot_tn(act[:, cols], d_exp[...]).astype(jnp.bfloat16)
        passed(sent2, got2, c, N_TILES).start()

    def made(slot, columns):
        return slope.at[:, pl.ds(pl.multiple_of(slot * WIDTH, WIDTH), columns)]

    def out1(c, slot):
        cols = pl.ds(pl.multiple_of(c * TILE, TILE), TILE)
        return pltpu.make_async_copy(made(slot, TILE), g1.at[:, cols], out_sems.at[slot])

    def out2(c, slot):
        rows = pl.ds(pl.multiple_of(c * TILE, TILE), TILE)
        return pltpu.make_async_copy(made(slot, WIDTH), g2.at[rows, :], out_sems.at[slot])

    @pl.loop(0, N_TILES)
    def _(c):
        slot = c % 2
        cols = pl.ds(pl.multiple_of(c * TILE, TILE), TILE)

        @pl.when(c >= 2)
        def _():
            out1(c - 2, slot).wait()

        passed(sent1, got1, c, 0).wait_recv()
        made(slot, TILE)[...] = dot_nn(in_rows(core), d_pre[:, cols]) + got1[c].astype(jnp.float32)
        out1(c, slot).start()

    out1(N_TILES - 2, 0).wait()
    out1(N_TILES - 1, 1).wait()

    @pl.loop(0, HALF_TILES)
    def _(c):
        slot = c % 2
        cols = pl.ds(pl.multiple_of(core * HALF_FF + c * TILE, TILE), TILE)

        @pl.when(c >= 2)
        def _():
            out2(c - 2, slot).wait()

        passed(sent2, got2, c, N_TILES).wait_recv()
        made(slot, WIDTH)[...] = dot_tn(act[:, cols], d_exp[...]) + got2[c].astype(jnp.float32)
        out2(c, slot).start()

    out2(HALF_TILES - 2, 0).wait()
    out2(HALF_TILES - 1, 1).wait()

    @pl.loop(0, N_TILES)
    def _(c):
        passed(sent1, got1, c, 0).wait_send()

    @pl.loop(0, HALF_TILES)
    def _(c):
        passed(sent2, got2, c, N_TILES).wait_send()

    own_d.wait()
    all_but_one(x_in, x_sems.at[0])
    all_but_one(r_in, r_sems.at[0])
    all_but_one(out_rows, d_sems.at[0])
    all_but_one(out_rows, y_sems.at[1])
    all_but_one(out_rows, d_sems.at[1])


def experts(x, r, w1_own, w1_other, w2_own, w2_other):
    low, wide = jnp.bfloat16, jnp.float32
    anywhere = pl.BlockSpec(memory_space=pl.ANY)
    return pl.pallas_call(
        expert_kernel,
        out_shape=(
            jax.ShapeDtypeStruct((64, 8, WIDTH), low),
            jax.ShapeDtypeStruct((64, 8, WIDTH), low),
            jax.ShapeDtypeStruct((HALF_IN, HIDDEN), wide),
            jax.ShapeDtypeStruct((HALF_FF, WIDTH), wide),
        ),
        in_specs=[anywhere] * 6,
        out_specs=(anywhere,) * 4,
        scratch_shapes=[
            pltpu.VMEM((2, HALF_IN, HIDDEN), low),
            pltpu.VMEM((2, HALF_FF, WIDTH), low),
            pltpu.VMEM((64, 8, WIDTH), low),
            pltpu.VMEM((64, 8, WIDTH + EXTRA), low),
            pltpu.VMEM((ROWS, WIDTH), low),
            pltpu.VMEM((WIDTH, ROWS), low),
            pltpu.VMEM((ROWS, HIDDEN), low),
            pltpu.VMEM((ROWS, HIDDEN), wide),
            pltpu.VMEM((ROWS, HIDDEN), low),
            pltpu.VMEM((ROWS, WIDTH), wide),
            pltpu.VMEM((ROWS, WIDTH), low),
            pltpu.VMEM((64, 8, WIDTH), low),
            pltpu.VMEM((N_TILES, HALF_IN, TILE), low),
            pltpu.VMEM((HALF_TILES, TILE, WIDTH), low),
            pltpu.VMEM((N_TILES, HALF_IN, TILE), low),
            pltpu.VMEM((HALF_TILES, TILE, WIDTH), low),
            pltpu.VMEM((2, ROWS, TILE), wide),
            pltpu.SemaphoreType.DMA((4,)),
            pltpu.SemaphoreType.DMA((3,)),
            pltpu.SemaphoreType.DMA((3,)),
            pltpu.SemaphoreType.DMA((2,)),
            pltpu.SemaphoreType.DMA((2,)),
            pltpu.SemaphoreType.DMA((4,)),
            pltpu.SemaphoreType.DMA((N_TILES + HALF_TILES,)),
            pltpu.SemaphoreType.DMA((N_TILES + HALF_TILES,)),
            pltpu.SemaphoreType.DMA((2,)),
        ],
        compiler_params=pltpu.CompilerParams(
            collective_id=2, has_side_effects=True, vmem_limit_bytes=63 * 1024 * 1024
        ),
        name="experts",
    )(x, r, w1_own, w1_other, w2_own, w2_other)


GROUP = 256
HEADS = 16
PAIRS = HEADS // 2
SLOTS = 512
BLOCK = 64
EPS = 1e-05
MASKED = -1e30


def lanes(start, size):
    return pl.ds(pl.multiple_of(start, 128), size)


def row_blocks(body, size=BLOCK):
    @pl.loop(0, GROUP // size)
    def _(i):
        body(pl.ds(pl.multiple_of(i * size, size), size), i * size)


def normed(v):
    centred = v - jnp.mean(v, -1, keepdims=True)
    inverse = lax.rsqrt(jnp.mean(centred * centred, -1, keepdims=True) + EPS)
    return centred * inverse, inverse


def lane_ids(rows, columns):
    return lax.broadcasted_iota(jnp.int32, (rows, columns), 1)


def row_ids(rows, columns):
    return lax.broadcasted_iota(jnp.int32, (rows, columns), 0)


def allowed_keys(core, length):
    query, key = row_ids(GROUP, GROUP), lane_ids(GROUP, GROUP)
    own = (key <= query) & (key + core * GROUP < length)
    other = (key < length) & (core == 1)
    return own, other


def head_scores(q, k_own, k_other, own, other):
    s_own = jnp.where(own, dot_nt(q, k_own), MASKED)
    s_other = jnp.where(other, dot_nt(q, k_other), MASKED)
    return s_own, s_other


def forward_kernel(
    tokens, teacher, routes_row, lengths, layer,
    x_out, parting_out, qkv_out, kv_other_out, attended_out, norm1_out, norm2_out, residual_out,
    lse_out, probs_out, placing_out, vectors_out,
    weights, norm1, qkv, kv_other, attended, norm2, residual, lse, probs, placing, vectors, parted, packed_x, packed_r,
    load_sems, out_sems, kv_sems,
):
    core = lax.axis_index("dp")
    length = lengths[0]
    spans = ((4096, 128), (1024, 1024), (2048, 1024), (0, 1024), (3072, 1024))
    loads = [
        pltpu.make_async_copy(layer.at[:, pl.ds(c, n)], weights.at[:, pl.ds(c, n)], load_sems.at[i])
        for i, (c, n) in enumerate(spans)
    ]
    for load in loads:
        load.start()
    outs = []

    def save(src, dst):
        copy = pltpu.make_async_copy(src, dst, out_sems.at[len(outs)])
        copy.start()
        outs.append(copy)

    barrier = pltpu.get_barrier_semaphore()
    pl.semaphore_signal(barrier, inc=1, device_id={"dp": 1 - core}, device_id_type=MESH)

    def statistics(rows, _):
        n, _ = normed(tokens[rows, :].astype(jnp.float32))
        residual[rows, :] = n

    row_blocks(statistics, 64)
    loads[0].wait()
    for g in range(16):
        part = weights[pl.ds(g * 64, 64), pl.ds(4096, 128)].astype(jnp.float32)
        part = jnp.sum(part.reshape(8, 8, 128), 0)
        vectors[:, g * 64 : (g + 1) * 64] = part[:, 64:]
    save(vectors, vectors_out)

    routes = jnp.where(row_ids(GROUP, GROUP) == lane_ids(GROUP, GROUP), routes_row[...], 0)
    route = jnp.sum(routes.astype(jnp.float32), -1, keepdims=True)

    def first_norm(rows, _):
        norm1[rows, :] = (residual[rows, :] * vectors[0:1, :] + vectors[1:2, :]).astype(jnp.bfloat16)

    row_blocks(first_norm, 64)
    save(norm1, norm1_out)

    def project(block):
        @pl.loop(0, 2)
        def _(i):
            cols = lanes(block * 1024 + i * 512, 512)
            qkv[:, cols] = dot_nn(norm1[...], weights[:, cols]).astype(jnp.bfloat16)

    loads[1].wait()
    project(1)
    loads[2].wait()
    project(2)
    pl.semaphore_wait(barrier, 1)
    passed = pltpu.make_async_remote_copy(
        src_ref=qkv.at[:, pl.ds(1024, 2048)],
        dst_ref=kv_other,
        send_sem=kv_sems.at[0],
        recv_sem=kv_sems.at[1],
        device_id={"dp": 1 - core},
        device_id_type=MESH,
    )
    passed.start()
    loads[3].wait()
    project(0)
    save(qkv, qkv_out)
    passed.wait_recv()
    save(kv_other, kv_other_out)

    own, other = allowed_keys(core, length)
    lse[...] = jnp.zeros_like(lse)

    @pl.loop(0, PAIRS)
    def _(pair):
        q = qkv[:, lanes(pair * 128, 128)] * 0.125
        k_own, v_own = qkv[:, lanes(1024 + pair * 128, 128)], qkv[:, lanes(2048 + pair * 128, 128)]
        k_other, v_other = kv_other[:, lanes(pair * 128, 128)], kv_other[:, lanes(1024 + pair * 128, 128)]
        left = lane_ids(GROUP, 128) < 64
        results = []
        for h in range(2):
            qh = jnp.where(left == (h == 0), q, jnp.zeros_like(q))
            s_own, s_other = head_scores(qh, k_own, k_other, own, other)
            top = jnp.max(jnp.maximum(s_own, s_other), -1, keepdims=True)
            e_own, e_other = jnp.exp(s_own - top), jnp.exp(s_other - top)
            total = jnp.sum(e_own + e_other, -1, keepdims=True)
            e_own, e_other = e_own.astype(jnp.bfloat16), e_other.astype(jnp.bfloat16)
            results.append((dot_nn(e_own, v_own) + dot_nn(e_other, v_other)) * (1.0 / total))
            lse[...] = jnp.where(lane_ids(GROUP, 128) == pair * 2 + h, top + jnp.log(total), lse[...])
        attended[:, lanes(pair * 128, 128)] = jnp.where(left, results[0], results[1]).astype(jnp.bfloat16)

    save(attended, attended_out)
    save(lse, lse_out)
    loads[4].wait()

    @pl.loop(0, 2)
    def _(i):
        cols = lanes(i * 512, 512)
        branch = dot_nn(attended[...], weights[:, lanes(3072 + i * 512, 512)])
        residual[:, cols] = tokens[:, cols].astype(jnp.float32) + branch

    save(residual, residual_out)

    def second_norm(rows, _):
        n, _ = normed(residual[rows, :])
        norm2[rows, :] = (n * vectors[2:3, :] + vectors[3:4, :]).astype(jnp.bfloat16)
        parted[rows, :WIDTH] = (residual[rows, :] - teacher[rows, :].astype(jnp.float32)).astype(jnp.bfloat16)

    row_blocks(second_norm, 64)
    save(norm2, norm2_out)
    logits = dot_nn(norm2[...], weights[:, pl.ds(4096, 128)])
    ids = lane_ids(GROUP, 128)
    logits = jnp.where(ids < 64, logits, MASKED)
    e = jnp.exp(logits - jnp.max(logits, -1, keepdims=True))
    share = e / jnp.sum(e, -1, keepdims=True)
    chosen = ids.astype(jnp.float32) == route
    gate = jnp.sum(jnp.where(chosen, share, 0.0), -1, keepdims=True)
    probs[...] = jnp.where(ids == 64, gate, jnp.where(ids == 65, route, share))
    save(probs, probs_out)
    low_gate = gate.astype(jnp.bfloat16).astype(jnp.float32)
    valid = (row_ids(GROUP, 128) + core * GROUP < length).astype(jnp.float32)
    extras = jnp.where(ids == 0, low_gate, jnp.where(ids == 1, gate - low_gate, jnp.where(ids == 2, valid, 0.0)))
    parted[:, WIDTH:] = extras.astype(jnp.bfloat16)
    marks = chosen.astype(jnp.float32).astype(jnp.bfloat16)
    before = (lane_ids(GROUP, GROUP) < row_ids(GROUP, GROUP)).astype(jnp.float32).astype(jnp.bfloat16)
    rank = jnp.sum(jnp.where(chosen, dot_nn(before, marks), 0.0), -1, keepdims=True)
    slot = route * 8.0 + rank
    placing[...] = (lane_ids(GROUP, SLOTS).astype(jnp.float32) == slot).astype(jnp.float32).astype(jnp.bfloat16)
    save(placing, placing_out)
    for half in range(2):
        to_slots = placing[:, half * 256 : (half + 1) * 256].astype(jnp.float32).T.astype(jnp.bfloat16)
        sent = dot_nn(to_slots, norm2[...])
        packed_x[half * 32 : (half + 1) * 32] = sent.reshape(32, 8, WIDTH).astype(jnp.bfloat16)
        sent = dot_nn(to_slots, parted[...])
        packed_r[half * 32 : (half + 1) * 32] = sent.reshape(32, 8, WIDTH + EXTRA).astype(jnp.bfloat16)
    save(packed_x, x_out)
    save(packed_r, parting_out)
    passed.wait_send()
    for copy in outs:
        copy.wait()


def forward(tokens, teacher, routes, lengths, layer):
    low, wide = jnp.bfloat16, jnp.float32
    anywhere = pl.BlockSpec(memory_space=pl.ANY)
    vmem = pl.BlockSpec(memory_space=pltpu.VMEM)
    saved = [
        ((64, 8, WIDTH), low),
        ((64, 8, WIDTH + EXTRA), low),
        ((GROUP, 3 * WIDTH), low),
        ((GROUP, 2 * WIDTH), low),
        ((GROUP, WIDTH), low),
        ((GROUP, WIDTH), low),
        ((GROUP, WIDTH), low),
        ((GROUP, WIDTH), wide),
        ((GROUP, 128), wide),
        ((GROUP, 128), wide),
        ((GROUP, SLOTS), low),
        ((8, WIDTH), wide),
    ]
    return pl.pallas_call(
        forward_kernel,
        out_shape=tuple(jax.ShapeDtypeStruct(s, t) for s, t in saved),
        in_specs=[vmem, vmem, vmem, pl.BlockSpec(memory_space=pltpu.SMEM), anywhere],
        out_specs=(anywhere,) * len(saved),
        scratch_shapes=[
            pltpu.VMEM((WIDTH, AG_COLS), low),
            pltpu.VMEM((GROUP, WIDTH), low),
            pltpu.VMEM((GROUP, 3 * WIDTH), low),
            pltpu.VMEM((GROUP, 2 * WIDTH), low),
            pltpu.VMEM((GROUP, WIDTH), low),
            pltpu.VMEM((GROUP, WIDTH), low),
            pltpu.VMEM((GROUP, WIDTH), wide),
            pltpu.VMEM((GROUP, 128), wide),
            pltpu.VMEM((GROUP, 128), wide),
            pltpu.VMEM((GROUP, SLOTS), low),
            pltpu.VMEM((8, WIDTH), wide),
            pltpu.VMEM((GROUP, WIDTH + EXTRA), low),
            pltpu.VMEM((64, 8, WIDTH), low),
            pltpu.VMEM((64, 8, WIDTH + EXTRA), low),
            pltpu.SemaphoreType.DMA((5,)),
            pltpu.SemaphoreType.DMA((len(saved),)),
            pltpu.SemaphoreType.DMA((2,)),
        ],
        compiler_params=pltpu.CompilerParams(
            collective_id=3, has_side_effects=True, vmem_limit_bytes=56 * 1024 * 1024
        ),
        name="forward",
    )(tokens, teacher, routes, lengths, layer)


def backward_kernel(
    y_back, d_back, teacher_in, lengths, layer, qkv_in, kv_other_in, norm2_in, residual_in, lse_in, probs_in,
    placing_in, vectors_in, g1, g2,
    mixed_to, d_resid_to, dq_to, dkv_own_to, dkv_other_to, d_branch_to, grad_router_to, norm_grads_to, g1_out, g2_out,
    y_in, d_in, teacher, qkv, kv_other, norm2, residual, lse, probs, placing, vectors,
    mixed_out, d_resid, dq, dkv_own, dkv_other, d_branch, grad_router, norm_grads,
    w_out, w_router, eo, dn, sums, d_attended, logit_parts,
    held1, held2, pass_sems, load_sems, out_sems,
):
    core = lax.axis_index("dp")
    length = lengths[0]
    spans = (
        (y_back, y_in),
        (placing_in, placing),
        (d_back, d_in),
        (probs_in, probs),
        (residual_in, residual),
        (teacher_in, teacher),
        (layer.at[:, pl.ds(4096, 128)], w_router),
        (norm2_in, norm2),
        (vectors_in, vectors),
        (layer.at[:, pl.ds(3072, 1024)], w_out),
        (qkv_in, qkv),
        (kv_other_in, kv_other),
        (lse_in, lse),
    )
    loads = [pltpu.make_async_copy(src, dst, load_sems.at[n]) for n, (src, dst) in enumerate(spans)]
    for load in loads:
        load.start()
    passing = [
        pltpu.make_async_copy(g1, held1, pass_sems.at[0]),
        pltpu.make_async_copy(g2, held2, pass_sems.at[1]),
    ]
    passed_on = [
        pltpu.make_async_copy(held1, g1_out, pass_sems.at[2]),
        pltpu.make_async_copy(held2, g2_out, pass_sems.at[3]),
    ]
    outs = []

    def save(src, dst):
        copy = pltpu.make_async_copy(src, dst, out_sems.at[len(outs)])
        copy.start()
        outs.append(copy)

    loads[0].wait()
    loads[1].wait()
    rows_back = y_in[...].astype(jnp.float32).reshape(SLOTS, WIDTH).astype(jnp.bfloat16)
    eo[...] = dot_nn(placing[...], rows_back)
    loads[2].wait()
    rows_back = d_in[...].astype(jnp.float32).reshape(SLOTS, WIDTH).astype(jnp.bfloat16)
    dn[...] = dot_nn(placing[...], rows_back)
    sums[...] = jnp.zeros_like(sums)
    for load in loads[3:6]:
        load.wait()

    def loss(rows, first):
        ids = lane_ids(BLOCK, 128)
        share = probs[rows, :]
        gate = share[:, 64:65]
        chosen = ids.astype(jnp.float32) == share[:, 65:66]
        share = jnp.where(ids < 64, share, 0.0)
        out = eo[rows, :]
        mixed = (residual[rows, :] + gate * out).astype(jnp.bfloat16)
        mixed_out[rows, :] = mixed
        valid = (row_ids(BLOCK, 1) + first + core * GROUP < length).astype(jnp.float32)
        d_mixed = valid * (mixed.astype(jnp.float32) - teacher[rows, :].astype(jnp.float32))
        d_resid[rows, :] = d_mixed
        d_gate = jnp.sum(d_mixed * out, -1, keepdims=True)
        d_logits = d_gate * gate * (chosen.astype(jnp.float32) - share)
        high = d_logits.astype(jnp.bfloat16)
        logit_parts[rows, :128] = high
        logit_parts[rows, 128:] = (d_logits - high.astype(jnp.float32)).astype(jnp.bfloat16)
        square = jnp.sum((d_mixed * d_mixed).reshape(BLOCK // 8, 8, WIDTH), 0)
        sums[0] += square

    row_blocks(loss)
    save(mixed_out, mixed_to)
    for load in loads[6:9]:
        load.wait()
    for copy in passing:
        copy.start()
    dn[...] += dot_nt(logit_parts[:, :128], w_router[...]) + dot_nt(logit_parts[:, 128:], w_router[...])
    both = dot_tn(norm2[...], logit_parts[...])
    grad_router[...] = both[:, :128] + both[:, 128:]

    def norm_back(rows, _):
        n, inverse = normed(residual[rows, :])
        u = dn[rows, :]
        scaled = u * vectors[2:3, :]
        average = jnp.mean(scaled, -1, keepdims=True)
        project = jnp.mean(scaled * n, -1, keepdims=True)
        d = d_resid[rows, :] + inverse * (scaled - average - n * project)
        d_resid[rows, :] = d
        d_branch[rows, :] = d.astype(jnp.bfloat16)
        sums[1] += jnp.sum((u * n).reshape(BLOCK // 8, 8, WIDTH), 0)
        sums[2] += jnp.sum(u.reshape(BLOCK // 8, 8, WIDTH), 0)

    row_blocks(norm_back)
    save(grad_router, grad_router_to)
    save(d_resid, d_resid_to)
    save(d_branch, d_branch_to)
    valid_all = jnp.clip(length - core * GROUP, 0, GROUP).astype(jnp.float32)
    ids = row_ids(8, WIDTH)
    square = jnp.sum(sums[0])
    norm_grads[...] = jnp.where(
        ids == 2,
        jnp.sum(sums[1], 0, keepdims=True),
        jnp.where(
            ids == 3,
            jnp.sum(sums[2], 0, keepdims=True),
            jnp.where(ids == 4, square, jnp.where(ids == 5, valid_all, 0.0)),
        ),
    )
    save(norm_grads, norm_grads_to)
    loads[9].wait()

    @pl.loop(0, 2)
    def _(i):
        cols = lanes(i * 512, 512)
        rows = pl.ds(pl.multiple_of(i * 512, 512), 512)
        d_attended[:, cols] = dot_nt(d_branch[...], w_out[rows, :]).astype(jnp.bfloat16)

    own, other = allowed_keys(core, length)
    for load in loads[10:]:
        load.wait()

    @pl.loop(0, PAIRS)
    def _(pair):
        @pl.when(pair == 3)
        def _():
            for copy, onward in zip(passing, passed_on):
                copy.wait()
                onward.start()

        q, do = qkv[:, lanes(pair * 128, 128)], d_attended[:, lanes(pair * 128, 128)]
        k_own, v_own = qkv[:, lanes(1024 + pair * 128, 128)], qkv[:, lanes(2048 + pair * 128, 128)]
        k_other, v_other = kv_other[:, lanes(pair * 128, 128)], kv_other[:, lanes(1024 + pair * 128, 128)]
        left = lane_ids(GROUP, 128) < 64
        zero = jnp.zeros_like(q)
        parts = []
        for h in range(2):
            qh = jnp.where(left == (h == 0), q * 0.125, zero)
            doh = jnp.where(left == (h == 0), do, zero)
            s_own, s_other = head_scores(qh, k_own, k_other, own, other)
            log_total = jnp.sum(jnp.where(lane_ids(GROUP, 128) == pair * 2 + h, lse[...], 0.0), -1, keepdims=True)
            p_own, p_other = jnp.exp(s_own - log_total), jnp.exp(s_other - log_total)
            dp_own, dp_other = dot_nt(doh, v_own), dot_nt(doh, v_other)
            total = jnp.sum(p_own * dp_own + p_other * dp_other, -1, keepdims=True)
            ds_own = (p_own * (dp_own - total)).astype(jnp.bfloat16)
            ds_other = (p_other * (dp_other - total)).astype(jnp.bfloat16)
            p_own, p_other = p_own.astype(jnp.bfloat16), p_other.astype(jnp.bfloat16)
            parts.append((
                dot_nn(ds_own, k_own) + dot_nn(ds_other, k_other),
                dot_tn(ds_own, q),
                dot_tn(ds_other, q),
                dot_tn(p_own, do),
                dot_tn(p_other, do),
            ))
        d_q, d_k, d_k_other, d_v, d_v_other = [jnp.where(left, a, b) for a, b in zip(*parts)]
        dq[:, lanes(pair * 128, 128)] = (d_q * 0.125).astype(jnp.bfloat16)
        dkv_own[:, lanes(pair * 128, 128)] = (d_k * 0.125).astype(jnp.bfloat16)
        dkv_own[:, lanes(1024 + pair * 128, 128)] = d_v.astype(jnp.bfloat16)
        dkv_other[:, lanes(pair * 128, 128)] = (d_k_other * 0.125).astype(jnp.bfloat16)
        dkv_other[:, lanes(1024 + pair * 128, 128)] = d_v_other.astype(jnp.bfloat16)

    save(dkv_other, dkv_other_to)
    save(dkv_own, dkv_own_to)
    save(dq, dq_to)
    for copy in passed_on + outs:
        copy.wait()


def backward(y_back, d_back, teacher, lengths, layer, qkv, kv_other, norm2, residual, lse, probs,
             placing, vectors, g1, g2):
    low, wide = jnp.bfloat16, jnp.float32
    anywhere = pl.BlockSpec(memory_space=pl.ANY)
    made = [
        ((GROUP, WIDTH), low),
        ((GROUP, WIDTH), wide),
        ((GROUP, WIDTH), low),
        ((GROUP, 2 * WIDTH), low),
        ((GROUP, 2 * WIDTH), low),
        ((GROUP, WIDTH), low),
        ((WIDTH, 128), wide),
        ((8, WIDTH), wide),
        (g1.shape, wide),
        (g2.shape, wide),
    ]
    return pl.pallas_call(
        backward_kernel,
        out_shape=tuple(jax.ShapeDtypeStruct(s, t) for s, t in made),
        in_specs=[anywhere] * 3 + [pl.BlockSpec(memory_space=pltpu.SMEM)] + [anywhere] * 11,
        out_specs=(anywhere,) * 10,
        scratch_shapes=[
            *[pltpu.VMEM(t.shape, t.dtype) for t in (y_back, d_back, teacher, qkv, kv_other, norm2, residual)],
            *[pltpu.VMEM(t.shape, t.dtype) for t in (lse, probs, placing, vectors)],
            *[pltpu.VMEM(shape, kind) for shape, kind in made[:8]],
            pltpu.VMEM((WIDTH, WIDTH), low),
            pltpu.VMEM((WIDTH, 128), low),
            pltpu.VMEM((GROUP, WIDTH), wide),
            pltpu.VMEM((GROUP, WIDTH), wide),
            pltpu.VMEM((3, 8, WIDTH), wide),
            pltpu.VMEM((GROUP, WIDTH), low),
            pltpu.VMEM((GROUP, 256), low),
            pltpu.VMEM(g1.shape, wide),
            pltpu.VMEM(g2.shape, wide),
            pltpu.SemaphoreType.DMA((4,)),
            pltpu.SemaphoreType.DMA((13,)),
            pltpu.SemaphoreType.DMA((8,)),
        ],
        compiler_params=pltpu.CompilerParams(vmem_limit_bytes=56 * 1024 * 1024),
        name="backward",
    )(y_back, d_back, teacher, lengths, layer, qkv, kv_other, norm2, residual, lse, probs,
      placing, vectors, g1, g2)


HALF = WIDTH // 2


def transposed(block):
    return block.astype(jnp.float32).T.astype(jnp.bfloat16)


def finish_kernel(
    tokens, norm1, attended, vectors, d_resid, dq, dkv_own, dkv_other, d_branch, grad_router, norm_grads, layer,
    sum_qkv, sum_out, sum_side, grad_tokens,
    weights, x, d_res, left, left_t, mine, theirs, got_left, dqkv, d_both, acc, sums, grad_qkv, grad_out,
    router, vec, norms, side, load_sems, *rest,
):
    pos = coords()
    core = lax.axis_index("dp")
    partner = {"dp": 1 - core}
    keep, give = pl.ds(core * HALF, HALF), pl.ds((1 - core) * HALF, HALF)
    own, other = pl.ds(0, GROUP), pl.ds(GROUP, GROUP)
    spans = (
        (norm1.at[:, keep], left.at[0]),
        (attended.at[:, keep], left.at[1]),
        (d_branch, d_both.at[own, :]),
        (layer.at[:, pl.ds(0, 3072)], weights),
        (dq, dqkv.at[own, pl.ds(0, WIDTH)]),
        (dkv_own, mine.at[0]),
        (dkv_other, mine.at[1]),
        (tokens, x),
        (vectors, vec),
        (d_resid, d_res),
        (grad_router, router),
        (norm_grads, norms),
    )
    loads = [pltpu.make_async_copy(src, dst, load_sems.at[n]) for n, (src, dst) in enumerate(spans)]
    for load in loads:
        load.start()
    greet(pos, core)
    send = Sender(*rest[-2:])
    to_left = send(attended.at[:, give], got_left.at[1], partner)
    to_branch = send(d_branch, d_both.at[other, :], partner)
    to_norm = send(norm1.at[:, give], got_left.at[0], partner)
    to_query = send(dq, dqkv.at[other, pl.ds(0, WIDTH)], partner)
    to_other = send(dkv_other, theirs.at[1], partner)
    to_own = send(dkv_own, theirs.at[0], partner)
    bufs, groups = list(rest[:-2]), []
    for piece in RS_PIECES + (SMALL,):
        kind = Reduction if piece is not SMALL else SmallReduction
        count = len(kind.scratch(piece))
        source, out = ((grad_qkv, sum_qkv), (grad_out, sum_out), (side, sum_side))[piece[0]]
        groups.append(kind(piece, pos, send, source, out, bufs[:count]))
        bufs = bufs[count:]
    query, value, branch, small = groups

    loads[0].wait()
    left_t[0, :, own] = transposed(left[0])
    loads[1].wait()
    left_t[1, :, own] = transposed(left[1])
    loads[2].wait()
    to_left.wait_recv()
    left_t[1, :, other] = transposed(got_left[1])
    to_branch.wait_recv()

    @pl.loop(0, 2)
    def _(i):
        cols = lanes(i * 512, 512)
        grad_out[:, :, :, :, cols] = dot_nn(left_t[1], d_both[:, cols]).reshape(SIDE, SIDE, SIDE, 8, 512)

    branch.first()
    loads[3].wait()
    loads[4].wait()
    acc[...] = jnp.zeros_like(acc)

    def back(first, count):
        @pl.loop(0, count)
        def _(i):
            cols = lanes(first + i * 512, 512)
            acc[...] += dot_nt(dqkv[own, cols], weights[:, cols])

    def grads(first, count):
        @pl.loop(0, count)
        def _(i):
            cols = lanes(first + i * 512, 512)
            grad_qkv[:, :, :, :, cols] = dot_nn(left_t[0], dqkv[:, cols]).reshape(SIDE, SIDE, SIDE, 8, 512)

    loads[5].wait()
    loads[6].wait()

    def join(first, a, b):
        def add(rows, start):
            spot = pl.ds(pl.multiple_of(first + start, BLOCK), BLOCK)
            dqkv[spot, pl.ds(WIDTH, 2 * WIDTH)] = (
                a[rows, :].astype(jnp.float32) + b[rows, :].astype(jnp.float32)
            ).astype(jnp.bfloat16)

        row_blocks(add)

    to_norm.wait_recv()
    left_t[0, :, other] = transposed(got_left[0])
    to_query.wait_recv()
    to_other.wait_recv()
    join(0, mine.at[0], theirs.at[1])
    to_own.wait_recv()
    join(GROUP, theirs.at[0], mine.at[1])
    grads(0, 3)
    query.first()
    branch.second()
    grads(1536, 3)
    value.first()
    back(0, 6)
    query.second()
    for load in loads[7:]:
        load.wait()
    sums[...] = jnp.zeros_like(sums)

    def norm_back(rows, _):
        n, inverse = normed(x[rows, :].astype(jnp.float32))
        u = acc[rows, :]
        scaled = u * vec[0:1, :]
        average = jnp.mean(scaled, -1, keepdims=True)
        project = jnp.mean(scaled * n, -1, keepdims=True)
        grad_tokens[rows, :] = d_res[rows, :] + inverse * (scaled - average - n * project)
        sums[0] += jnp.sum((u * n).reshape(BLOCK // 8, 8, WIDTH), 0)
        sums[1] += jnp.sum(u.reshape(BLOCK // 8, 8, WIDTH), 0)

    row_blocks(norm_back)
    ids = row_ids(8, WIDTH)
    vector_grads = jnp.where(
        ids == 0,
        jnp.sum(sums[0], 0, keepdims=True),
        jnp.where(ids == 1, jnp.sum(sums[1], 0, keepdims=True), norms[...]),
    )
    for half in range(2):
        rows = router[half * 512 : (half + 1) * 512, :]
        side[half, :, :, :, :, pl.ds(0, 128)] = rows.reshape(SIDE, SIDE, SIDE, 8, 128)
        for at in range(SIDE):
            block = vector_grads[:, (half * SIDE + at) * 128 : (half * SIDE + at + 1) * 128]
            side[half, at, :, :, :, pl.ds(128, 128)] = jnp.broadcast_to(block[None, None], (SIDE, SIDE, 8, 128))
    small.open(core, side)
    value.second()
    branch.third()
    small.first()
    query.third()
    value.third()
    small.third()
    branch.fourth()
    query.fourth()
    value.fourth()
    small.fourth()
    branch.last()
    query.last()
    value.last()
    small.last()
    send.close()


def finish(tokens, norm1, attended, vectors, d_resid, dq, dkv_own, dkv_other, d_branch, grad_router, norm_grads,
           layer):
    low, wide = jnp.bfloat16, jnp.float32
    anywhere = pl.BlockSpec(memory_space=pl.ANY)
    vmem = pl.BlockSpec(memory_space=pltpu.VMEM)
    lead = (SIDE, SIDE, SIDE, 8)
    scratch, copies = SmallReduction.scratch(SMALL), 6 + SmallReduction.COPIES
    for piece in RS_PIECES[::-1]:
        scratch, copies = Reduction.scratch(piece) + scratch, copies + Reduction.COPIES
    return pl.pallas_call(
        finish_kernel,
        out_shape=tuple(jax.ShapeDtypeStruct((8, c), wide) for c in RS_COLS)
        + (jax.ShapeDtypeStruct((GROUP, WIDTH), wide),),
        in_specs=[anywhere] * 12,
        out_specs=(vmem,) * 4,
        scratch_shapes=[
            pltpu.VMEM((WIDTH, 3 * WIDTH), low),
            pltpu.VMEM((GROUP, WIDTH), low),
            pltpu.VMEM((GROUP, WIDTH), wide),
            pltpu.VMEM((2, GROUP, HALF), low),
            pltpu.VMEM((2, HALF, 2 * GROUP), low),
            pltpu.VMEM((2, GROUP, 2 * WIDTH), low),
            pltpu.VMEM((2, GROUP, 2 * WIDTH), low),
            pltpu.VMEM((2, GROUP, HALF), low),
            pltpu.VMEM((2 * GROUP, 3 * WIDTH), low),
            pltpu.VMEM((2 * GROUP, WIDTH), low),
            pltpu.VMEM((GROUP, WIDTH), wide),
            pltpu.VMEM((2, 8, WIDTH), wide),
            pltpu.VMEM(lead + (3 * WIDTH,), wide),
            pltpu.VMEM(lead + (WIDTH,), wide),
            pltpu.VMEM((WIDTH, 128), wide),
            pltpu.VMEM((8, WIDTH), wide),
            pltpu.VMEM((8, WIDTH), wide),
            pltpu.VMEM((2,) + lead + (256,), wide),
            pltpu.SemaphoreType.DMA((12,)),
            *scratch,
            pltpu.SemaphoreType.DMA((copies,)),
            pltpu.SemaphoreType.DMA((copies,)),
        ],
        compiler_params=pltpu.CompilerParams(
            collective_id=1, has_side_effects=True, vmem_limit_bytes=60 * 1024 * 1024
        ),
        name="finish",
    )(tokens, norm1, attended, vectors, d_resid, dq, dkv_own, dkv_other, d_branch, grad_router, norm_grads, layer)


def results_kernel(sum_qkv, sum_out, side, given_tokens, qkv, out, router, *rest):
    vectors, (loss, tokens) = rest[:4], rest[4:]
    place = (lax.axis_index("dp") * 64 + lax.axis_index("expert")) % 16
    qkv[...] = sum_qkv[...]
    out[...] = sum_out[...]
    tokens[...] = given_tokens[...]
    router[...] = side[:, :64]
    sums = side[:, 128:256]
    sums_here = pltpu.roll(sums, (16 - place) * 8 % 128, 1)
    for n in range(4):
        vectors[n][...] = sums_here[n : n + 1, :8]
    loss[...] = sums[4:5, 0:1] / (sums[5:6, 0:1] * WIDTH)


def results(*sums):
    wide = jnp.float32
    shapes = ((8, 3072), (8, 1024), (8, 64), (1, 8), (1, 8), (1, 8), (1, 8), (1, 1), (GROUP, WIDTH))
    vmem = pl.BlockSpec(memory_space=pltpu.VMEM)
    return pl.pallas_call(
        results_kernel,
        out_shape=tuple(jax.ShapeDtypeStruct(s, wide) for s in shapes),
        in_specs=[vmem] * 4,
        out_specs=(vmem,) * 9,
        name="results",
    )(*sums)


def per_device(
    tokens,
    teacher,
    lengths,
    routes,
    ln1_gain,
    ln1_bias,
    query_key_value_weight,
    output_weight,
    ln2_gain,
    ln2_bias,
    router_weight,
    w_in,
    w_down,
):
    vectors = [vector.reshape(1, 8) for vector in (ln1_gain, ln1_bias, ln2_gain, ln2_bias)]
    layer, in_other, down_other = gather_layer(
        query_key_value_weight, output_weight, router_weight, vectors, w_in[0], w_down[0]
    )
    x, parting, qkv, kv_other, attended, norm1, norm2, residual, lse, probs, placing, vectors = forward(
        tokens[0], teacher[0], routes.reshape(1, GROUP), lengths, layer
    )
    y_back, d_back, g1, g2 = experts(x, parting, w_in[0], in_other, w_down[0], down_other)
    mixed, d_resid, dq, dkv_own, dkv_other, d_branch, grad_router, norm_grads, g1, g2 = backward(
        y_back, d_back, teacher[0], lengths, layer, qkv, kv_other, norm2, residual, lse, probs, placing, vectors,
        g1, g2,
    )
    sums = finish(
        tokens[0], norm1, attended, vectors, d_resid, dq, dkv_own, dkv_other, d_branch, grad_router, norm_grads,
        layer,
    )
    grad_qkv, grad_out, grad_router, *vector_grads, loss_value, grad_tokens = results(*sums)
    return (
        mixed[None],
        loss_value[0, 0],
        grad_tokens[None],
        vector_grads[0][0],
        vector_grads[1][0],
        grad_qkv,
        grad_out,
        vector_grads[2][0],
        vector_grads[3][0],
        grad_router,
        g1[None],
        g2[None],
    )


def solution(mesh):
    placed = (
        P("expert", "dp", None),
        P("expert", "dp", None),
        P("expert"),
        P("expert", "dp", None),
        P(("dp", "expert")),
        P(("dp", "expert")),
        P(("dp", "expert"), None),
        P(("dp", "expert"), None),
        P(("dp", "expert")),
        P(("dp", "expert")),
        P(("dp", "expert"), None),
        P("expert", "dp", None),
        P("expert", "dp", None),
    )
    return jax.shard_map(
        per_device,
        mesh=mesh,
        in_specs=placed,
        out_specs=(
            P("expert", "dp", None),
            P(),
            P("expert", "dp", None),
            P(("dp", "expert")),
            P(("dp", "expert")),
            P(("dp", "expert"), None),
            P(("dp", "expert"), None),
            P(("dp", "expert")),
            P(("dp", "expert")),
            P(("dp", "expert"), None),
            P("expert", "dp", None),
            P("expert", "dp", None),
        ),
        check_vma=False,
    )
```
